32 devices in a mesh: tensor: 4 (over z), dp: 4 (over y, x), replica: 2 (over core).
Axes of the slice: x: 2, y: 2, z: 4, core: 2. Of those that a mesh axis runs over, the one named last changes fastest.
Arguments:
- states: bfloat16 [8, 256, 4096], P(('dp', 'replica')), may hold values from -6 to 6
- norm_gain: float32 [4096], replicated, may hold values from 0.26 to 4.4
- gate_up: bfloat16 [4096, 2, 14336], P('replica', None, 'tensor'), may hold values from -0.09375 to 0.09375
- cotangent: bfloat16 [8, 256, 14336], P(('dp', 'replica'), None, 'tensor'), may hold values from -120 to 120
- prompt: bfloat16 [32, 4096], replicated, may hold values from -6 to 6
- step_sizes: float32 [3], replicated, may hold values from 0.3 to 1
- insert_at: int32 [8], P(('dp', 'replica')), may hold values from 0 to 224, as said below
- lengths: int32 [8], P(('dp', 'replica')), may hold values from 128 to 256, as said below
Outputs:
- prompt_final: float32 [32, 4096], P(None, 'tensor')
- weight_step: bfloat16 [4096, 2, 14336], P(('dp', 'replica'), None, 'tensor')
The draws below stay inside these ranges and needn't reach their ends.
Inputs may be any that keep to these rules, and one draw needn't show every extreme that they name: Each prompt lies inside its sequence: insert_at[b] + 32 <= lengths[b]; in every draw some prompt begins at row 0 and some prompt ends at the last row 255. `lengths`: in every draw some sequence has all 256 rows live and some has 128.
All inputs are finite; a program needn't handle non-finite values.
Results may differ from the reference program's by a relative error of at most 0.012.
Values may be sent and summed in bfloat16 or wider, within the bound.
A program may use at most 320 MiB of HBM per device.

```python
import math
import jax
import jax.numpy as jnp
from jax import lax

D = 4096
FF = 14336
NP = 32
ITERS = 3
SEQ = 256
BATCH = 8


def sequence_plan(key):
    inner_key = jax.random.fold_in(key, 11)
    key_lengths, key_longest, key_starts = jax.random.split(inner_key, 3)
    drawn_lengths = jax.random.randint(key_lengths, (BATCH,), SEQ // 2, SEQ + 1)
    longest = jax.random.randint(key_longest, (), 0, BATCH)
    shortest = (longest + 1) % BATCH
    seq_index = jnp.arange(BATCH)
    seq_lengths = jnp.where(seq_index == longest, SEQ, drawn_lengths)
    seq_lengths = jnp.where(seq_index == shortest, SEQ // 2, seq_lengths).astype(jnp.int32)
    starts = jax.random.randint(key_starts, (BATCH,), 0, seq_lengths - NP + 1)
    starts = jnp.where(seq_index == longest, SEQ - NP, starts)
    starts = jnp.where(seq_index == shortest, 0, starts)
    return (seq_lengths, starts.astype(jnp.int32))


def draw_lengths(key, part):
    return sequence_plan(key)[0]


def draw_insert_at(key, part):
    return sequence_plan(key)[1]


def draw_norm_gain(key, part):
    feature_ramp = jnp.arange(D, dtype=jnp.float32) / D
    jitter = jax.random.uniform(key, (D,), jnp.float32, -1.0, 1.0)
    return (0.35 * 10.0 ** feature_ramp * (1.0 + 0.25 * jitter)).astype(jnp.float32)


def draw_cotangent(key, part):
    key_values, key_rows = jax.random.split(key, 2)
    column_ramp = jnp.arange(FF, dtype=jnp.float32) / FF
    row_scales = 10.0 ** jax.random.uniform(key_rows, (BATCH, SEQ, 1), jnp.float32)
    values = jax.random.truncated_normal(key_values, -4.0, 4.0, (BATCH, SEQ, FF), jnp.float32)
    return (values * (0.3 * 10.0 ** column_ramp) * row_scales).astype(jnp.bfloat16)


def level_of(key, extent, cuts, low, largest):
    level, own = 1.0, jax.random.fold_in(key, 6)
    for dim, shards_of in cuts:
        steps = jnp.exp(jax.random.uniform(jax.random.fold_in(own, dim), (shards_of,), jnp.float32, low / len(cuts), largest / len(cuts)))
        level = level * jnp.repeat(steps, extent[dim] // shards_of).reshape([-1 if axis == dim else 1 for axis in range(len(extent))])
    return level


def centred(rng, extent, spread, limit, cuts=(), kind=jnp.bfloat16):
    values = jax.random.normal(rng, extent, jnp.float32) * spread
    if len(cuts) > 0:
        values = level_of(rng, extent, cuts, -0.22, 0.18) * values
    return jnp.clip(values, min=-limit, max=limit).astype(kind)


def setup_inputs(seed: int = 0) -> dict:
    keys = jax.random.split(jax.random.key(seed), 9)
    states = centred(keys[0], (BATCH, SEQ, D), 1.0, 6.0, ((0, 8),))
    norm_gain = draw_norm_gain(jax.random.fold_in(keys[8], 71), 0)
    gate_up = centred(keys[2], (D, 2, FF), D ** -0.5, 0.09375, ((0, 2), (2, 4)))
    cotangent = draw_cotangent(jax.random.fold_in(keys[8], 71), 0)
    prompt = centred(keys[4], (NP, D), 1.0, 6.0)
    step_sizes = jnp.clip(jnp.exp(jax.random.uniform(keys[5], (ITERS,), jnp.float32, math.log(0.3), math.log(1.0))), 0.3, 1.0)
    insert_at = draw_insert_at(jax.random.fold_in(keys[8], 71), 0)
    lengths = draw_lengths(jax.random.fold_in(keys[8], 71), 0)
    return dict(states=states, norm_gain=norm_gain, gate_up=gate_up, cotangent=cotangent, prompt=prompt, step_sizes=step_sizes, insert_at=insert_at, lengths=lengths)


def row_scale(feature_rows):
    return lax.rsqrt(lax.optimization_barrier(jnp.mean(feature_rows * feature_rows, axis=-1, keepdims=True)) + 1e-05)

def silu_parts(gate_values):
    sigmoid_value = jax.nn.sigmoid(gate_values)
    return (gate_values * sigmoid_value, sigmoid_value * (1.0 + gate_values * (1.0 - sigmoid_value)))

def hidden_grads(normalized, weight_pair, cotan_rows):
    unit_count = weight_pair.shape[1] // 2
    projected = jnp.dot(normalized, weight_pair, preferred_element_type=jnp.float32)
    activated, derivative = silu_parts(projected[:, :unit_count])
    up_part = projected[:, unit_count:]
    return jnp.concatenate([cotan_rows * up_part * derivative, cotan_rows * activated], axis=1).astype(jnp.bfloat16)

def norm_back(shifted, inverse_rms, norm_gain, feature_grad):
    feature_mean = lax.optimization_barrier(jnp.mean(shifted * norm_gain * feature_grad, axis=-1, keepdims=True))
    return inverse_rms * norm_gain * feature_grad - shifted * (inverse_rms * inverse_rms * inverse_rms) * feature_mean

def take_rows(seq_array, row_start):
    return lax.dynamic_slice_in_dim(seq_array, row_start.astype(jnp.int32), NP, 0)

def reference(states, norm_gain, gate_up, cotangent, prompt, step_sizes, insert_at, lengths):
    weight_pair = gate_up.reshape(D, 2 * FF)
    prompt_base = jax.vmap(take_rows)(states, insert_at).astype(jnp.float32)
    prompt_cotan = jax.vmap(take_rows)(cotangent, insert_at).astype(jnp.float32).reshape(BATCH * NP, FF)
    adversary = prompt.astype(jnp.float32)
    for attack_step in range(ITERS):
        shifted = (prompt_base + adversary[None]).reshape(BATCH * NP, D)
        inverse_rms = row_scale(shifted)
        normalized = (shifted * inverse_rms * norm_gain).astype(jnp.bfloat16)
        unit_grads = hidden_grads(normalized, weight_pair, prompt_cotan)
        feature_grad = lax.dot_general(unit_grads, weight_pair, (((1,), (1,)), ((), ())), preferred_element_type=jnp.float32)
        row_grads = norm_back(shifted, inverse_rms, norm_gain, feature_grad)
        summed_grad = lax.optimization_barrier(jnp.sum(row_grads.reshape(BATCH, NP, D), axis=0))
        adversary = adversary + step_sizes[attack_step] * summed_grad * lax.rsqrt(lax.optimization_barrier(jnp.mean(summed_grad * summed_grad, axis=-1, keepdims=True)) + 1e-06)
    slot_match = jnp.arange(SEQ, dtype=jnp.int32)[None, :, None] - insert_at[:, None, None] == jnp.arange(NP, dtype=jnp.int32)[None, None, :]
    placed = jnp.einsum('bsn,nd->bsd', slot_match.astype(jnp.float32), adversary, precision=lax.Precision.HIGHEST)
    full_rows = (states.astype(jnp.float32) + placed).reshape(BATCH * SEQ, D)
    full_normed = (full_rows * row_scale(full_rows) * norm_gain).astype(jnp.bfloat16)
    live_rows = jnp.arange(SEQ, dtype=jnp.int32)[None, :] < lengths[:, None]
    live_cotan = jnp.where(live_rows[:, :, None], cotangent.astype(jnp.float32), 0.0).reshape(BATCH * SEQ, FF)
    token_grads = hidden_grads(full_normed, weight_pair, live_cotan)
    weight_grad = lax.dot_general(full_normed, token_grads, (((0,), (0,)), ((), ())), preferred_element_type=jnp.float32)
    squares = jnp.sum(weight_grad * weight_grad)
    weight_step = (weight_grad * lax.rsqrt(squares / (2 * D * FF) + 1e-06)).astype(jnp.bfloat16).reshape(D, 2, FF)
    return (adversary, weight_step)
```

```python
import functools

import jax
import jax.numpy as jnp
from jax import lax
from jax.experimental import pallas as pl
from jax.experimental.pallas import tpu as pltpu
from jax.sharding import PartitionSpec as P

D = 4096
FF = 14336
MESH = pl.DeviceIdType.MESH


def row_scale(feature_rows):
    return lax.rsqrt(jnp.mean(feature_rows * feature_rows, axis=-1, keepdims=True) + 1e-05)


def silu_parts(gate_values):
    sigmoid_value = jax.nn.sigmoid(gate_values)
    return (
        gate_values * sigmoid_value,
        sigmoid_value * (1.0 + gate_values * (1.0 - sigmoid_value)),
    )


def hidden_grads(normalized, weight_pair, cotan_rows):
    unit_count = weight_pair.shape[1] // 2
    projected = jnp.dot(normalized, weight_pair, preferred_element_type=jnp.float32)
    activated, derivative = silu_parts(projected[:, :unit_count])
    up_part = projected[:, unit_count:]
    return jnp.concatenate(
        [cotan_rows * up_part * derivative, cotan_rows * activated], axis=1
    ).astype(jnp.bfloat16)


def step_kernel(
    tensors, chips, cores, partial_ref, adversary_ref, step_ref, out_ref,
    plane_buf, line_buf, mine, send1, recv1, send2, recv2, send3, recv3, send4, recv4,
):
    group = chips * cores
    t = lax.axis_index("tensor")
    g = lax.axis_index("dp") * cores + lax.axis_index("replica")
    rows = partial_ref.shape[0] // group
    own = rows // tensors
    plane = [lax.rem(g + k, group) for k in range(1, group)]
    line = [lax.rem(t + k, tensors) for k in range(1, tensors)]
    plane_ids = [{"dp": p // cores, "replica": lax.rem(p, cores)} for p in plane]
    line_ids = [{"tensor": p} for p in line]

    barrier = pltpu.get_barrier_semaphore()
    for device in plane_ids + line_ids:
        pl.semaphore_signal(barrier, inc=1, device_id=device, device_id_type=MESH)
    pl.semaphore_wait(barrier, group + tensors - 2)

    def exchange(pairs, ids, sends, recvs):
        copies = []
        for k, ((source, target), device) in enumerate(zip(pairs, ids)):
            copy = pltpu.make_async_remote_copy(
                src_ref=source, dst_ref=target, send_sem=sends.at[k], recv_sem=recvs.at[k],
                device_id=device, device_id_type=MESH,
            )
            copy.start()
            copies.append(copy)
        return copies

    first = exchange(
        [(partial_ref.at[pl.ds(p * rows, rows)], plane_buf.at[k]) for k, p in enumerate(plane)],
        plane_ids, send1, recv1,
    )
    total = partial_ref[pl.ds(g * rows, rows)]
    for k, copy in enumerate(first):
        copy.wait_recv()
        total = total + plane_buf[k]
    mine[...] = total
    second = exchange(
        [(mine.at[pl.ds(p * own, own)], line_buf.at[k]) for k, p in enumerate(line)],
        line_ids, send2, recv2,
    )
    grad = mine[pl.ds(t * own, own)]
    for k, copy in enumerate(second):
        copy.wait_recv()
        grad = grad + line_buf[k]
    square = jnp.sum(jnp.sum(grad * grad, axis=2, keepdims=True), axis=1, keepdims=True)
    count = partial_ref.shape[1] * partial_ref.shape[2]
    row = g * rows + t * own
    block = pl.ds(row, own)
    out_ref[block] = adversary_ref[block] + step_ref[0] * grad * lax.rsqrt(square / count + 1e-06)
    third = exchange([(out_ref.at[block], out_ref.at[block])] * len(line), line_ids, send3, recv3)
    for copy in third:
        copy.wait_recv()
    wide = pl.ds(g * rows, rows)
    fourth = exchange([(out_ref.at[wide], out_ref.at[wide])] * len(plane), plane_ids, send4, recv4)
    for copy in fourth:
        copy.wait_recv()
    for copy in first + second + third + fourth:
        copy.wait_send()


def apply_step(partial, adversary, step_size):
    tensors, chips, cores = (lax.axis_size(a) for a in ("tensor", "dp", "replica"))
    group = chips * cores
    count, width = partial.shape
    if count % (group * tensors) == 0 and width % 1024 == 0:
        shape = (count, 8, width // 8)
        rows = count // group
        own = rows // tensors
        dma = pltpu.SemaphoreType.DMA
        vmem = pl.BlockSpec(memory_space=pltpu.VMEM)
        result = pl.pallas_call(
            functools.partial(step_kernel, tensors, chips, cores),
            out_shape=jax.ShapeDtypeStruct(shape, jnp.float32),
            in_specs=[vmem, vmem, pl.BlockSpec(memory_space=pltpu.SMEM)],
            out_specs=vmem,
            scratch_shapes=[
                pltpu.VMEM((group - 1, rows) + shape[1:], jnp.float32),
                pltpu.VMEM((tensors - 1, own) + shape[1:], jnp.float32),
                pltpu.VMEM((rows,) + shape[1:], jnp.float32),
            ]
            + [dma((group - 1,))] * 2 + [dma((tensors - 1,))] * 4 + [dma((group - 1,))] * 2,
            compiler_params=pltpu.CompilerParams(
                collective_id=0, has_side_effects=True, vmem_limit_bytes=16 << 20
            ),
            cost_estimate=pl.CostEstimate(
                flops=20_000_000_000, bytes_accessed=3 * count * width * 4, transcendentals=0
            ),
            name="attack_step",
        )(partial.reshape(shape), adversary.reshape(shape), step_size)
        return result.reshape(count, width)
    grad = lax.psum(partial, ("tensor", "dp", "replica"))
    scale = lax.rsqrt(jnp.mean(grad * grad, axis=-1, keepdims=True) + 1e-06)
    return adversary + step_size[0] * grad * scale


def scalar_kernel(tensors, chips, cores, value_ref, out_ref, buf1, buf2, mine, send1, recv1, send2, recv2):
    group = chips * cores
    t = lax.axis_index("tensor")
    g = lax.axis_index("dp") * cores + lax.axis_index("replica")
    plane = [lax.rem(g + k, group) for k in range(1, group)]
    plane_ids = [{"dp": p // cores, "replica": lax.rem(p, cores)} for p in plane]
    line_ids = [{"tensor": lax.rem(t + k, tensors)} for k in range(1, tensors)]
    barrier = pltpu.get_barrier_semaphore()
    for device in plane_ids + line_ids:
        pl.semaphore_signal(barrier, inc=1, device_id=device, device_id_type=MESH)
    pl.semaphore_wait(barrier, group + tensors - 2)
    copies = []
    total = value_ref[...]
    source = value_ref
    for ids, buf, sends, recvs in ((plane_ids, buf1, send1, recv1), (line_ids, buf2, send2, recv2)):
        stage = []
        for k, device in enumerate(ids):
            copy = pltpu.make_async_remote_copy(
                src_ref=source, dst_ref=buf.at[k], send_sem=sends.at[k], recv_sem=recvs.at[k],
                device_id=device, device_id_type=MESH,
            )
            copy.start()
            stage.append(copy)
        for k, copy in enumerate(stage):
            copy.wait_recv()
            total = total + buf[k]
        copies += stage
        if buf is buf1:
            mine[...] = total
            source = mine
    out_ref[...] = total
    for copy in copies:
        copy.wait_send()


def sum_everywhere(value):
    tensors, chips, cores = (lax.axis_size(a) for a in ("tensor", "dp", "replica"))
    group = chips * cores
    if not 1 < tensors <= 8 or not 1 < group <= 16:
        return lax.psum(value, ("tensor", "dp", "replica"))
    dma = pltpu.SemaphoreType.DMA
    vmem = pl.BlockSpec(memory_space=pltpu.VMEM)
    return pl.pallas_call(
        functools.partial(scalar_kernel, tensors, chips, cores),
        out_shape=jax.ShapeDtypeStruct((8, 128), jnp.float32),
        in_specs=[vmem],
        out_specs=vmem,
        scratch_shapes=[
            pltpu.VMEM((group - 1, 8, 128), jnp.float32),
            pltpu.VMEM((tensors - 1, 8, 128), jnp.float32),
            pltpu.VMEM((8, 128), jnp.float32),
        ]
        + [dma((group - 1,))] * 2 + [dma((tensors - 1,))] * 2,
        compiler_params=pltpu.CompilerParams(
            collective_id=1, has_side_effects=True, vmem_limit_bytes=4 << 20
        ),
        name="scalar_sum",
    )(jnp.full((8, 128), value, jnp.float32))[0, 0]


def norm_kernel(start_ref, state_ref, parts_ref, gain_ref, out_ref):
    slots = parts_ref.shape[0] // 3
    tokens = state_ref.shape[1]
    shape = (tokens, 3 * slots)
    slot = lax.broadcasted_iota(jnp.int32, shape, 0) - start_ref[pl.program_id(0)]
    column = lax.rem(lax.broadcasted_iota(jnp.int32, shape, 1), slots)
    placed = jnp.dot(
        jnp.where(slot == column, 1.0, 0.0).astype(jnp.bfloat16), parts_ref[...],
        preferred_element_type=jnp.float32,
    )
    rows = state_ref[0].astype(jnp.float32) + placed
    scale = lax.rsqrt(jnp.mean(rows * rows, axis=-1, keepdims=True) + 1e-05)
    out_ref[0] = (rows * scale * gain_ref[...]).astype(jnp.bfloat16)


def normed_rows(starts, states, parts, gain):
    count, tokens, width = states.shape
    return pl.pallas_call(
        norm_kernel,
        out_shape=jax.ShapeDtypeStruct(states.shape, jnp.bfloat16),
        grid_spec=pltpu.PrefetchScalarGridSpec(
            num_scalar_prefetch=1,
            grid=(count,),
            in_specs=[
                pl.BlockSpec((1, tokens, width), lambda b, s: (b, 0, 0)),
                pl.BlockSpec(parts.shape, lambda b, s: (0, 0)),
                pl.BlockSpec((1, width), lambda b, s: (0, 0)),
            ],
            out_specs=pl.BlockSpec((1, tokens, width), lambda b, s: (b, 0, 0)),
        ),
        compiler_params=pltpu.CompilerParams(vmem_limit_bytes=48 << 20),
        cost_estimate=pl.CostEstimate(
            flops=count * tokens * width * 200, bytes_accessed=count * tokens * width * 4,
            transcendentals=0,
        ),
        name="normed_rows",
    )(starts, states, parts, gain.reshape(1, width)).reshape(count * tokens, width)


def per_device_general(states, norm_gain, gate_up, cotangent, prompt, step_sizes, insert_at, lengths):
    chips, cores = lax.axis_size("dp"), lax.axis_size("replica")
    chip, core = lax.axis_index("dp"), lax.axis_index("replica")
    half, _, shard_units = gate_up.shape
    units = shard_units // chips
    count = prompt.shape[0]
    tokens = states.shape[1]
    width = half * cores

    unit_slice = lax.dynamic_slice_in_dim(gate_up, chip * units, units, 2)
    weight_pair = lax.all_gather(
        unit_slice.reshape(half, 2 * units), "replica", axis=0, tiled=True
    )

    seq_states, seq_cotan, prompt_start = states[0], cotangent[0], insert_at[0]
    package = jnp.concatenate(
        [
            lax.dynamic_slice_in_dim(seq_states, prompt_start, count, 0),
            lax.dynamic_slice_in_dim(seq_cotan, prompt_start, count, 0),
            jnp.broadcast_to(insert_at.astype(jnp.bfloat16).reshape(1, 1), (count, 128)),
        ],
        axis=1,
    )
    package = lax.all_gather(package, "dp", axis=0, tiled=False)
    prompt_base = package[:, :, :width].astype(jnp.float32)
    prompt_cotan = (
        lax.dynamic_slice_in_dim(package, width + chip * units, units, 2)
        .reshape(chips * count, units)
        .astype(jnp.float32)
    )

    swap = [(i, (i + 1) % cores) for i in range(cores)]
    own_starts = package[:, 0, package.shape[2] - 1].astype(jnp.int32)
    seq_states, seq_cotan, _ = lax.optimization_barrier((seq_states, seq_cotan, weight_pair))
    own_states = lax.all_gather(seq_states, "dp", axis=0, tiled=False)
    other_starts = lax.ppermute(own_starts, "replica", swap)
    positions = lax.broadcasted_iota(jnp.int32, (tokens, 1), 0)
    live_cotan = jnp.where(positions < lengths[0], seq_cotan, jnp.zeros_like(seq_cotan))

    def shifted_perm(k):
        return [(i, (i + k) % chips) for i in range(chips)]

    cotan_blocks = []
    for k in range(chips):
        block = lax.dynamic_slice_in_dim(live_cotan, lax.rem(chip + k, chips) * units, units, 1)
        cotan_blocks.append(lax.ppermute(block, "dp", shifted_perm(k)) if k else block)
    stacked = jnp.stack(cotan_blocks)
    token_cotan = jnp.concatenate(
        [
            lax.dynamic_index_in_dim(stacked, lax.rem(chip - j + chips, chips), 0, keepdims=False)
            for j in range(chips)
        ],
        axis=0,
    )

    adversary = prompt.astype(jnp.float32)
    for attack_step in range(step_sizes.shape[0]):
        shifted = prompt_base + adversary[None]
        inverse_rms = row_scale(shifted)
        normalized = (shifted * inverse_rms * norm_gain).astype(jnp.bfloat16)
        unit_grads = hidden_grads(normalized.reshape(chips * count, width), weight_pair, prompt_cotan)
        feature_grad = lax.dot_general(
            unit_grads, weight_pair, (((1,), (1,)), ((), ())), preferred_element_type=jnp.float32
        ).reshape(chips, count, width)
        scaled = norm_gain * feature_grad
        feature_mean = jnp.mean(shifted * scaled, axis=-1, keepdims=True)
        partial = jnp.sum(
            inverse_rms * scaled - shifted * (inverse_rms * inverse_rms * inverse_rms) * feature_mean,
            axis=0,
        )
        adversary = apply_step(partial, adversary, step_sizes[attack_step : attack_step + 1])
        if attack_step == step_sizes.shape[0] - 2:
            own_states, adversary = lax.optimization_barrier((own_states, adversary))
            other_states = lax.ppermute(own_states, "replica", swap)

    high = lax.reduce_precision(adversary, 8, 7)
    middle = lax.reduce_precision(adversary - high, 8, 7)
    low = adversary - high - middle
    parts = jnp.concatenate([high, middle, low], axis=0).astype(jnp.bfloat16)
    own_normed = normed_rows(own_starts, own_states, parts, norm_gain)
    own_grads = hidden_grads(own_normed, weight_pair, token_cotan.astype(jnp.float32))
    other_grads = lax.ppermute(own_grads, "replica", swap)
    other_normed = normed_rows(other_starts, other_states, parts, norm_gain)

    block_width = width // (chips * cores)
    dims = (((0,), (0,)), ((), ()))
    squares = 0.0
    received = [None] * chips
    for k in [2 % chips, *[i for i in range(1, chips) if i != 2 % chips], 0] if chips > 2 else range(chips):
        start = (lax.rem(chip + k, chips) * cores + core) * block_width
        block = lax.dot_general(
            lax.dynamic_slice_in_dim(own_normed, start, block_width, 1), own_grads, dims,
            preferred_element_type=jnp.float32,
        ) + lax.dot_general(
            lax.dynamic_slice_in_dim(other_normed, start, block_width, 1), other_grads, dims,
            preferred_element_type=jnp.float32,
        )
        squares = squares + jnp.sum(block * block)
        sent = block.astype(jnp.bfloat16)
        received[k] = lax.ppermute(sent, "dp", shifted_perm(k)) if k else sent
    squares = sum_everywhere(squares)
    scale = lax.rsqrt(squares / (2 * D * FF) + 1e-06)
    stacked = jnp.stack(received)
    pieces = [
        lax.dynamic_index_in_dim(stacked, lax.rem(chip - j + chips, chips), 0, keepdims=False)
        for j in range(chips)
    ]
    weight_step = jnp.concatenate(
        [piece.reshape(block_width, 2, units) for piece in pieces], axis=2
    )
    weight_step = (weight_step.astype(jnp.float32) * scale).astype(jnp.bfloat16)
    column_count = width // lax.axis_size("tensor")
    prompt_final = lax.dynamic_slice_in_dim(
        adversary, lax.axis_index("tensor") * column_count, column_count, 1
    )
    return (prompt_final, weight_step)


def relative_devices(chip, core):
    pairs = []
    for m in range(4):
        other_chip = [chip, chip + 1 - 2 * lax.rem(chip, 2), lax.rem(chip + 2, 4), 3 - chip][m]
        for q in range(2):
            pairs.append((other_chip, core if q == 0 else 1 - core))
    return pairs


def main_kernel(
    tensors, steps,
    g_own, x_own, w_near, w_far, prompt_in, base_rows, base_cot, gain_ref, step_ref,
    adv_out, xp_out, g_all, x_all, gp_all,
    base_buf, cot_buf, near_v, far_v, x_v, fg_v, inv_v, adv, part, send_a, recv_a, recv_b, recv_c, gp_v,
    s_local, s_x, r_x, s_g, r_g, s_p, r_p, s_c, r_c, s_1, r_1, s_2, r_2, s_3, r_3, s_o, r_o,
):
    t = lax.axis_index("tensor")
    chip = lax.axis_index("dp")
    core = lax.axis_index("replica")
    me = chip * 2 + core
    rel = relative_devices(chip, core)
    ids = [{"dp": a, "replica": b} for a, b in rel]
    place = [a * 2 + b for a, b in rel]
    wide = w_near.shape[2]
    units = base_cot.shape[1] // 4
    half = w_near.shape[1]
    count, width = base_rows.shape
    block = width // 8
    own_base = g_own.shape[0]
    cols = g_own.shape[1]
    split = cols // 2

    def remote(src, dst, send, recv, device):
        return pltpu.make_async_remote_copy(
            src_ref=src, dst_ref=dst, send_sem=send, recv_sem=recv,
            device_id=device, device_id_type=MESH,
        )

    barrier = pltpu.get_barrier_semaphore()
    line_ids = [{"tensor": lax.rem(t + k, tensors)} for k in range(1, tensors)]
    for device in ids[1:] + line_ids:
        pl.semaphore_signal(barrier, inc=1, device_id=device, device_id_type=MESH)
    pl.semaphore_wait(barrier, 7 + tensors - 1)

    rows_a = [remote(base_rows, base_buf.at[me], s_p.at[m], r_p.at[m], ids[2 * m]) for m in range(1, 4)]
    cots = [None] * 8
    for j in range(1, 8):
        first = pl.multiple_of(rel[j][0] * units + rel[j][1] * (units - wide), 128)
        cots[j] = remote(base_cot.at[:, pl.ds(first, wide)], cot_buf.at[me], s_c.at[j], r_c.at[j], ids[j])
    for copy in rows_a + cots[1:]:
        copy.start()
    my_first = pl.multiple_of(chip * units + core * (units - wide), 128)
    local = [
        pltpu.make_async_copy(base_rows, base_buf.at[me], s_local.at[0]),
        pltpu.make_async_copy(base_cot.at[:, pl.ds(my_first, wide)], cot_buf.at[me], s_local.at[1]),
        pltpu.make_async_copy(w_near, near_v, s_local.at[2]),
        pltpu.make_async_copy(w_far, far_v, s_local.at[3]),
    ]
    for copy in local:
        copy.start()
    rows_b = [
        remote(base_buf.at[place[2 * m]], base_buf.at[place[2 * m]], s_p.at[4 + m], r_p.at[4 + m], ids[1])
        for m in range(4)
    ]
    local[0].wait()
    rows_b[0].start()
    xs = [None] * 8
    for j in range(1, 8):
        first = pl.multiple_of(place[j] * block, 128)
        xs[j] = remote(x_own.at[:, pl.ds(first, block)], x_all.at[j], s_x.at[j], r_x.at[j], ids[j])
    halves = [pl.ds(0, split), pl.ds(split, split)]

    def gcopy(src, dst, k, device):
        return remote(src, dst, s_g.at[k], r_g.at[k], device)

    gx = [gcopy(g_own.at[:, halves[h]], g_all.at[2, :, halves[h]], h, ids[2]) for h in range(2)]
    gy = [gcopy(g_own.at[:, halves[h]], g_all.at[4, :, halves[h]], 2 + h, ids[4]) for h in range(2)]
    gs = gcopy(g_own, g_all.at[1], 4, ids[1])
    fy = gcopy(g_all.at[2, :, halves[0]], g_all.at[6, :, halves[0]], 5, ids[4])
    fx = gcopy(g_all.at[4, :, halves[1]], g_all.at[6, :, halves[1]], 6, ids[2])
    side = [None] + [
        [gcopy(g_all.at[2 * m, :, halves[h]], g_all.at[2 * m + 1, :, halves[h]], 7 + 2 * m + h, ids[1]) for h in range(2)]
        for m in range(1, 4)
    ]
    for m in range(1, 4):
        rows_a[m - 1].wait_recv()
        rows_b[m].start()
    for copy in [gx[0], gy[1]] + xs[1:] + [gx[1], gy[0], gs]:
        copy.start()
    g_local = pltpu.make_async_copy(g_own, g_all.at[0], s_local.at[4])
    x_first = pl.multiple_of(me * block, 128)
    x_local = pltpu.make_async_copy(x_own.at[:, pl.ds(x_first, block)], x_all.at[0], s_local.at[5])
    g_local.start()
    x_local.start()

    adv[...] = prompt_in[...].astype(jnp.float32)
    for copy in rows_b + cots[1:]:
        copy.wait_recv()
    for copy in local[1:]:
        copy.wait()
    lane = lax.broadcasted_iota(jnp.int32, (count, wide), 1)
    keep = lane >= core * (2 * wide - units)

    def norm_rows():
        def one(b, _):
            shifted = base_buf[b].astype(jnp.float32) + adv[...]
            inverse = lax.rsqrt(jnp.mean(shifted * shifted, axis=-1, keepdims=True) + 1e-05)
            x_v[pl.ds(pl.multiple_of(b * count, count), count)] = (shifted * inverse * gain_ref[...]).astype(jnp.bfloat16)
            inv_v[b] = jnp.broadcast_to(inverse, (count, 128))
            return 0
        lax.fori_loop(0, 8, one, 0)

    def unit_grads():
        near = x_v[:, pl.ds(pl.multiple_of(core * half, 128), half)]
        far = x_v[:, pl.ds(pl.multiple_of((1 - core) * half, 128), half)]
        gate, up = [
            jnp.dot(near, near_v[p], preferred_element_type=jnp.float32)
            + jnp.dot(far, far_v[p], preferred_element_type=jnp.float32)
            for p in range(2)
        ]
        act, slope = silu_parts(gate)
        cot = jnp.concatenate(
            [jnp.where(keep, cot_buf[b].astype(jnp.float32), 0.0) for b in range(8)], axis=0
        )
        gp_v[:, pl.ds(0, wide)] = (cot * up * slope).astype(jnp.bfloat16)
        gp_v[:, pl.ds(wide, wide)] = (cot * act).astype(jnp.bfloat16)

    dims = (((1,), (1,)), ((), ()))
    chunk = 512

    def feature_grads():
        for source, base in ((near_v, core * half), (far_v, (1 - core) * half)):
            def one(i, _):
                rows = pl.ds(pl.multiple_of(i * chunk, chunk), chunk)
                fg_v[:, pl.ds(pl.multiple_of(base + i * chunk, chunk), chunk)] = lax.dot_general(
                    gp_v[:, pl.ds(0, wide)], source[0, rows], dims, preferred_element_type=jnp.float32
                ) + lax.dot_general(
                    gp_v[:, pl.ds(wide, wide)], source[1, rows], dims, preferred_element_type=jnp.float32
                )
                return 0
            lax.fori_loop(0, half // chunk, one, 0)

    def row_grads():
        part[...] = jnp.zeros_like(part)
        def one(b, _):
            shifted = base_buf[b].astype(jnp.float32) + adv[...]
            scaled = gain_ref[...] * fg_v[pl.ds(pl.multiple_of(b * count, count), count)]
            inverse = inv_v[b][:, :1]
            middle = jnp.mean(shifted * scaled, axis=-1, keepdims=True)
            part[...] += inverse * scaled - shifted * (inverse * inverse * inverse * middle)
            return 0
        lax.fori_loop(0, 8, one, 0)

    waits = []

    def exchange(k):
        for p in range(8):
            send_a[k, p] = part[:, p * block : (p + 1) * block].astype(jnp.bfloat16)
        first = [
            remote(send_a.at[k, place[j]], recv_a.at[k, j], s_1.at[k, j], r_1.at[k, j], ids[j]) for j in range(1, 8)
        ]
        for copy in first:
            copy.start()
        total = send_a[k, me].astype(jnp.float32)
        for j, copy in enumerate(first):
            copy.wait_recv()
            total = total + recv_a[k, j + 1].astype(jnp.float32)
        recv_b[k, t] = total.astype(jnp.bfloat16)
        second = [
            remote(recv_b.at[k, t], recv_b.at[k, t], s_2.at[k, j], r_2.at[k, j], line_ids[j])
            for j in range(tensors - 1)
        ]
        for copy in second:
            copy.start()
        for copy in second:
            copy.wait_recv()
        total = recv_b[k, 0].astype(jnp.float32)
        for j in range(1, tensors):
            total = total + recv_b[k, j].astype(jnp.float32)
        recv_c[k, me] = total.astype(jnp.bfloat16)
        third = [
            remote(recv_c.at[k, me], recv_c.at[k, me], s_3.at[k, j], r_3.at[k, j], ids[j]) for j in range(1, 8)
        ]
        for copy in third:
            copy.start()
        for copy in third:
            copy.wait_recv()
        waits.extend(first + second + third)
        square = jnp.zeros((count, 1), jnp.float32)
        for p in range(8):
            piece = recv_c[k, p].astype(jnp.float32)
            square = square + jnp.sum(piece * piece, axis=-1, keepdims=True)
        scale = step_ref[k] * lax.rsqrt(square / width + 1e-06)
        for p in range(8):
            at = slice(p * block, (p + 1) * block)
            adv[:, at] = adv[:, at] + scale * recv_c[k, p].astype(jnp.float32)

    for k in range(steps):
        norm_rows()
        unit_grads()
        feature_grads()
        row_grads()
        exchange(k)
        if k == steps - 2:
            gx[0].wait_recv()
            fy.start()
            gy[1].wait_recv()
            fx.start()
            side[1][0].start()
            side[2][1].start()
    adv_out[...] = adv[...]
    norm_rows()
    unit_grads()
    xp_out[...] = x_v[:, pl.ds(x_first, block)]
    mine = gp_all.at[me]
    out_a = [remote(gp_v, mine, s_o.at[m], r_o.at[m], ids[2 * m]) for m in range(1, 4)]
    out_local = pltpu.make_async_copy(gp_v, mine, s_local.at[6])
    out_b = [remote(gp_v, mine, s_o.at[4], r_o.at[4], ids[1])]
    for m in range(1, 4):
        slot = gp_all.at[place[2 * m]]
        out_b.append(remote(slot, slot, s_o.at[4 + m], r_o.at[4 + m], ids[1]))
    for copy in out_a + [out_local, out_b[0]]:
        copy.start()
    gx[1].wait_recv()
    side[1][1].start()
    gy[0].wait_recv()
    side[2][0].start()
    for m in range(1, 4):
        out_a[m - 1].wait_recv()
        out_b[m].start()
    fy.wait_recv()
    side[3][0].start()
    fx.wait_recv()
    side[3][1].start()
    gs.wait_recv()
    sides = side[1] + side[2] + side[3]
    for copy in xs[1:] + out_b + sides:
        copy.wait_recv()
    for copy in [g_local, x_local, out_local]:
        copy.wait()
    for copy in rows_a + rows_b + cots[1:] + xs[1:] + gx + gy + [gs, fy, fx] + sides + waits + out_a + out_b:
        copy.wait_send()


def main_call(g_own, x_own, w_near, w_far, prompt, base_rows, base_cot, gain, step_sizes):
    tensors = lax.axis_size("tensor")
    steps = step_sizes.shape[0]
    count, width = base_rows.shape
    wide, half = w_near.shape[2], w_near.shape[1]
    block = width // 8
    own_base, cols = g_own.shape
    bf, f32 = jnp.bfloat16, jnp.float32
    dma = pltpu.SemaphoreType.DMA
    vmem = pl.BlockSpec(memory_space=pltpu.VMEM)
    hbm = pl.BlockSpec(memory_space=pl.ANY)
    return pl.pallas_call(
        functools.partial(main_kernel, tensors, steps),
        out_shape=[
            jax.ShapeDtypeStruct((count, width), f32),
            jax.ShapeDtypeStruct((8 * count, block), bf),
            jax.ShapeDtypeStruct((8, own_base, cols), bf),
            jax.ShapeDtypeStruct((8, own_base, block), bf),
            jax.ShapeDtypeStruct((8, 8 * count, 2 * wide), bf),
        ],
        in_specs=[hbm, hbm, hbm, hbm, vmem, hbm, hbm, vmem, pl.BlockSpec(memory_space=pltpu.SMEM)],
        out_specs=[vmem, vmem, hbm, hbm, hbm],
        scratch_shapes=[
            pltpu.VMEM((8, count, width), bf),
            pltpu.VMEM((8, count, wide), bf),
            pltpu.VMEM((2, half, wide), bf),
            pltpu.VMEM((2, half, wide), bf),
            pltpu.VMEM((8 * count, width), bf),
            pltpu.VMEM((8 * count, width), f32),
            pltpu.VMEM((8, count, 128), f32),
            pltpu.VMEM((count, width), f32),
            pltpu.VMEM((count, width), f32),
            pltpu.VMEM((steps, 8, count, block), bf),
            pltpu.VMEM((steps, 8, count, block), bf),
            pltpu.VMEM((steps, tensors, count, block), bf),
            pltpu.VMEM((steps, 8, count, block), bf),
            pltpu.VMEM((8 * count, 2 * wide), bf),
        ]
        + [dma((7,))] + [dma((8,))] * 2 + [dma((16,))] * 2 + [dma((8,))] * 4
        + [dma((steps, 8))] * 2 + [dma((steps, tensors))] * 2 + [dma((steps, 8))] * 2 + [dma((8,))] * 2,
        compiler_params=pltpu.CompilerParams(
            collective_id=2, has_side_effects=True, vmem_limit_bytes=52 << 20
        ),
        cost_estimate=pl.CostEstimate(flops=100_000_000_000, bytes_accessed=100_000_000, transcendentals=0),
        name="attack_and_gather",
    )(g_own, x_own, w_near, w_far, prompt, base_rows, base_cot, gain.reshape(1, width), step_sizes)


def grad_kernel(x_ref, xp_ref, g_ref, gp0_ref, gp1_ref, out_ref, sq_ref, xt_v, xpt_v):
    step = pl.program_id(0) * pl.num_programs(1) + pl.program_id(1)

    @pl.when(step == 0)
    def _():
        xt_v[...] = x_ref[...].T
        xpt_v[...] = xp_ref[...].T
        sq_ref[...] = jnp.zeros_like(sq_ref)

    extra = 2 * gp0_ref.shape[2] - out_ref.shape[2]
    rows = g_ref.shape[0] * g_ref.shape[1]
    gp = jnp.concatenate([gp0_ref[0], gp1_ref[0][:, extra:]], axis=1)
    block = jnp.dot(
        xt_v[...], g_ref[...].reshape(rows, g_ref.shape[2]), preferred_element_type=jnp.float32
    ) + jnp.dot(xpt_v[...], gp, preferred_element_type=jnp.float32)
    out_ref[0] = block
    sq_ref[...] += jnp.sum((block * block).reshape(-1, 8, block.shape[1]), axis=0)


def grad_call(x_all, xp, g_all, gp_all):
    eight, own_base, cols = g_all.shape
    block = x_all.shape[2]
    wide = gp_all.shape[2] // 2
    shard = cols // 2
    units = shard // 4
    prompts = xp.shape[0]
    f32 = jnp.float32
    return pl.pallas_call(
        grad_kernel,
        out_shape=[
            jax.ShapeDtypeStruct((2, block, shard), f32),
            jax.ShapeDtypeStruct((8, units), f32),
        ],
        grid=(2, 4),
        in_specs=[
            pl.BlockSpec((eight * own_base, block), lambda p, j: (0, 0)),
            pl.BlockSpec((prompts, block), lambda p, j: (0, 0)),
            pl.BlockSpec((eight, own_base, units), lambda p, j: (0, 0, p * 4 + j)),
            pl.BlockSpec((1, prompts, wide), lambda p, j: (2 * j, 0, p)),
            pl.BlockSpec((1, prompts, wide), lambda p, j: (2 * j + 1, 0, p)),
        ],
        out_specs=[
            pl.BlockSpec((1, block, units), lambda p, j: (p, 0, j)),
            pl.BlockSpec((8, units), lambda p, j: (0, 0)),
        ],
        scratch_shapes=[
            pltpu.VMEM((block, eight * own_base), jnp.bfloat16),
            pltpu.VMEM((block, prompts), jnp.bfloat16),
        ],
        compiler_params=pltpu.CompilerParams(vmem_limit_bytes=48 << 20),
        cost_estimate=pl.CostEstimate(
            flops=2 * block * cols * (eight * own_base + prompts), bytes_accessed=50_000_000, transcendentals=0
        ),
        name="weight_grad",
    )(x_all.reshape(eight * own_base, block), xp, g_all, gp_all, gp_all)


def per_device(states, norm_gain, gate_up, cotangent, prompt, step_sizes, insert_at, lengths):
    chips, cores = lax.axis_size("dp"), lax.axis_size("replica")
    shard = gate_up.shape[2]
    count = prompt.shape[0]
    fits = (
        chips == 4 and cores == 2 and states.shape[0] == 1 and shard % (chips * 128) == 0
        and shard // chips > 512 and shard // chips <= 1024
        and gate_up.shape[0] % 1024 == 0 and count % 16 == 0 and (states.shape[1] - count) % 16 == 0
    )
    if not fits:
        return per_device_general(
            states, norm_gain, gate_up, cotangent, prompt, step_sizes, insert_at, lengths
        )
    chip, core = lax.axis_index("dp"), lax.axis_index("replica")
    half = gate_up.shape[0]
    width = half * cores
    tokens = states.shape[1]
    base = tokens - count
    units = shard // chips
    wide = 512
    swap = [(0, 1), (1, 0)]
    start = insert_at[0]

    pair = jnp.transpose(gate_up, (1, 0, 2))

    def attack_slice(which):
        return lax.dynamic_slice_in_dim(pair, chip * units + which * (units - wide), wide, 2)

    w_near = attack_slice(core)
    w_far = lax.ppermute(attack_slice(1 - core), "replica", swap)

    spot = lax.broadcasted_iota(jnp.int32, (base, 1), 0)
    ahead = spot < start
    position = jnp.where(ahead, spot, spot + count)
    rows = jnp.where(ahead, states[0, :base], states[0, count:]).astype(jnp.float32)
    cot = jnp.where(ahead, cotangent[0, :base], cotangent[0, count:])
    cot = jnp.where(position < lengths[0], cot, jnp.zeros_like(cot)).astype(jnp.float32)
    normed = (rows * row_scale(rows) * norm_gain).astype(jnp.bfloat16)
    base_rows = lax.dynamic_slice_in_dim(states[0], start, count, 0)
    base_cot = lax.dynamic_slice_in_dim(cotangent[0], start, count, 0)

    own_part = lax.dynamic_slice_in_dim(normed, core * half, half, 1)
    other_part = lax.ppermute(
        lax.dynamic_slice_in_dim(normed, (1 - core) * half, half, 1), "replica", swap
    )
    both = jnp.concatenate([own_part, other_part], axis=0)
    sums = []
    for p in range(2):
        product = jnp.dot(both, pair[p], preferred_element_type=jnp.float32)
        sums.append(product[:base] + lax.ppermute(product[base:], "replica", swap))
    act, slope = silu_parts(sums[0])
    g_own = jnp.concatenate([cot * sums[1] * slope, cot * act], axis=1).astype(jnp.bfloat16)

    adversary, xp, g_all, x_all, gp_all = main_call(
        g_own, normed, w_near, w_far, prompt, base_rows, base_cot, norm_gain, step_sizes
    )
    weight_grad, squares = grad_call(x_all, xp, g_all, gp_all)
    squares = sum_everywhere(jnp.sum(squares))
    scale = lax.rsqrt(squares / (2 * D * FF) + 1e-06)
    weight_step = jnp.transpose((weight_grad * scale).astype(jnp.bfloat16), (1, 0, 2))
    column_count = width // lax.axis_size("tensor")
    prompt_final = lax.dynamic_slice_in_dim(
        adversary, lax.axis_index("tensor") * column_count, column_count, 1
    )
    return (prompt_final, weight_step)


def solution(mesh):
    return jax.shard_map(
        per_device,
        mesh=mesh,
        in_specs=(
            P(("dp", "replica"), None, None),
            P(),
            P("replica", None, "tensor"),
            P(("dp", "replica"), None, "tensor"),
            P(),
            P(),
            P(("dp", "replica")),
            P(("dp", "replica")),
        ),
        out_specs=(P(None, "tensor"), P(("dp", "replica"), None, "tensor")),
        check_vma=False,
    )
```

```python
import functools

import jax
import jax.numpy as jnp
from jax import lax
from jax.experimental import pallas as pl
from jax.experimental.pallas import tpu as pltpu
from jax.sharding import PartitionSpec as P

D = 4096
FF = 14336
MESH = pl.DeviceIdType.MESH


def row_scale(feature_rows):
    return lax.rsqrt(jnp.mean(feature_rows * feature_rows, axis=-1, keepdims=True) + 1e-05)


def silu_parts(gate_values):
    sigmoid_value = jax.nn.sigmoid(gate_values)
    return (
        gate_values * sigmoid_value,
        sigmoid_value * (1.0 + gate_values * (1.0 - sigmoid_value)),
    )


def hidden_grads(normalized, weight_pair, cotan_rows):
    unit_count = weight_pair.shape[1] // 2
    projected = jnp.dot(normalized, weight_pair, preferred_element_type=jnp.float32)
    activated, derivative = silu_parts(projected[:, :unit_count])
    up_part = projected[:, unit_count:]
    return jnp.concatenate(
        [cotan_rows * up_part * derivative, cotan_rows * activated], axis=1
    ).astype(jnp.bfloat16)


def step_kernel(
    tensors, chips, cores, partial_ref, adversary_ref, step_ref, out_ref,
    plane_buf, line_buf, mine, send1, recv1, send2, recv2, send3, recv3, send4, recv4,
):
    group = chips * cores
    t = lax.axis_index("tensor")
    g = lax.axis_index("dp") * cores + lax.axis_index("replica")
    rows = partial_ref.shape[0] // group
    own = rows // tensors
    plane = [lax.rem(g + k, group) for k in range(1, group)]
    line = [lax.rem(t + k, tensors) for k in range(1, tensors)]
    plane_ids = [{"dp": p // cores, "replica": lax.rem(p, cores)} for p in plane]
    line_ids = [{"tensor": p} for p in line]

    barrier = pltpu.get_barrier_semaphore()
    for device in plane_ids + line_ids:
        pl.semaphore_signal(barrier, inc=1, device_id=device, device_id_type=MESH)
    pl.semaphore_wait(barrier, group + tensors - 2)

    def exchange(pairs, ids, sends, recvs):
        copies = []
        for k, ((source, target), device) in enumerate(zip(pairs, ids)):
            copy = pltpu.make_async_remote_copy(
                src_ref=source, dst_ref=target, send_sem=sends.at[k], recv_sem=recvs.at[k],
                device_id=device, device_id_type=MESH,
            )
            copy.start()
            copies.append(copy)
        return copies

    first = exchange(
        [(partial_ref.at[pl.ds(p * rows, rows)], plane_buf.at[k]) for k, p in enumerate(plane)],
        plane_ids, send1, recv1,
    )
    total = partial_ref[pl.ds(g * rows, rows)]
    for k, copy in enumerate(first):
        copy.wait_recv()
        total = total + plane_buf[k]
    mine[...] = total
    second = exchange(
        [(mine.at[pl.ds(p * own, own)], line_buf.at[k]) for k, p in enumerate(line)],
        line_ids, send2, recv2,
    )
    grad = mine[pl.ds(t * own, own)]
    for k, copy in enumerate(second):
        copy.wait_recv()
        grad = grad + line_buf[k]
    square = jnp.sum(jnp.sum(grad * grad, axis=2, keepdims=True), axis=1, keepdims=True)
    count = partial_ref.shape[1] * partial_ref.shape[2]
    row = g * rows + t * own
    block = pl.ds(row, own)
    out_ref[block] = adversary_ref[block] + step_ref[0] * grad * lax.rsqrt(square / count + 1e-06)
    third = exchange([(out_ref.at[block], out_ref.at[block])] * len(line), line_ids, send3, recv3)
    for copy in third:
        copy.wait_recv()
    wide = pl.ds(g * rows, rows)
    fourth = exchange([(out_ref.at[wide], out_ref.at[wide])] * len(plane), plane_ids, send4, recv4)
    for copy in fourth:
        copy.wait_recv()
    for copy in first + second + third + fourth:
        copy.wait_send()


def apply_step(partial, adversary, step_size):
    tensors, chips, cores = (lax.axis_size(a) for a in ("tensor", "dp", "replica"))
    group = chips * cores
    count, width = partial.shape
    if count % (group * tensors) == 0 and width % 1024 == 0:
        shape = (count, 8, width // 8)
        rows = count // group
        own = rows // tensors
        dma = pltpu.SemaphoreType.DMA
        vmem = pl.BlockSpec(memory_space=pltpu.VMEM)
        result = pl.pallas_call(
            functools.partial(step_kernel, tensors, chips, cores),
            out_shape=jax.ShapeDtypeStruct(shape, jnp.float32),
            in_specs=[vmem, vmem, pl.BlockSpec(memory_space=pltpu.SMEM)],
            out_specs=vmem,
            scratch_shapes=[
                pltpu.VMEM((group - 1, rows) + shape[1:], jnp.float32),
                pltpu.VMEM((tensors - 1, own) + shape[1:], jnp.float32),
                pltpu.VMEM((rows,) + shape[1:], jnp.float32),
            ]
            + [dma((group - 1,))] * 2 + [dma((tensors - 1,))] * 4 + [dma((group - 1,))] * 2,
            compiler_params=pltpu.CompilerParams(
                collective_id=0, has_side_effects=True, vmem_limit_bytes=16 << 20
            ),
            cost_estimate=pl.CostEstimate(
                flops=20_000_000_000, bytes_accessed=3 * count * width * 4, transcendentals=0
            ),
            name="attack_step",
        )(partial.reshape(shape), adversary.reshape(shape), step_size)
        return result.reshape(count, width)
    grad = lax.psum(partial, ("tensor", "dp", "replica"))
    scale = lax.rsqrt(jnp.mean(grad * grad, axis=-1, keepdims=True) + 1e-06)
    return adversary + step_size[0] * grad * scale


def scalar_kernel(tensors, chips, cores, value_ref, out_ref, buf1, buf2, mine, send1, recv1, send2, recv2):
    group = chips * cores
    t = lax.axis_index("tensor")
    g = lax.axis_index("dp") * cores + lax.axis_index("replica")
    plane = [lax.rem(g + k, group) for k in range(1, group)]
    plane_ids = [{"dp": p // cores, "replica": lax.rem(p, cores)} for p in plane]
    line_ids = [{"tensor": lax.rem(t + k, tensors)} for k in range(1, tensors)]
    barrier = pltpu.get_barrier_semaphore()
    for device in plane_ids + line_ids:
        pl.semaphore_signal(barrier, inc=1, device_id=device, device_id_type=MESH)
    pl.semaphore_wait(barrier, group + tensors - 2)
    copies = []
    total = value_ref[...]
    source = value_ref
    for ids, buf, sends, recvs in ((plane_ids, buf1, send1, recv1), (line_ids, buf2, send2, recv2)):
        stage = []
        for k, device in enumerate(ids):
            copy = pltpu.make_async_remote_copy(
                src_ref=source, dst_ref=buf.at[k], send_sem=sends.at[k], recv_sem=recvs.at[k],
                device_id=device, device_id_type=MESH,
            )
            copy.start()
            stage.append(copy)
        for k, copy in enumerate(stage):
            copy.wait_recv()
            total = total + buf[k]
        copies += stage
        if buf is buf1:
            mine[...] = total
            source = mine
    out_ref[...] = total
    for copy in copies:
        copy.wait_send()


def sum_everywhere(value):
    tensors, chips, cores = (lax.axis_size(a) for a in ("tensor", "dp", "replica"))
    group = chips * cores
    if not 1 < tensors <= 8 or not 1 < group <= 16:
        return lax.psum(value, ("tensor", "dp", "replica"))
    dma = pltpu.SemaphoreType.DMA
    vmem = pl.BlockSpec(memory_space=pltpu.VMEM)
    return pl.pallas_call(
        functools.partial(scalar_kernel, tensors, chips, cores),
        out_shape=jax.ShapeDtypeStruct((8, 128), jnp.float32),
        in_specs=[vmem],
        out_specs=vmem,
        scratch_shapes=[
            pltpu.VMEM((group - 1, 8, 128), jnp.float32),
            pltpu.VMEM((tensors - 1, 8, 128), jnp.float32),
            pltpu.VMEM((8, 128), jnp.float32),
        ]
        + [dma((group - 1,))] * 2 + [dma((tensors - 1,))] * 2,
        compiler_params=pltpu.CompilerParams(
            collective_id=1, has_side_effects=True, vmem_limit_bytes=4 << 20
        ),
        name="scalar_sum",
    )(jnp.full((8, 128), value, jnp.float32))[0, 0]


def norm_kernel(start_ref, state_ref, parts_ref, gain_ref, out_ref):
    slots = parts_ref.shape[0] // 3
    tokens = state_ref.shape[1]
    shape = (tokens, 3 * slots)
    slot = lax.broadcasted_iota(jnp.int32, shape, 0) - start_ref[pl.program_id(0)]
    column = lax.rem(lax.broadcasted_iota(jnp.int32, shape, 1), slots)
    placed = jnp.dot(
        jnp.where(slot == column, 1.0, 0.0).astype(jnp.bfloat16), parts_ref[...],
        preferred_element_type=jnp.float32,
    )
    rows = state_ref[0].astype(jnp.float32) + placed
    scale = lax.rsqrt(jnp.mean(rows * rows, axis=-1, keepdims=True) + 1e-05)
    out_ref[0] = (rows * scale * gain_ref[...]).astype(jnp.bfloat16)


def normed_rows(starts, states, parts, gain):
    count, tokens, width = states.shape
    return pl.pallas_call(
        norm_kernel,
        out_shape=jax.ShapeDtypeStruct(states.shape, jnp.bfloat16),
        grid_spec=pltpu.PrefetchScalarGridSpec(
            num_scalar_prefetch=1,
            grid=(count,),
            in_specs=[
                pl.BlockSpec((1, tokens, width), lambda b, s: (b, 0, 0)),
                pl.BlockSpec(parts.shape, lambda b, s: (0, 0)),
                pl.BlockSpec((1, width), lambda b, s: (0, 0)),
            ],
            out_specs=pl.BlockSpec((1, tokens, width), lambda b, s: (b, 0, 0)),
        ),
        compiler_params=pltpu.CompilerParams(vmem_limit_bytes=48 << 20),
        cost_estimate=pl.CostEstimate(
            flops=count * tokens * width * 200, bytes_accessed=count * tokens * width * 4,
            transcendentals=0,
        ),
        name="normed_rows",
    )(starts, states, parts, gain.reshape(1, width)).reshape(count * tokens, width)


def per_device_general(states, norm_gain, gate_up, cotangent, prompt, step_sizes, insert_at, lengths):
    chips, cores = lax.axis_size("dp"), lax.axis_size("replica")
    chip, core = lax.axis_index("dp"), lax.axis_index("replica")
    half, _, shard_units = gate_up.shape
    units = shard_units // chips
    count = prompt.shape[0]
    tokens = states.shape[1]
    width = half * cores

    unit_slice = lax.dynamic_slice_in_dim(gate_up, chip * units, units, 2)
    weight_pair = lax.all_gather(
        unit_slice.reshape(half, 2 * units), "replica", axis=0, tiled=True
    )

    seq_states, seq_cotan, prompt_start = states[0], cotangent[0], insert_at[0]
    package = jnp.concatenate(
        [
            lax.dynamic_slice_in_dim(seq_states, prompt_start, count, 0),
            lax.dynamic_slice_in_dim(seq_cotan, prompt_start, count, 0),
            jnp.broadcast_to(insert_at.astype(jnp.bfloat16).reshape(1, 1), (count, 128)),
        ],
        axis=1,
    )
    package = lax.all_gather(package, "dp", axis=0, tiled=False)
    prompt_base = package[:, :, :width].astype(jnp.float32)
    prompt_cotan = (
        lax.dynamic_slice_in_dim(package, width + chip * units, units, 2)
        .reshape(chips * count, units)
        .astype(jnp.float32)
    )

    swap = [(i, (i + 1) % cores) for i in range(cores)]
    own_starts = package[:, 0, package.shape[2] - 1].astype(jnp.int32)
    seq_states, seq_cotan, _ = lax.optimization_barrier((seq_states, seq_cotan, weight_pair))
    own_states = lax.all_gather(seq_states, "dp", axis=0, tiled=False)
    other_starts = lax.ppermute(own_starts, "replica", swap)
    positions = lax.broadcasted_iota(jnp.int32, (tokens, 1), 0)
    live_cotan = jnp.where(positions < lengths[0], seq_cotan, jnp.zeros_like(seq_cotan))

    def shifted_perm(k):
        return [(i, (i + k) % chips) for i in range(chips)]

    cotan_blocks = []
    for k in range(chips):
        block = lax.dynamic_slice_in_dim(live_cotan, lax.rem(chip + k, chips) * units, units, 1)
        cotan_blocks.append(lax.ppermute(block, "dp", shifted_perm(k)) if k else block)
    stacked = jnp.stack(cotan_blocks)
    token_cotan = jnp.concatenate(
        [
            lax.dynamic_index_in_dim(stacked, lax.rem(chip - j + chips, chips), 0, keepdims=False)
            for j in range(chips)
        ],
        axis=0,
    )

    adversary = prompt.astype(jnp.float32)
    for attack_step in range(step_sizes.shape[0]):
        shifted = prompt_base + adversary[None]
        inverse_rms = row_scale(shifted)
        normalized = (shifted * inverse_rms * norm_gain).astype(jnp.bfloat16)
        unit_grads = hidden_grads(normalized.reshape(chips * count, width), weight_pair, prompt_cotan)
        feature_grad = lax.dot_general(
            unit_grads, weight_pair, (((1,), (1,)), ((), ())), preferred_element_type=jnp.float32
        ).reshape(chips, count, width)
        scaled = norm_gain * feature_grad
        feature_mean = jnp.mean(shifted * scaled, axis=-1, keepdims=True)
        partial = jnp.sum(
            inverse_rms * scaled - shifted * (inverse_rms * inverse_rms * inverse_rms) * feature_mean,
            axis=0,
        )
        adversary = apply_step(partial, adversary, step_sizes[attack_step : attack_step + 1])
        if attack_step == step_sizes.shape[0] - 2:
            own_states, adversary = lax.optimization_barrier((own_states, adversary))
            other_states = lax.ppermute(own_states, "replica", swap)

    high = lax.reduce_precision(adversary, 8, 7)
    middle = lax.reduce_precision(adversary - high, 8, 7)
    low = adversary - high - middle
    parts = jnp.concatenate([high, middle, low], axis=0).astype(jnp.bfloat16)
    own_normed = normed_rows(own_starts, own_states, parts, norm_gain)
    own_grads = hidden_grads(own_normed, weight_pair, token_cotan.astype(jnp.float32))
    other_grads = lax.ppermute(own_grads, "replica", swap)
    other_normed = normed_rows(other_starts, other_states, parts, norm_gain)

    block_width = width // (chips * cores)
    dims = (((0,), (0,)), ((), ()))
    squares = 0.0
    received = [None] * chips
    for k in [2 % chips, *[i for i in range(1, chips) if i != 2 % chips], 0] if chips > 2 else range(chips):
        start = (lax.rem(chip + k, chips) * cores + core) * block_width
        block = lax.dot_general(
            lax.dynamic_slice_in_dim(own_normed, start, block_width, 1), own_grads, dims,
            preferred_element_type=jnp.float32,
        ) + lax.dot_general(
            lax.dynamic_slice_in_dim(other_normed, start, block_width, 1), other_grads, dims,
            preferred_element_type=jnp.float32,
        )
        squares = squares + jnp.sum(block * block)
        sent = block.astype(jnp.bfloat16)
        received[k] = lax.ppermute(sent, "dp", shifted_perm(k)) if k else sent
    squares = sum_everywhere(squares)
    scale = lax.rsqrt(squares / (2 * D * FF) + 1e-06)
    stacked = jnp.stack(received)
    pieces = [
        lax.dynamic_index_in_dim(stacked, lax.rem(chip - j + chips, chips), 0, keepdims=False)
        for j in range(chips)
    ]
    weight_step = jnp.concatenate(
        [piece.reshape(block_width, 2, units) for piece in pieces], axis=2
    )
    weight_step = (weight_step.astype(jnp.float32) * scale).astype(jnp.bfloat16)
    column_count = width // lax.axis_size("tensor")
    prompt_final = lax.dynamic_slice_in_dim(
        adversary, lax.axis_index("tensor") * column_count, column_count, 1
    )
    return (prompt_final, weight_step)


def relative_devices(chip, core):
    pairs = []
    for m in range(4):
        other_chip = [chip, chip + 1 - 2 * lax.rem(chip, 2), lax.rem(chip + 2, 4), 3 - chip][m]
        for q in range(2):
            pairs.append((other_chip, core if q == 0 else 1 - core))
    return pairs


def main_kernel(
    tensors, steps,
    pair, normed, cot_ref, prompt_in, base_rows, base_cot, gain_ref, step_ref,
    adv_out, xp_out, g_all, gp_all,
    rows_v, w_buf, keep_v, send_v, got_v, g_v,
    base_buf, cot_buf, near_v, far_v, x_v, fg_v, inv_v, adv, part,
    send_a, send_b, recv_s, recv_a, recv_b, recv_c, gp_v,
    s_local, s_w, s_r, r_r, s_f, r_f, s_g, r_g, s_p, r_p, s_c, r_c,
    s_0, r_0, s_1, r_1, s_2, r_2, s_3, r_3, s_o, r_o,
):
    t = lax.axis_index("tensor")
    chip = lax.axis_index("dp")
    core = lax.axis_index("replica")
    me = chip * 2 + core
    rel = relative_devices(chip, core)
    ids = [{"dp": a, "replica": b} for a, b in rel]
    place = [a * 2 + b for a, b in rel]
    wide = near_v.shape[2]
    half = pair.shape[1]
    units = pair.shape[2] // 4
    count, width = base_rows.shape
    block = width // 8
    base = normed.shape[0]

    def remote(src, dst, send, recv, device):
        return pltpu.make_async_remote_copy(
            src_ref=src, dst_ref=dst, send_sem=send, recv_sem=recv,
            device_id=device, device_id_type=MESH,
        )

    def w_copy(i):
        return pltpu.make_async_copy(pair.at[:, :, pl.ds(i * units, units)], w_buf.at[i % 2], s_w.at[i % 2])

    w_copies = [w_copy(0), w_copy(1)]
    for copy in w_copies:
        copy.start()
    near_half = pl.ds(pl.multiple_of(core * half, 128), half)
    far_half = pl.ds(pl.multiple_of((1 - core) * half, 128), half)
    rows_local = pltpu.make_async_copy(normed.at[:, near_half], rows_v.at[pl.ds(0, base)], s_local.at[0])
    rows_local.start()

    barrier = pltpu.get_barrier_semaphore()
    line_ids = [{"tensor": lax.rem(t + k, tensors)} for k in range(1, tensors)]
    for device in ids[1:] + line_ids:
        pl.semaphore_signal(barrier, inc=1, device_id=device, device_id_type=MESH)
    pl.semaphore_wait(barrier, 7 + tensors - 1)

    rows_far = remote(normed.at[:, far_half], rows_v.at[pl.ds(base, base)], s_r.at[0], r_r.at[0], ids[1])
    rows_far.start()
    rows_a = [remote(base_rows, base_buf.at[me], s_p.at[m], r_p.at[m], ids[2 * m]) for m in range(1, 4)]

    def first_unit(a, b):
        return pl.multiple_of(a * units + b * (units - wide), 128)

    cots = [None] + [
        remote(
            base_cot.at[:, pl.ds(first_unit(*rel[j]), wide)], cot_buf.at[me], s_c.at[j], r_c.at[j], ids[j]
        )
        for j in range(1, 8)
    ]
    w_far = remote(pair.at[:, :, pl.ds(first_unit(chip, 1 - core), wide)], far_v, s_r.at[1], r_r.at[1], ids[1])
    local = [
        pltpu.make_async_copy(base_rows, base_buf.at[me], s_local.at[1]),
        pltpu.make_async_copy(base_cot.at[:, pl.ds(first_unit(chip, core), wide)], cot_buf.at[me], s_local.at[2]),
        pltpu.make_async_copy(pair.at[:, :, pl.ds(first_unit(chip, core), wide)], near_v, s_local.at[3]),
    ]
    rows_b = [
        remote(base_buf.at[place[2 * m]], base_buf.at[place[2 * m]], s_p.at[4 + m], r_p.at[4 + m], ids[1])
        for m in range(4)
    ]
    for copy in rows_a + cots[1:] + local:
        copy.start()

    gx = [remote(g_v.at[i], g_all.at[2, i], s_g.at[i], r_g.at[i], ids[2]) for i in range(4)]
    gy = [remote(g_v.at[i], g_all.at[4, i], s_g.at[4 + i], r_g.at[4 + i], ids[4]) for i in range(4)]
    gs = [remote(g_v.at[i], g_all.at[1, i], s_g.at[8 + i], r_g.at[8 + i], ids[1]) for i in range(4)]
    gl = [pltpu.make_async_copy(g_v.at[i], g_all.at[0, i], s_local.at[5 + i]) for i in range(4)]
    fd = [
        remote(g_all.at[2 if i < 2 else 4, i], g_all.at[6, i], s_g.at[12 + i], r_g.at[12 + i], ids[4 if i < 2 else 2])
        for i in range(4)
    ]
    side = [None] + [
        [
            remote(g_all.at[2 * m, i], g_all.at[2 * m + 1, i], s_g.at[12 + 4 * m + i], r_g.at[12 + 4 * m + i], ids[1])
            for i in range(4)
        ]
        for m in range(1, 4)
    ]
    swaps = [remote(send_v.at[i % 2], got_v.at[i], s_f.at[i], r_f.at[i], ids[1]) for i in range(4)]

    def combine(i):
        swaps[i].wait_recv()
        gate = keep_v[i % 2, 0] + got_v[i, 0]
        up = keep_v[i % 2, 1] + got_v[i, 1]
        act, slope = silu_parts(gate)
        cot = cot_ref[:, i * units : (i + 1) * units].astype(jnp.float32)
        g_v[i, :, :units] = (cot * up * slope).astype(jnp.bfloat16)
        g_v[i, :, units:] = (cot * act).astype(jnp.bfloat16)
        for copy in (gx[i], gy[i], gs[i], gl[i]):
            copy.start()

    rows_local.wait()
    rows_far.wait_recv()
    for i in range(4):
        w_copies[i].wait()
        if i >= 2:
            swaps[i - 2].wait_send()
        for p in range(2):
            product = jnp.dot(rows_v[...], w_buf[i % 2, p], preferred_element_type=jnp.float32)
            keep_v[i % 2, p] = product[:base]
            send_v[i % 2, p] = product[base:]
        swaps[i].start()
        if i < 2:
            w_copies.append(w_copy(i + 2))
            w_copies[-1].start()
        if i == 0:
            local[0].wait()
            rows_b[0].start()
            w_far.start()
        else:
            combine(i - 1)
        if i == 2:
            for m in range(1, 4):
                rows_a[m - 1].wait_recv()
                rows_b[m].start()
    adv[...] = prompt_in[...].astype(jnp.float32)
    combine(3)
    for copy in rows_b + cots[1:] + [w_far]:
        copy.wait_recv()
    for copy in local[1:]:
        copy.wait()
    lane = lax.broadcasted_iota(jnp.int32, (count, wide), 1)
    keep = lane >= core * (2 * wide - units)

    def norm_rows():
        def one(b, _):
            shifted = base_buf[b].astype(jnp.float32) + adv[...]
            inverse = lax.rsqrt(jnp.mean(shifted * shifted, axis=-1, keepdims=True) + 1e-05)
            x_v[pl.ds(pl.multiple_of(b * count, count), count)] = (shifted * inverse * gain_ref[...]).astype(jnp.bfloat16)
            inv_v[b] = jnp.broadcast_to(inverse, (count, 128))
            return 0
        lax.fori_loop(0, 8, one, 0)

    def unit_grads():
        near = x_v[:, near_half]
        far = x_v[:, far_half]
        gate, up = [
            jnp.dot(near, near_v[p], preferred_element_type=jnp.float32)
            + jnp.dot(far, far_v[p], preferred_element_type=jnp.float32)
            for p in range(2)
        ]
        act, slope = silu_parts(gate)
        cot = jnp.concatenate(
            [jnp.where(keep, cot_buf[b].astype(jnp.float32), 0.0) for b in range(8)], axis=0
        )
        gp_v[:, pl.ds(0, wide)] = (cot * up * slope).astype(jnp.bfloat16)
        gp_v[:, pl.ds(wide, wide)] = (cot * act).astype(jnp.bfloat16)

    dims = (((1,), (1,)), ((), ()))
    chunk = 512

    def feature_grads():
        for source, start in ((near_v, core * half), (far_v, (1 - core) * half)):
            def one(i, _):
                rows = pl.ds(pl.multiple_of(i * chunk, chunk), chunk)
                fg_v[:, pl.ds(pl.multiple_of(start + i * chunk, chunk), chunk)] = lax.dot_general(
                    gp_v[:, pl.ds(0, wide)], source[0, rows], dims, preferred_element_type=jnp.float32
                ) + lax.dot_general(
                    gp_v[:, pl.ds(wide, wide)], source[1, rows], dims, preferred_element_type=jnp.float32
                )
                return 0
            lax.fori_loop(0, half // chunk, one, 0)

    def row_grads():
        part[...] = jnp.zeros_like(part)
        def one(b, _):
            shifted = base_buf[b].astype(jnp.float32) + adv[...]
            scaled = gain_ref[...] * fg_v[pl.ds(pl.multiple_of(b * count, count), count)]
            inverse = inv_v[b][:, :1]
            middle = jnp.mean(shifted * scaled, axis=-1, keepdims=True)
            part[...] += inverse * scaled - shifted * (inverse * inverse * inverse * middle)
            return 0
        lax.fori_loop(0, 8, one, 0)

    waits = []

    def exchange(k):
        for p in range(8):
            send_a[k, p % 2, p // 2] = part[:, p * block : (p + 1) * block].astype(jnp.bfloat16)
        sib = remote(send_a.at[k, 1 - core], recv_s.at[k], s_0.at[k], r_0.at[k], ids[1])
        sib.start()
        sib.wait_recv()
        for a in range(4):
            send_b[k, a] = (
                send_a[k, core, a].astype(jnp.float32) + recv_s[k, a].astype(jnp.float32)
            ).astype(jnp.bfloat16)
        first = [
            remote(send_b.at[k, rel[2 * m][0]], recv_a.at[k, m], s_1.at[k, m], r_1.at[k, m], ids[2 * m])
            for m in range(1, 4)
        ]
        for copy in first:
            copy.start()
        total = send_b[k, chip].astype(jnp.float32)
        for m in range(1, 4):
            first[m - 1].wait_recv()
            total = total + recv_a[k, m].astype(jnp.float32)
        recv_b[k, t] = total.astype(jnp.bfloat16)
        second = [
            remote(recv_b.at[k, t], recv_b.at[k, t], s_2.at[k, j], r_2.at[k, j], line_ids[j])
            for j in range(tensors - 1)
        ]
        for copy in second:
            copy.start()
        for copy in second:
            copy.wait_recv()
        total = recv_b[k, 0].astype(jnp.float32)
        for j in range(1, tensors):
            total = total + recv_b[k, j].astype(jnp.float32)
        recv_c[k, me] = total.astype(jnp.bfloat16)
        third = [
            remote(recv_c.at[k, me], recv_c.at[k, me], s_3.at[k, m], r_3.at[k, m], ids[2 * m]) for m in range(1, 4)
        ]
        fourth = [
            remote(
                recv_c.at[k, place[2 * m]], recv_c.at[k, place[2 * m]],
                s_3.at[k, 4 + m], r_3.at[k, 4 + m], ids[1],
            )
            for m in range(4)
        ]
        for copy in third + fourth[:1]:
            copy.start()
        for m in range(1, 4):
            third[m - 1].wait_recv()
            fourth[m].start()
        for copy in fourth:
            copy.wait_recv()
        waits.extend([sib] + first + second + third + fourth)
        square = jnp.zeros((count, 1), jnp.float32)
        for p in range(8):
            piece = recv_c[k, p].astype(jnp.float32)
            square = square + jnp.sum(piece * piece, axis=-1, keepdims=True)
        scale = step_ref[k] * lax.rsqrt(square / width + 1e-06)
        for p in range(8):
            at = slice(p * block, (p + 1) * block)
            adv[:, at] = adv[:, at] + scale * recv_c[k, p].astype(jnp.float32)

    def forward_some(k):
        if k == 0:
            for i in range(2):
                gx[i].wait_recv()
                fd[i].start()
                side[1][i].start()
        if k == 1:
            for i in range(2, 4):
                gy[i].wait_recv()
                fd[i].start()
                side[2][i].start()

    for k in range(steps):
        norm_rows()
        unit_grads()
        feature_grads()
        row_grads()
        exchange(k)
        forward_some(k)
    for k in range(steps, 2):
        forward_some(k)
    adv_out[...] = adv[...]
    norm_rows()
    unit_grads()
    xp_out[...] = x_v[:, pl.ds(pl.multiple_of(me * block, 128), block)]
    mid = 4 * count
    parts = [pl.ds(0, mid), pl.ds(mid, mid)]

    def hop(slot, h, k, device):
        ref = gp_all.at[slot, parts[h]]
        return remote(ref, ref, s_o.at[k], r_o.at[k], device)

    ox = [remote(gp_v.at[parts[h]], gp_all.at[me, parts[h]], s_o.at[h], r_o.at[h], ids[2]) for h in range(2)]
    oy = [remote(gp_v.at[parts[h]], gp_all.at[me, parts[h]], s_o.at[2 + h], r_o.at[2 + h], ids[4]) for h in range(2)]
    os = remote(gp_v, gp_all.at[me], s_o.at[4], r_o.at[4], ids[1])
    ol = pltpu.make_async_copy(gp_v, gp_all.at[me], s_local.at[4])
    od = [hop(place[2], 0, 5, ids[4]), hop(place[4], 1, 6, ids[2])]
    sx = [hop(place[2], h, 7 + h, ids[1]) for h in range(2)]
    sy = [hop(place[4], h, 9 + h, ids[1]) for h in range(2)]
    sd = [hop(place[6], h, 11 + h, ids[1]) for h in range(2)]
    for copy in (ox[0], oy[1], ox[1], oy[0], os, ol):
        copy.start()
    ox[0].wait_recv()
    od[0].start()
    sx[0].start()
    oy[1].wait_recv()
    od[1].start()
    sy[1].start()
    for i in range(2, 4):
        gx[i].wait_recv()
        side[1][i].start()
    for i in range(2):
        gy[i].wait_recv()
        side[2][i].start()
    for i in range(4):
        fd[i].wait_recv()
        side[3][i].start()
    ox[1].wait_recv()
    sx[1].start()
    oy[0].wait_recv()
    sy[0].start()
    for h in range(2):
        od[h].wait_recv()
        sd[h].start()
    sides = side[1] + side[2] + side[3]
    for copy in gs + sides + [os] + sx + sy + sd:
        copy.wait_recv()
    for copy in gl + [ol]:
        copy.wait()
    for copy in [rows_far, w_far] + rows_a + rows_b + cots[1:] + swaps[2:] + gx + gy + gs + fd + sides + waits:
        copy.wait_send()
    for copy in ox + oy + [os] + od + sx + sy + sd:
        copy.wait_send()


def main_call(pair, normed, cot, prompt, base_rows, base_cot, gain, step_sizes):
    tensors = lax.axis_size("tensor")
    steps = step_sizes.shape[0]
    count, width = base_rows.shape
    half, shard = pair.shape[1:]
    units, wide = shard // 4, 512
    block = width // 8
    base = normed.shape[0]
    bf, f32 = jnp.bfloat16, jnp.float32
    dma = pltpu.SemaphoreType.DMA
    vmem = pl.BlockSpec(memory_space=pltpu.VMEM)
    hbm = pl.BlockSpec(memory_space=pl.ANY)
    return pl.pallas_call(
        functools.partial(main_kernel, tensors, steps),
        out_shape=[
            jax.ShapeDtypeStruct((count, width), f32),
            jax.ShapeDtypeStruct((8 * count, block), bf),
            jax.ShapeDtypeStruct((8, 4, base, 2 * units), bf),
            jax.ShapeDtypeStruct((8, 8 * count, 2 * wide), bf),
        ],
        in_specs=[hbm, hbm, vmem, vmem, hbm, hbm, vmem, pl.BlockSpec(memory_space=pltpu.SMEM)],
        out_specs=[vmem, vmem, hbm, hbm],
        scratch_shapes=[
            pltpu.VMEM((2 * base, half), bf),
            pltpu.VMEM((2, 2, half, units), bf),
            pltpu.VMEM((2, 2, base, units), f32),
            pltpu.VMEM((2, 2, base, units), f32),
            pltpu.VMEM((4, 2, base, units), f32),
            pltpu.VMEM((4, base, 2 * units), bf),
            pltpu.VMEM((8, count, width), bf),
            pltpu.VMEM((8, count, wide), bf),
            pltpu.VMEM((2, half, wide), bf),
            pltpu.VMEM((2, half, wide), bf),
            pltpu.VMEM((8 * count, width), bf),
            pltpu.VMEM((8 * count, width), f32),
            pltpu.VMEM((8, count, 128), f32),
            pltpu.VMEM((count, width), f32),
            pltpu.VMEM((count, width), f32),
            pltpu.VMEM((steps, 2, 4, count, block), bf),
            pltpu.VMEM((steps, 4, count, block), bf),
            pltpu.VMEM((steps, 4, count, block), bf),
            pltpu.VMEM((steps, 4, count, block), bf),
            pltpu.VMEM((steps, tensors, count, block), bf),
            pltpu.VMEM((steps, 8, count, block), bf),
            pltpu.VMEM((8 * count, 2 * wide), bf),
        ]
        + [dma((9,))] + [dma((2,))] * 3 + [dma((4,))] * 2 + [dma((28,))] * 2 + [dma((8,))] * 4
        + [dma((steps,))] * 2 + [dma((steps, 4))] * 2 + [dma((steps, tensors))] * 2
        + [dma((steps, 8))] * 2 + [dma((13,))] * 2,
        compiler_params=pltpu.CompilerParams(
            collective_id=2, has_side_effects=True, vmem_limit_bytes=62 << 20
        ),
        cost_estimate=pl.CostEstimate(flops=100_000_000_000, bytes_accessed=100_000_000, transcendentals=0),
        name="attack_and_gather",
    )(pair, normed, cot, prompt, base_rows, base_cot, gain.reshape(1, width), step_sizes)


def grad_kernel(x_ref, xp_ref, g_ref, gp0_ref, gp1_ref, out_ref, sq_ref, xt_v, xpt_v):
    step = pl.program_id(0) * pl.num_programs(1) + pl.program_id(1)

    @pl.when(step == 0)
    def _():
        xt_v[...] = x_ref[...].T
        xpt_v[...] = xp_ref[...].T
        sq_ref[...] = jnp.zeros_like(sq_ref)

    extra = 2 * gp0_ref.shape[2] - out_ref.shape[2]
    rows = g_ref.shape[0] * g_ref.shape[2]
    gp = jnp.concatenate([gp0_ref[0], gp1_ref[0][:, extra:]], axis=1)
    block = jnp.dot(
        xt_v[...], g_ref[...].reshape(rows, g_ref.shape[3]), preferred_element_type=jnp.float32
    ) + jnp.dot(xpt_v[...], gp, preferred_element_type=jnp.float32)
    out_ref[0] = block
    sq_ref[...] += jnp.sum((block * block).reshape(-1, 8, block.shape[1]), axis=0)


def grad_call(x_all, xp, g_all, gp_all):
    eight, _, own_base, pair_units = g_all.shape
    cols = 4 * pair_units
    block = x_all.shape[2]
    wide = gp_all.shape[2] // 2
    shard = cols // 2
    units = shard // 4
    prompts = xp.shape[0]
    f32 = jnp.float32
    return pl.pallas_call(
        grad_kernel,
        out_shape=[
            jax.ShapeDtypeStruct((2, block, shard), f32),
            jax.ShapeDtypeStruct((8, units), f32),
        ],
        grid=(2, 4),
        in_specs=[
            pl.BlockSpec((eight * own_base, block), lambda p, j: (0, 0)),
            pl.BlockSpec((prompts, block), lambda p, j: (0, 0)),
            pl.BlockSpec((eight, 1, own_base, units), lambda p, j: (0, j, 0, p)),
            pl.BlockSpec((1, prompts, wide), lambda p, j: (2 * j, 0, p)),
            pl.BlockSpec((1, prompts, wide), lambda p, j: (2 * j + 1, 0, p)),
        ],
        out_specs=[
            pl.BlockSpec((1, block, units), lambda p, j: (p, 0, j)),
            pl.BlockSpec((8, units), lambda p, j: (0, 0)),
        ],
        scratch_shapes=[
            pltpu.VMEM((block, eight * own_base), jnp.bfloat16),
            pltpu.VMEM((block, prompts), jnp.bfloat16),
        ],
        compiler_params=pltpu.CompilerParams(vmem_limit_bytes=48 << 20),
        cost_estimate=pl.CostEstimate(
            flops=2 * block * cols * (eight * own_base + prompts), bytes_accessed=50_000_000, transcendentals=0
        ),
        name="weight_grad",
    )(x_all.reshape(eight * own_base, block), xp, g_all, gp_all, gp_all)


def result_kernel(scale_ref, grad_ref, out_ref):
    _, rows, cols = grad_ref.shape
    n = 128
    to = lax.broadcasted_iota(jnp.int32, (2 * n, 2 * n), 0)
    source = jnp.where(lax.rem(to, 2) == 0, to // 2, n + to // 2)
    order = jnp.where(lax.broadcasted_iota(jnp.int32, (2 * n, 2 * n), 1) == source, 1.0, 0.0).astype(jnp.bfloat16)
    for r in range(0, rows, n):
        both = jnp.concatenate(
            [(grad_ref[p, r : r + n] * scale_ref[0]).astype(jnp.bfloat16) for p in range(2)], axis=0
        )
        mixed = jnp.dot(order, both, preferred_element_type=jnp.float32).astype(jnp.bfloat16)
        out_ref[r : r + n] = mixed.reshape(n, 2, cols)


def result_call(scale, weight_grad):
    _, rows, shard = weight_grad.shape
    cols = 512
    return pl.pallas_call(
        result_kernel,
        out_shape=jax.ShapeDtypeStruct((rows, 2, shard), jnp.bfloat16),
        grid=(shard // cols,),
        in_specs=[
            pl.BlockSpec(memory_space=pltpu.SMEM),
            pl.BlockSpec((2, rows, cols), lambda j: (0, 0, j)),
        ],
        out_specs=pl.BlockSpec((rows, 2, cols), lambda j: (0, 0, j)),
        compiler_params=pltpu.CompilerParams(vmem_limit_bytes=48 << 20),
        name="scaled_result",
    )(scale.reshape(1), weight_grad)


def per_device(states, norm_gain, gate_up, cotangent, prompt, step_sizes, insert_at, lengths):
    chips, cores = lax.axis_size("dp"), lax.axis_size("replica")
    shard = gate_up.shape[2]
    count = prompt.shape[0]
    fits = (
        chips == 4 and cores == 2 and states.shape[0] == 1 and shard % (chips * 128) == 0
        and shard // chips > 512 and shard // chips <= 1024 and shard % 512 == 0
        and gate_up.shape[0] % 1024 == 0 and count % 16 == 0 and (states.shape[1] - count) % 16 == 0
    )
    if not fits:
        return per_device_general(
            states, norm_gain, gate_up, cotangent, prompt, step_sizes, insert_at, lengths
        )
    chip, core = lax.axis_index("dp"), lax.axis_index("replica")
    half = gate_up.shape[0]
    width = half * cores
    tokens = states.shape[1]
    base = tokens - count
    units = shard // chips
    start = insert_at[0]

    pair = jnp.transpose(gate_up, (1, 0, 2))

    spot = lax.broadcasted_iota(jnp.int32, (base, 1), 0)
    ahead = spot < start
    position = jnp.where(ahead, spot, spot + count)
    rows = jnp.where(ahead, states[0, :base], states[0, count:]).astype(jnp.float32)
    cot = jnp.where(ahead, cotangent[0, :base], cotangent[0, count:])
    cot = jnp.where(position < lengths[0], cot, jnp.zeros_like(cot))
    normed = (rows * row_scale(rows) * norm_gain).astype(jnp.bfloat16)
    base_rows = lax.dynamic_slice_in_dim(states[0], start, count, 0)
    base_cot = lax.dynamic_slice_in_dim(cotangent[0], start, count, 0)

    block = width // 8
    x_pieces = []
    for j, (a, b) in enumerate(relative_devices(chip, core)):
        piece = lax.dynamic_slice_in_dim(normed, (a * 2 + b) * block, block, 1)
        if j:
            perm = [(i, ((i // 2) ^ (j // 2)) * 2 + ((i % 2) ^ (j % 2))) for i in range(8)]
            piece = lax.ppermute(piece, ("dp", "replica"), perm)
        x_pieces.append(piece)
    x_all = jnp.stack(x_pieces)
    normed, x_all = lax.optimization_barrier((normed, x_all))

    adversary, xp, g_all, gp_all = main_call(
        pair, normed, cot, prompt, base_rows, base_cot, norm_gain, step_sizes
    )
    weight_grad, squares = grad_call(x_all, xp, g_all, gp_all)
    squares = sum_everywhere(jnp.sum(squares))
    scale = lax.rsqrt(squares / (2 * D * FF) + 1e-06)
    weight_step = result_call(scale, weight_grad)
    column_count = width // lax.axis_size("tensor")
    prompt_final = lax.dynamic_slice_in_dim(
        adversary, lax.axis_index("tensor") * column_count, column_count, 1
    )
    return (prompt_final, weight_step)


def solution(mesh):
    return jax.shard_map(
        per_device,
        mesh=mesh,
        in_specs=(
            P(("dp", "replica"), None, None),
            P(),
            P("replica", None, "tensor"),
            P(("dp", "replica"), None, "tensor"),
            P(),
            P(),
            P(("dp", "replica")),
            P(("dp", "replica")),
        ),
        out_specs=(P(None, "tensor"), P(("dp", "replica"), None, "tensor")),
        check_vma=False,
    )
```

```python
import functools

import jax
import jax.numpy as jnp
from jax import lax
from jax.experimental import pallas as pl
from jax.experimental.pallas import tpu as pltpu
from jax.sharding import PartitionSpec as P

D = 4096
FF = 14336
MESH = pl.DeviceIdType.MESH


def row_scale(feature_rows):
    return lax.rsqrt(jnp.mean(feature_rows * feature_rows, axis=-1, keepdims=True) + 1e-05)


def silu_parts(gate_values):
    sigmoid_value = jax.nn.sigmoid(gate_values)
    return (
        gate_values * sigmoid_value,
        sigmoid_value * (1.0 + gate_values * (1.0 - sigmoid_value)),
    )


def hidden_grads(normalized, weight_pair, cotan_rows):
    unit_count = weight_pair.shape[1] // 2
    projected = jnp.dot(normalized, weight_pair, preferred_element_type=jnp.float32)
    activated, derivative = silu_parts(projected[:, :unit_count])
    up_part = projected[:, unit_count:]
    return jnp.concatenate(
        [cotan_rows * up_part * derivative, cotan_rows * activated], axis=1
    ).astype(jnp.bfloat16)


def step_kernel(
    tensors, chips, cores, partial_ref, adversary_ref, step_ref, out_ref,
    plane_buf, line_buf, mine, send1, recv1, send2, recv2, send3, recv3, send4, recv4,
):
    group = chips * cores
    t = lax.axis_index("tensor")
    g = lax.axis_index("dp") * cores + lax.axis_index("replica")
    rows = partial_ref.shape[0] // group
    own = rows // tensors
    plane = [lax.rem(g + k, group) for k in range(1, group)]
    line = [lax.rem(t + k, tensors) for k in range(1, tensors)]
    plane_ids = [{"dp": p // cores, "replica": lax.rem(p, cores)} for p in plane]
    line_ids = [{"tensor": p} for p in line]

    barrier = pltpu.get_barrier_semaphore()
    for device in plane_ids + line_ids:
        pl.semaphore_signal(barrier, inc=1, device_id=device, device_id_type=MESH)
    pl.semaphore_wait(barrier, group + tensors - 2)

    def exchange(pairs, ids, sends, recvs):
        copies = []
        for k, ((source, target), device) in enumerate(zip(pairs, ids)):
            copy = pltpu.make_async_remote_copy(
                src_ref=source, dst_ref=target, send_sem=sends.at[k], recv_sem=recvs.at[k],
                device_id=device, device_id_type=MESH,
            )
            copy.start()
            copies.append(copy)
        return copies

    first = exchange(
        [(partial_ref.at[pl.ds(p * rows, rows)], plane_buf.at[k]) for k, p in enumerate(plane)],
        plane_ids, send1, recv1,
    )
    total = partial_ref[pl.ds(g * rows, rows)]
    for k, copy in enumerate(first):
        copy.wait_recv()
        total = total + plane_buf[k]
    mine[...] = total
    second = exchange(
        [(mine.at[pl.ds(p * own, own)], line_buf.at[k]) for k, p in enumerate(line)],
        line_ids, send2, recv2,
    )
    grad = mine[pl.ds(t * own, own)]
    for k, copy in enumerate(second):
        copy.wait_recv()
        grad = grad + line_buf[k]
    square = jnp.sum(jnp.sum(grad * grad, axis=2, keepdims=True), axis=1, keepdims=True)
    count = partial_ref.shape[1] * partial_ref.shape[2]
    row = g * rows + t * own
    block = pl.ds(row, own)
    out_ref[block] = adversary_ref[block] + step_ref[0] * grad * lax.rsqrt(square / count + 1e-06)
    third = exchange([(out_ref.at[block], out_ref.at[block])] * len(line), line_ids, send3, recv3)
    for copy in third:
        copy.wait_recv()
    wide = pl.ds(g * rows, rows)
    fourth = exchange([(out_ref.at[wide], out_ref.at[wide])] * len(plane), plane_ids, send4, recv4)
    for copy in fourth:
        copy.wait_recv()
    for copy in first + second + third + fourth:
        copy.wait_send()


def apply_step(partial, adversary, step_size):
    tensors, chips, cores = (lax.axis_size(a) for a in ("tensor", "dp", "replica"))
    group = chips * cores
    count, width = partial.shape
    if count % (group * tensors) == 0 and width % 1024 == 0:
        shape = (count, 8, width // 8)
        rows = count // group
        own = rows // tensors
        dma = pltpu.SemaphoreType.DMA
        vmem = pl.BlockSpec(memory_space=pltpu.VMEM)
        result = pl.pallas_call(
            functools.partial(step_kernel, tensors, chips, cores),
            out_shape=jax.ShapeDtypeStruct(shape, jnp.float32),
            in_specs=[vmem, vmem, pl.BlockSpec(memory_space=pltpu.SMEM)],
            out_specs=vmem,
            scratch_shapes=[
                pltpu.VMEM((group - 1, rows) + shape[1:], jnp.float32),
                pltpu.VMEM((tensors - 1, own) + shape[1:], jnp.float32),
                pltpu.VMEM((rows,) + shape[1:], jnp.float32),
            ]
            + [dma((group - 1,))] * 2 + [dma((tensors - 1,))] * 4 + [dma((group - 1,))] * 2,
            compiler_params=pltpu.CompilerParams(
                collective_id=0, has_side_effects=True, vmem_limit_bytes=16 << 20
            ),
            cost_estimate=pl.CostEstimate(
                flops=20_000_000_000, bytes_accessed=3 * count * width * 4, transcendentals=0
            ),
            name="attack_step",
        )(partial.reshape(shape), adversary.reshape(shape), step_size)
        return result.reshape(count, width)
    grad = lax.psum(partial, ("tensor", "dp", "replica"))
    scale = lax.rsqrt(jnp.mean(grad * grad, axis=-1, keepdims=True) + 1e-06)
    return adversary + step_size[0] * grad * scale


def scalar_kernel(tensors, chips, cores, value_ref, out_ref, buf1, buf2, mine, send1, recv1, send2, recv2):
    group = chips * cores
    t = lax.axis_index("tensor")
    g = lax.axis_index("dp") * cores + lax.axis_index("replica")
    plane = [lax.rem(g + k, group) for k in range(1, group)]
    plane_ids = [{"dp": p // cores, "replica": lax.rem(p, cores)} for p in plane]
    line_ids = [{"tensor": lax.rem(t + k, tensors)} for k in range(1, tensors)]
    barrier = pltpu.get_barrier_semaphore()
    for device in plane_ids + line_ids:
        pl.semaphore_signal(barrier, inc=1, device_id=device, device_id_type=MESH)
    pl.semaphore_wait(barrier, group + tensors - 2)
    copies = []
    total = value_ref[...]
    source = value_ref
    for ids, buf, sends, recvs in ((plane_ids, buf1, send1, recv1), (line_ids, buf2, send2, recv2)):
        stage = []
        for k, device in enumerate(ids):
            copy = pltpu.make_async_remote_copy(
                src_ref=source, dst_ref=buf.at[k], send_sem=sends.at[k], recv_sem=recvs.at[k],
                device_id=device, device_id_type=MESH,
            )
            copy.start()
            stage.append(copy)
        for k, copy in enumerate(stage):
            copy.wait_recv()
            total = total + buf[k]
        copies += stage
        if buf is buf1:
            mine[...] = total
            source = mine
    out_ref[...] = total
    for copy in copies:
        copy.wait_send()


def sum_everywhere(value):
    tensors, chips, cores = (lax.axis_size(a) for a in ("tensor", "dp", "replica"))
    group = chips * cores
    if not 1 < tensors <= 8 or not 1 < group <= 16:
        return lax.psum(value, ("tensor", "dp", "replica"))
    dma = pltpu.SemaphoreType.DMA
    vmem = pl.BlockSpec(memory_space=pltpu.VMEM)
    return pl.pallas_call(
        functools.partial(scalar_kernel, tensors, chips, cores),
        out_shape=jax.ShapeDtypeStruct((8, 128), jnp.float32),
        in_specs=[vmem],
        out_specs=vmem,
        scratch_shapes=[
            pltpu.VMEM((group - 1, 8, 128), jnp.float32),
            pltpu.VMEM((tensors - 1, 8, 128), jnp.float32),
            pltpu.VMEM((8, 128), jnp.float32),
        ]
        + [dma((group - 1,))] * 2 + [dma((tensors - 1,))] * 2,
        compiler_params=pltpu.CompilerParams(
            collective_id=1, has_side_effects=True, vmem_limit_bytes=4 << 20
        ),
        name="scalar_sum",
    )(jnp.full((8, 128), value, jnp.float32))[0, 0]


def norm_kernel(start_ref, state_ref, parts_ref, gain_ref, out_ref):
    slots = parts_ref.shape[0] // 3
    tokens = state_ref.shape[1]
    shape = (tokens, 3 * slots)
    slot = lax.broadcasted_iota(jnp.int32, shape, 0) - start_ref[pl.program_id(0)]
    column = lax.rem(lax.broadcasted_iota(jnp.int32, shape, 1), slots)
    placed = jnp.dot(
        jnp.where(slot == column, 1.0, 0.0).astype(jnp.bfloat16), parts_ref[...],
        preferred_element_type=jnp.float32,
    )
    rows = state_ref[0].astype(jnp.float32) + placed
    scale = lax.rsqrt(jnp.mean(rows * rows, axis=-1, keepdims=True) + 1e-05)
    out_ref[0] = (rows * scale * gain_ref[...]).astype(jnp.bfloat16)


def normed_rows(starts, states, parts, gain):
    count, tokens, width = states.shape
    return pl.pallas_call(
        norm_kernel,
        out_shape=jax.ShapeDtypeStruct(states.shape, jnp.bfloat16),
        grid_spec=pltpu.PrefetchScalarGridSpec(
            num_scalar_prefetch=1,
            grid=(count,),
            in_specs=[
                pl.BlockSpec((1, tokens, width), lambda b, s: (b, 0, 0)),
                pl.BlockSpec(parts.shape, lambda b, s: (0, 0)),
                pl.BlockSpec((1, width), lambda b, s: (0, 0)),
            ],
            out_specs=pl.BlockSpec((1, tokens, width), lambda b, s: (b, 0, 0)),
        ),
        compiler_params=pltpu.CompilerParams(vmem_limit_bytes=48 << 20),
        cost_estimate=pl.CostEstimate(
            flops=count * tokens * width * 200, bytes_accessed=count * tokens * width * 4,
            transcendentals=0,
        ),
        name="normed_rows",
    )(starts, states, parts, gain.reshape(1, width)).reshape(count * tokens, width)


def per_device_general(states, norm_gain, gate_up, cotangent, prompt, step_sizes, insert_at, lengths):
    chips, cores = lax.axis_size("dp"), lax.axis_size("replica")
    chip, core = lax.axis_index("dp"), lax.axis_index("replica")
    half, _, shard_units = gate_up.shape
    units = shard_units // chips
    count = prompt.shape[0]
    tokens = states.shape[1]
    width = half * cores

    unit_slice = lax.dynamic_slice_in_dim(gate_up, chip * units, units, 2)
    weight_pair = lax.all_gather(
        unit_slice.reshape(half, 2 * units), "replica", axis=0, tiled=True
    )

    seq_states, seq_cotan, prompt_start = states[0], cotangent[0], insert_at[0]
    package = jnp.concatenate(
        [
            lax.dynamic_slice_in_dim(seq_states, prompt_start, count, 0),
            lax.dynamic_slice_in_dim(seq_cotan, prompt_start, count, 0),
            jnp.broadcast_to(insert_at.astype(jnp.bfloat16).reshape(1, 1), (count, 128)),
        ],
        axis=1,
    )
    package = lax.all_gather(package, "dp", axis=0, tiled=False)
    prompt_base = package[:, :, :width].astype(jnp.float32)
    prompt_cotan = (
        lax.dynamic_slice_in_dim(package, width + chip * units, units, 2)
        .reshape(chips * count, units)
        .astype(jnp.float32)
    )

    swap = [(i, (i + 1) % cores) for i in range(cores)]
    own_starts = package[:, 0, package.shape[2] - 1].astype(jnp.int32)
    seq_states, seq_cotan, _ = lax.optimization_barrier((seq_states, seq_cotan, weight_pair))
    own_states = lax.all_gather(seq_states, "dp", axis=0, tiled=False)
    other_starts = lax.ppermute(own_starts, "replica", swap)
    positions = lax.broadcasted_iota(jnp.int32, (tokens, 1), 0)
    live_cotan = jnp.where(positions < lengths[0], seq_cotan, jnp.zeros_like(seq_cotan))

    def shifted_perm(k):
        return [(i, (i + k) % chips) for i in range(chips)]

    cotan_blocks = []
    for k in range(chips):
        block = lax.dynamic_slice_in_dim(live_cotan, lax.rem(chip + k, chips) * units, units, 1)
        cotan_blocks.append(lax.ppermute(block, "dp", shifted_perm(k)) if k else block)
    stacked = jnp.stack(cotan_blocks)
    token_cotan = jnp.concatenate(
        [
            lax.dynamic_index_in_dim(stacked, lax.rem(chip - j + chips, chips), 0, keepdims=False)
            for j in range(chips)
        ],
        axis=0,
    )

    adversary = prompt.astype(jnp.float32)
    for attack_step in range(step_sizes.shape[0]):
        shifted = prompt_base + adversary[None]
        inverse_rms = row_scale(shifted)
        normalized = (shifted * inverse_rms * norm_gain).astype(jnp.bfloat16)
        unit_grads = hidden_grads(normalized.reshape(chips * count, width), weight_pair, prompt_cotan)
        feature_grad = lax.dot_general(
            unit_grads, weight_pair, (((1,), (1,)), ((), ())), preferred_element_type=jnp.float32
        ).reshape(chips, count, width)
        scaled = norm_gain * feature_grad
        feature_mean = jnp.mean(shifted * scaled, axis=-1, keepdims=True)
        partial = jnp.sum(
            inverse_rms * scaled - shifted * (inverse_rms * inverse_rms * inverse_rms) * feature_mean,
            axis=0,
        )
        adversary = apply_step(partial, adversary, step_sizes[attack_step : attack_step + 1])
        if attack_step == step_sizes.shape[0] - 2:
            own_states, adversary = lax.optimization_barrier((own_states, adversary))
            other_states = lax.ppermute(own_states, "replica", swap)

    high = lax.reduce_precision(adversary, 8, 7)
    middle = lax.reduce_precision(adversary - high, 8, 7)
    low = adversary - high - middle
    parts = jnp.concatenate([high, middle, low], axis=0).astype(jnp.bfloat16)
    own_normed = normed_rows(own_starts, own_states, parts, norm_gain)
    own_grads = hidden_grads(own_normed, weight_pair, token_cotan.astype(jnp.float32))
    other_grads = lax.ppermute(own_grads, "replica", swap)
    other_normed = normed_rows(other_starts, other_states, parts, norm_gain)

    block_width = width // (chips * cores)
    dims = (((0,), (0,)), ((), ()))
    squares = 0.0
    received = [None] * chips
    for k in [2 % chips, *[i for i in range(1, chips) if i != 2 % chips], 0] if chips > 2 else range(chips):
        start = (lax.rem(chip + k, chips) * cores + core) * block_width
        block = lax.dot_general(
            lax.dynamic_slice_in_dim(own_normed, start, block_width, 1), own_grads, dims,
            preferred_element_type=jnp.float32,
        ) + lax.dot_general(
            lax.dynamic_slice_in_dim(other_normed, start, block_width, 1), other_grads, dims,
            preferred_element_type=jnp.float32,
        )
        squares = squares + jnp.sum(block * block)
        sent = block.astype(jnp.bfloat16)
        received[k] = lax.ppermute(sent, "dp", shifted_perm(k)) if k else sent
    squares = sum_everywhere(squares)
    scale = lax.rsqrt(squares / (2 * D * FF) + 1e-06)
    stacked = jnp.stack(received)
    pieces = [
        lax.dynamic_index_in_dim(stacked, lax.rem(chip - j + chips, chips), 0, keepdims=False)
        for j in range(chips)
    ]
    weight_step = jnp.concatenate(
        [piece.reshape(block_width, 2, units) for piece in pieces], axis=2
    )
    weight_step = (weight_step.astype(jnp.float32) * scale).astype(jnp.bfloat16)
    column_count = width // lax.axis_size("tensor")
    prompt_final = lax.dynamic_slice_in_dim(
        adversary, lax.axis_index("tensor") * column_count, column_count, 1
    )
    return (prompt_final, weight_step)


def relative_devices(chip, core):
    pairs = []
    for m in range(4):
        other_chip = [chip, chip + 1 - 2 * lax.rem(chip, 2), lax.rem(chip + 2, 4), 3 - chip][m]
        for q in range(2):
            pairs.append((other_chip, core if q == 0 else 1 - core))
    return pairs


def main_kernel(
    tensors, steps,
    pair, normed, cot_ref, prompt_in, base_rows, base_cot, gain_ref, step_ref,
    adv_out, xp_out, g_all, x_all, gp_all,
    rows_v, w_buf, keep_v, send_v, got_v, g_v,
    base_buf, cot_buf, near_v, far_v, x_v, fg_v, inv_v, adv, part,
    send_a, send_b, recv_s, recv_a, recv_b, recv_c, gp_v,
    s_local, s_w, s_r, r_r, s_f, r_f, s_g, r_g, s_p, r_p, s_c, r_c, s_x, r_x,
    s_0, r_0, s_1, r_1, s_2, r_2, s_3, r_3, s_o, r_o,
):
    t = lax.axis_index("tensor")
    chip = lax.axis_index("dp")
    core = lax.axis_index("replica")
    me = chip * 2 + core
    lead = core == 0
    rel = relative_devices(chip, core)
    ids = [{"dp": a, "replica": b} for a, b in rel]
    place = [a * 2 + b for a, b in rel]
    wide = near_v.shape[2]
    half = pair.shape[1]
    units = pair.shape[2] // 4
    count, width = base_rows.shape
    block = width // 8
    base = normed.shape[0]

    def remote(src, dst, send, recv, device):
        return pltpu.make_async_remote_copy(
            src_ref=src, dst_ref=dst, send_sem=send, recv_sem=recv,
            device_id=device, device_id_type=MESH,
        )

    def w_copy(i):
        return pltpu.make_async_copy(pair.at[:, :, pl.ds(i * units, units)], w_buf.at[i % 2], s_w.at[i % 2])

    w_copies = [w_copy(0), w_copy(1)]
    for copy in w_copies:
        copy.start()
    near_half = pl.ds(pl.multiple_of(core * half, 128), half)
    far_half = pl.ds(pl.multiple_of((1 - core) * half, 128), half)
    rows_local = pltpu.make_async_copy(normed.at[:, near_half], rows_v.at[pl.ds(0, base)], s_local.at[0])
    rows_local.start()

    barrier = pltpu.get_barrier_semaphore()
    line_ids = [{"tensor": lax.rem(t + k, tensors)} for k in range(1, tensors)]
    for device in ids[1:] + line_ids:
        pl.semaphore_signal(barrier, inc=1, device_id=device, device_id_type=MESH)
    pl.semaphore_wait(barrier, 7 + tensors - 1)

    rows_far = remote(normed.at[:, far_half], rows_v.at[pl.ds(base, base)], s_r.at[0], r_r.at[0], ids[1])
    rows_far.start()
    rows_a = [remote(base_rows, base_buf.at[me], s_p.at[m], r_p.at[m], ids[2 * m]) for m in range(1, 4)]

    def first_unit(a, b):
        return pl.multiple_of(a * units + b * (units - wide), 128)

    cots = [None] + [
        remote(
            base_cot.at[:, pl.ds(first_unit(*rel[j]), wide)], cot_buf.at[me], s_c.at[j], r_c.at[j], ids[j]
        )
        for j in range(1, 8)
    ]
    w_far = remote(pair.at[:, :, pl.ds(first_unit(chip, 1 - core), wide)], far_v, s_r.at[1], r_r.at[1], ids[1])
    local = [
        pltpu.make_async_copy(base_rows, base_buf.at[me], s_local.at[1]),
        pltpu.make_async_copy(base_cot.at[:, pl.ds(first_unit(chip, core), wide)], cot_buf.at[me], s_local.at[2]),
        pltpu.make_async_copy(pair.at[:, :, pl.ds(first_unit(chip, core), wide)], near_v, s_local.at[3]),
    ]
    rows_b = [
        remote(base_buf.at[place[2 * m]], base_buf.at[place[2 * m]], s_p.at[4 + m], r_p.at[4 + m], ids[1])
        for m in range(4)
    ]
    xs = [None] + [
        remote(
            normed.at[:, pl.ds(pl.multiple_of(place[j] * block, 128), block)], x_all.at[j],
            s_x.at[j], r_x.at[j], ids[j],
        )
        for j in range(1, 8)
    ]
    mine_block = pl.ds(pl.multiple_of(me * block, 128), block)
    xl = pltpu.make_async_copy(normed.at[:, mine_block], x_all.at[0], s_local.at[9])
    for copy in rows_a + cots[1:] + local + xs[1:] + [xl]:
        copy.start()

    def bulk(src, slot, i, k, device):
        return remote(src, g_all.at[slot, i], s_g.at[k], r_g.at[k], device)

    gx = [[bulk(g_v.at[i] if q == 0 else g_all.at[1, i], 2 + q, i, 4 * q + i, ids[2]) for i in range(4)] for q in range(2)]
    gy = [[bulk(g_v.at[i] if q == 0 else g_all.at[1, i], 4 + q, i, 8 + 4 * q + i, ids[4]) for i in range(4)] for q in range(2)]
    gs = [bulk(g_v.at[i], 1, i, 16 + i, ids[1]) for i in range(4)]
    gl = [pltpu.make_async_copy(g_v.at[i], g_all.at[0, i], s_local.at[5 + i]) for i in range(4)]
    fd = [
        [bulk(g_all.at[(2 if i < 2 else 4) + q, i], 6 + q, i, 20 + 4 * q + i, ids[4 if i < 2 else 2]) for i in range(4)]
        for q in range(2)
    ]
    side = [[bulk(g_all.at[n, i], n + 1 - 2 * (n % 2), i, 28 + 4 * (n - 2) + i, ids[1]) for i in range(4)] for n in range(2, 8)]
    swaps = [remote(send_v.at[i % 2], got_v.at[i], s_f.at[i], r_f.at[i], ids[1]) for i in range(4)]

    def combine(i):
        swaps[i].wait_recv()
        gate = keep_v[i % 2, 0] + got_v[i, 0]
        up = keep_v[i % 2, 1] + got_v[i, 1]
        act, slope = silu_parts(gate)
        cot = cot_ref[:, i * units : (i + 1) * units].astype(jnp.float32)
        g_v[i, :, :units] = (cot * up * slope).astype(jnp.bfloat16)
        g_v[i, :, units:] = (cot * act).astype(jnp.bfloat16)
        gs[i].start()
        gl[i].start()

        @pl.when(lead)
        def _():
            gx[0][i].start()
            gy[0][i].start()
            for n in [i - 1] * (i > 0) + [i] * (i == 3):
                gs[n].wait_recv()
                gx[1][n].start()
                gy[1][n].start()

    rows_local.wait()
    rows_far.wait_recv()
    for i in range(4):
        w_copies[i].wait()
        if i >= 2:
            swaps[i - 2].wait_send()
        for p in range(2):
            product = jnp.dot(rows_v[...], w_buf[i % 2, p], preferred_element_type=jnp.float32)
            keep_v[i % 2, p] = product[:base]
            send_v[i % 2, p] = product[base:]
        swaps[i].start()
        if i < 2:
            w_copies.append(w_copy(i + 2))
            w_copies[-1].start()
        if i == 0:
            local[0].wait()
            rows_b[0].start()
            w_far.start()
        else:
            combine(i - 1)
        if i == 2:
            for m in range(1, 4):
                rows_a[m - 1].wait_recv()
                rows_b[m].start()
    adv[...] = prompt_in[...].astype(jnp.float32)
    combine(3)
    for copy in rows_b + cots[1:] + [w_far]:
        copy.wait_recv()
    for copy in local[1:]:
        copy.wait()
    lane = lax.broadcasted_iota(jnp.int32, (count, wide), 1)
    keep = lane >= core * (2 * wide - units)

    def norm_rows():
        def one(b, _):
            shifted = base_buf[b].astype(jnp.float32) + adv[...]
            inverse = lax.rsqrt(jnp.mean(shifted * shifted, axis=-1, keepdims=True) + 1e-05)
            x_v[pl.ds(pl.multiple_of(b * count, count), count)] = (shifted * inverse * gain_ref[...]).astype(jnp.bfloat16)
            inv_v[b] = jnp.broadcast_to(inverse, (count, 128))
            return 0
        lax.fori_loop(0, 8, one, 0)

    def unit_grads():
        near = x_v[:, near_half]
        far = x_v[:, far_half]
        gate, up = [
            jnp.dot(near, near_v[p], preferred_element_type=jnp.float32)
            + jnp.dot(far, far_v[p], preferred_element_type=jnp.float32)
            for p in range(2)
        ]
        act, slope = silu_parts(gate)
        cot = jnp.concatenate(
            [jnp.where(keep, cot_buf[b].astype(jnp.float32), 0.0) for b in range(8)], axis=0
        )
        gp_v[:, pl.ds(0, wide)] = (cot * up * slope).astype(jnp.bfloat16)
        gp_v[:, pl.ds(wide, wide)] = (cot * act).astype(jnp.bfloat16)

    dims = (((1,), (1,)), ((), ()))
    chunk = 512

    def feature_grads():
        for source, start in ((near_v, core * half), (far_v, (1 - core) * half)):
            def one(i, _):
                rows = pl.ds(pl.multiple_of(i * chunk, chunk), chunk)
                fg_v[:, pl.ds(pl.multiple_of(start + i * chunk, chunk), chunk)] = lax.dot_general(
                    gp_v[:, pl.ds(0, wide)], source[0, rows], dims, preferred_element_type=jnp.float32
                ) + lax.dot_general(
                    gp_v[:, pl.ds(wide, wide)], source[1, rows], dims, preferred_element_type=jnp.float32
                )
                return 0
            lax.fori_loop(0, half // chunk, one, 0)

    def row_grads():
        part[...] = jnp.zeros_like(part)
        def one(b, _):
            shifted = base_buf[b].astype(jnp.float32) + adv[...]
            scaled = gain_ref[...] * fg_v[pl.ds(pl.multiple_of(b * count, count), count)]
            inverse = inv_v[b][:, :1]
            middle = jnp.mean(shifted * scaled, axis=-1, keepdims=True)
            part[...] += inverse * scaled - shifted * (inverse * inverse * inverse * middle)
            return 0
        lax.fori_loop(0, 8, one, 0)

    lead_waits, other_waits = [], []

    def exchange(k):
        for a in range(4):
            send_a[k, a] = part[:, 2 * a * block : 2 * (a + 1) * block].astype(jnp.bfloat16)
        sib = remote(send_a.at[k], recv_s.at[k], s_0.at[k], r_0.at[k], ids[1])
        first = [
            remote(send_b.at[k, rel[2 * m][0]], recv_a.at[k, m], s_1.at[k, m], r_1.at[k, m], ids[2 * m])
            for m in range(1, 4)
        ]
        second = [
            remote(recv_b.at[k, t], recv_b.at[k, t], s_2.at[k, j], r_2.at[k, j], line_ids[j])
            for j in range(tensors - 1)
        ]
        third = [
            remote(recv_c.at[k, chip], recv_c.at[k, chip], s_3.at[k, m], r_3.at[k, m], ids[2 * m])
            for m in range(1, 4)
        ]
        fourth = [
            remote(
                recv_c.at[k, rel[2 * m][0]], recv_c.at[k, rel[2 * m][0]],
                s_3.at[k, 4 + m], r_3.at[k, 4 + m], ids[1],
            )
            for m in range(4)
        ]

        @pl.when(lead)
        def _():
            sib.start()
            for copy in fourth:
                copy.wait_recv()

        @pl.when(core == 1)
        def _():
            sib.wait_recv()
            for a in range(4):
                send_b[k, a] = (
                    send_a[k, a].astype(jnp.float32) + recv_s[k, a].astype(jnp.float32)
                ).astype(jnp.bfloat16)
            for copy in first:
                copy.start()
            total = send_b[k, chip].astype(jnp.float32)
            for m in range(1, 4):
                first[m - 1].wait_recv()
                total = total + recv_a[k, m].astype(jnp.float32)
            recv_b[k, t] = total.astype(jnp.bfloat16)
            for copy in second:
                copy.start()
            for copy in second:
                copy.wait_recv()
            total = recv_b[k, 0].astype(jnp.float32)
            for j in range(1, tensors):
                total = total + recv_b[k, j].astype(jnp.float32)
            recv_c[k, chip] = total.astype(jnp.bfloat16)
            for copy in third + fourth[:1]:
                copy.start()
            for m in range(1, 4):
                third[m - 1].wait_recv()
                fourth[m].start()

        lead_waits.append(sib)
        other_waits.extend(first + second + third + fourth)
        square = jnp.zeros((count, 1), jnp.float32)
        for p in range(4):
            piece = recv_c[k, p].astype(jnp.float32)
            square = square + jnp.sum(piece * piece, axis=-1, keepdims=True)
        scale = step_ref[k] * lax.rsqrt(square / width + 1e-06)
        for p in range(4):
            at = slice(2 * p * block, 2 * (p + 1) * block)
            adv[:, at] = adv[:, at] + scale * recv_c[k, p].astype(jnp.float32)

    def pass_on(source, n, i):
        source.wait_recv()
        if n < 6 and (n < 4) == (i < 2):
            fd[n % 2][i].start()
        side[n - 2][i].start()

    def forward_some(pieces):
        @pl.when(lead)
        def _():
            for n, i in pieces:
                pass_on((gx, gy)[n // 2 - 1][n % 2][i], n, i)

    stages = [[], [(2, 0), (2, 1), (3, 0), (3, 1)], [(4, 2), (5, 2), (4, 3)], [(5, 3)]]
    rest = [(2, 2), (2, 3), (3, 2), (3, 3), (4, 0), (4, 1), (5, 0), (5, 1)]
    for k in range(steps):
        norm_rows()
        unit_grads()
        feature_grads()
        row_grads()
        exchange(k)
        if k + 1 < len(stages):
            forward_some(stages[k + 1])
    for k in range(steps, 3):
        forward_some(stages[k + 1])
    adv_out[...] = adv[...]
    norm_rows()
    unit_grads()
    xp_out[...] = x_v[:, mine_block]
    mid = 4 * count
    parts = [pl.ds(0, mid), pl.ds(mid, mid)]

    def hop(src, slot, h, k, device):
        source = gp_all.at[slot] if src is None else src
        return remote(source.at[parts[h]], gp_all.at[slot, parts[h]], s_o.at[k], r_o.at[k], device)

    os = remote(gp_v, gp_all.at[me], s_o.at[4], r_o.at[4], ids[1])
    ol = pltpu.make_async_copy(gp_v, gp_all.at[me], s_local.at[4])
    os.start()
    ol.start()
    ox = [[hop(gp_v if q == 0 else None, place[q], h, (0, 5)[q] + h, ids[2]) for h in range(2)] for q in range(2)]
    oy = [[hop(gp_v if q == 0 else None, place[q], h, (2, 7)[q] + h, ids[4]) for h in range(2)] for q in range(2)]
    od = [[hop(None, place[2 + q], 0, 9 + q, ids[4]) for q in range(2)], [hop(None, place[4 + q], 1, 11 + q, ids[2]) for q in range(2)]]
    back = [[hop(None, place[n], h, 13 + 2 * (n - 2) + h, ids[1]) for h in range(2)] for n in range(2, 8)]
    backs = [copy for two in back for copy in two]

    @pl.when(core == 1)
    def _():
        for copy in (ox[0][0], oy[0][1], ox[0][1], oy[0][0]):
            copy.start()
        os.wait_recv()
        for copy in (ox[1][0], oy[1][1], ox[1][1], oy[1][0]):
            copy.start()
        for q in range(2):
            ox[q][0].wait_recv()
            od[0][q].start()
            back[q][0].start()
            oy[q][1].wait_recv()
            od[1][q].start()
            back[2 + q][1].start()
        for q in range(2):
            ox[q][1].wait_recv()
            back[q][1].start()
            oy[q][0].wait_recv()
            back[2 + q][0].start()
        for q in range(2):
            for h in range(2):
                od[h][q].wait_recv()
                back[4 + q][h].start()
        for copy in gs:
            copy.wait_recv()
        for four in side:
            for copy in four:
                copy.wait_recv()
        for copy in other_waits + ox[0] + ox[1] + oy[0] + oy[1] + od[0] + od[1] + backs:
            copy.wait_send()

    @pl.when(lead)
    def _():
        for n, i in rest:
            pass_on((gx, gy)[n // 2 - 1][n % 2][i], n, i)
        for i in range(4):
            for q in range(2):
                pass_on(fd[q][i], 6 + q, i)
        os.wait_recv()
        for copy in backs:
            copy.wait_recv()
        for copy in lead_waits + gx[0] + gx[1] + gy[0] + gy[1] + fd[0] + fd[1]:
            copy.wait_send()
        for four in side:
            for copy in four:
                copy.wait_send()

    for copy in xs[1:]:
        copy.wait_recv()
    for copy in gl + [ol, xl]:
        copy.wait()
    for copy in [rows_far, w_far, os] + rows_a + rows_b + cots[1:] + xs[1:] + swaps[2:] + gs:
        copy.wait_send()


def main_call(pair, normed, cot, prompt, base_rows, base_cot, gain, step_sizes):
    tensors = lax.axis_size("tensor")
    steps = step_sizes.shape[0]
    count, width = base_rows.shape
    half, shard = pair.shape[1:]
    units, wide = shard // 4, 512
    block = width // 8
    base = normed.shape[0]
    bf, f32 = jnp.bfloat16, jnp.float32
    dma = pltpu.SemaphoreType.DMA
    vmem = pl.BlockSpec(memory_space=pltpu.VMEM)
    hbm = pl.BlockSpec(memory_space=pl.ANY)
    return pl.pallas_call(
        functools.partial(main_kernel, tensors, steps),
        out_shape=[
            jax.ShapeDtypeStruct((count, width), f32),
            jax.ShapeDtypeStruct((8 * count, block), bf),
            jax.ShapeDtypeStruct((8, 4, base, 2 * units), bf),
            jax.ShapeDtypeStruct((8, base, block), bf),
            jax.ShapeDtypeStruct((8, 8 * count, 2 * wide), bf),
        ],
        in_specs=[hbm, hbm, vmem, vmem, hbm, hbm, vmem, pl.BlockSpec(memory_space=pltpu.SMEM)],
        out_specs=[vmem, vmem, hbm, hbm, hbm],
        scratch_shapes=[
            pltpu.VMEM((2 * base, half), bf),
            pltpu.VMEM((2, 2, half, units), bf),
            pltpu.VMEM((2, 2, base, units), f32),
            pltpu.VMEM((2, 2, base, units), f32),
            pltpu.VMEM((4, 2, base, units), f32),
            pltpu.VMEM((4, base, 2 * units), bf),
            pltpu.VMEM((8, count, width), bf),
            pltpu.VMEM((8, count, wide), bf),
            pltpu.VMEM((2, half, wide), bf),
            pltpu.VMEM((2, half, wide), bf),
            pltpu.VMEM((8 * count, width), bf),
            pltpu.VMEM((8 * count, width), f32),
            pltpu.VMEM((8, count, 128), f32),
            pltpu.VMEM((count, width), f32),
            pltpu.VMEM((count, width), f32),
            pltpu.VMEM((steps, 4, count, 2 * block), bf),
            pltpu.VMEM((steps, 4, count, 2 * block), bf),
            pltpu.VMEM((steps, 4, count, 2 * block), bf),
            pltpu.VMEM((steps, 4, count, 2 * block), bf),
            pltpu.VMEM((steps, tensors, count, 2 * block), bf),
            pltpu.VMEM((steps, 4, count, 2 * block), bf),
            pltpu.VMEM((8 * count, 2 * wide), bf),
        ]
        + [dma((10,))] + [dma((2,))] * 3 + [dma((4,))] * 2 + [dma((52,))] * 2 + [dma((8,))] * 6
        + [dma((steps,))] * 2 + [dma((steps, 4))] * 2 + [dma((steps, tensors))] * 2
        + [dma((steps, 8))] * 2 + [dma((25,))] * 2,
        compiler_params=pltpu.CompilerParams(
            collective_id=2, has_side_effects=True, vmem_limit_bytes=62 << 20
        ),
        cost_estimate=pl.CostEstimate(flops=100_000_000_000, bytes_accessed=100_000_000, transcendentals=0),
        name="attack_and_gather",
    )(pair, normed, cot, prompt, base_rows, base_cot, gain.reshape(1, width), step_sizes)


def grad_kernel(x_ref, xp_ref, g_ref, gp0_ref, gp1_ref, out_ref, sq_ref, xt_v, xpt_v):
    step = pl.program_id(0) * pl.num_programs(1) + pl.program_id(1)

    @pl.when(step == 0)
    def _():
        xt_v[...] = x_ref[...].T
        xpt_v[...] = xp_ref[...].T
        sq_ref[...] = jnp.zeros_like(sq_ref)

    extra = 2 * gp0_ref.shape[2] - out_ref.shape[2]
    rows = g_ref.shape[0] * g_ref.shape[2]
    gp = jnp.concatenate([gp0_ref[0], gp1_ref[0][:, extra:]], axis=1)
    block = jnp.dot(
        xt_v[...], g_ref[...].reshape(rows, g_ref.shape[3]), preferred_element_type=jnp.float32
    ) + jnp.dot(xpt_v[...], gp, preferred_element_type=jnp.float32)
    out_ref[0] = block
    sq_ref[...] += jnp.sum((block * block).reshape(-1, 8, block.shape[1]), axis=0)


def grad_call(x_all, xp, g_all, gp_all):
    eight, _, own_base, pair_units = g_all.shape
    cols = 4 * pair_units
    block = x_all.shape[2]
    wide = gp_all.shape[2] // 2
    shard = cols // 2
    units = shard // 4
    prompts = xp.shape[0]
    f32 = jnp.float32
    return pl.pallas_call(
        grad_kernel,
        out_shape=[
            jax.ShapeDtypeStruct((2, block, shard), f32),
            jax.ShapeDtypeStruct((8, units), f32),
        ],
        grid=(2, 4),
        in_specs=[
            pl.BlockSpec((eight * own_base, block), lambda p, j: (0, 0)),
            pl.BlockSpec((prompts, block), lambda p, j: (0, 0)),
            pl.BlockSpec((eight, 1, own_base, units), lambda p, j: (0, j, 0, p)),
            pl.BlockSpec((1, prompts, wide), lambda p, j: (2 * j, 0, p)),
            pl.BlockSpec((1, prompts, wide), lambda p, j: (2 * j + 1, 0, p)),
        ],
        out_specs=[
            pl.BlockSpec((1, block, units), lambda p, j: (p, 0, j)),
            pl.BlockSpec((8, units), lambda p, j: (0, 0)),
        ],
        scratch_shapes=[
            pltpu.VMEM((block, eight * own_base), jnp.bfloat16),
            pltpu.VMEM((block, prompts), jnp.bfloat16),
        ],
        compiler_params=pltpu.CompilerParams(vmem_limit_bytes=48 << 20),
        cost_estimate=pl.CostEstimate(
            flops=2 * block * cols * (eight * own_base + prompts), bytes_accessed=50_000_000, transcendentals=0
        ),
        name="weight_grad",
    )(x_all.reshape(eight * own_base, block), xp, g_all, gp_all, gp_all)


def result_kernel(scale_ref, grad_ref, out_ref):
    _, rows, cols = grad_ref.shape
    n = 128
    to = lax.broadcasted_iota(jnp.int32, (2 * n, 2 * n), 0)
    source = jnp.where(lax.rem(to, 2) == 0, to // 2, n + to // 2)
    order = jnp.where(lax.broadcasted_iota(jnp.int32, (2 * n, 2 * n), 1) == source, 1.0, 0.0).astype(jnp.bfloat16)
    for r in range(0, rows, n):
        both = jnp.concatenate(
            [(grad_ref[p, r : r + n] * scale_ref[0]).astype(jnp.bfloat16) for p in range(2)], axis=0
        )
        mixed = jnp.dot(order, both, preferred_element_type=jnp.float32).astype(jnp.bfloat16)
        out_ref[r : r + n] = mixed.reshape(n, 2, cols)


def result_call(scale, weight_grad):
    _, rows, shard = weight_grad.shape
    cols = 512
    return pl.pallas_call(
        result_kernel,
        out_shape=jax.ShapeDtypeStruct((rows, 2, shard), jnp.bfloat16),
        grid=(shard // cols,),
        in_specs=[
            pl.BlockSpec(memory_space=pltpu.SMEM),
            pl.BlockSpec((2, rows, cols), lambda j: (0, 0, j)),
        ],
        out_specs=pl.BlockSpec((rows, 2, cols), lambda j: (0, 0, j)),
        compiler_params=pltpu.CompilerParams(vmem_limit_bytes=48 << 20),
        name="scaled_result",
    )(scale.reshape(1), weight_grad)


def per_device(states, norm_gain, gate_up, cotangent, prompt, step_sizes, insert_at, lengths):
    chips, cores = lax.axis_size("dp"), lax.axis_size("replica")
    shard = gate_up.shape[2]
    count = prompt.shape[0]
    fits = (
        chips == 4 and cores == 2 and states.shape[0] == 1 and shard % (chips * 128) == 0
        and shard // chips > 512 and shard // chips <= 1024 and shard % 512 == 0
        and gate_up.shape[0] % 1024 == 0 and count % 16 == 0 and (states.shape[1] - count) % 16 == 0
    )
    if not fits:
        return per_device_general(
            states, norm_gain, gate_up, cotangent, prompt, step_sizes, insert_at, lengths
        )
    chip, core = lax.axis_index("dp"), lax.axis_index("replica")
    half = gate_up.shape[0]
    width = half * cores
    tokens = states.shape[1]
    base = tokens - count
    units = shard // chips
    start = insert_at[0]

    pair = jnp.transpose(gate_up, (1, 0, 2))

    spot = lax.broadcasted_iota(jnp.int32, (base, 1), 0)
    ahead = spot < start
    position = jnp.where(ahead, spot, spot + count)
    rows = jnp.where(ahead, states[0, :base], states[0, count:]).astype(jnp.float32)
    cot = jnp.where(ahead, cotangent[0, :base], cotangent[0, count:])
    cot = jnp.where(position < lengths[0], cot, jnp.zeros_like(cot))
    normed = (rows * row_scale(rows) * norm_gain).astype(jnp.bfloat16)
    base_rows = lax.dynamic_slice_in_dim(states[0], start, count, 0)
    base_cot = lax.dynamic_slice_in_dim(cotangent[0], start, count, 0)

    adversary, xp, g_all, x_all, gp_all = main_call(
        pair, normed, cot, prompt, base_rows, base_cot, norm_gain, step_sizes
    )
    weight_grad, squares = grad_call(x_all, xp, g_all, gp_all)
    squares = sum_everywhere(jnp.sum(squares))
    scale = lax.rsqrt(squares / (2 * D * FF) + 1e-06)
    weight_step = result_call(scale, weight_grad)
    column_count = width // lax.axis_size("tensor")
    prompt_final = lax.dynamic_slice_in_dim(
        adversary, lax.axis_index("tensor") * column_count, column_count, 1
    )
    return (prompt_final, weight_step)


def solution(mesh):
    return jax.shard_map(
        per_device,
        mesh=mesh,
        in_specs=(
            P(("dp", "replica"), None, None),
            P(),
            P("replica", None, "tensor"),
            P(("dp", "replica"), None, "tensor"),
            P(),
            P(),
            P(("dp", "replica")),
            P(("dp", "replica")),
        ),
        out_specs=(P(None, "tensor"), P(("dp", "replica"), None, "tensor")),
        check_vma=False,
    )
```

```python
import functools

import jax
import jax.numpy as jnp
from jax import lax
from jax.experimental import pallas as pl
from jax.experimental.pallas import tpu as pltpu
from jax.sharding import PartitionSpec as P

D = 4096
FF = 14336
MESH = pl.DeviceIdType.MESH


def row_scale(feature_rows):
    return lax.rsqrt(jnp.mean(feature_rows * feature_rows, axis=-1, keepdims=True) + 1e-05)


def silu_parts(gate_values):
    sigmoid_value = jax.nn.sigmoid(gate_values)
    return (
        gate_values * sigmoid_value,
        sigmoid_value * (1.0 + gate_values * (1.0 - sigmoid_value)),
    )


def hidden_grads(normalized, weight_pair, cotan_rows):
    unit_count = weight_pair.shape[1] // 2
    projected = jnp.dot(normalized, weight_pair, preferred_element_type=jnp.float32)
    activated, derivative = silu_parts(projected[:, :unit_count])
    up_part = projected[:, unit_count:]
    return jnp.concatenate(
        [cotan_rows * up_part * derivative, cotan_rows * activated], axis=1
    ).astype(jnp.bfloat16)


def step_kernel(
    tensors, chips, cores, partial_ref, adversary_ref, step_ref, out_ref,
    plane_buf, line_buf, mine, send1, recv1, send2, recv2, send3, recv3, send4, recv4,
):
    group = chips * cores
    t = lax.axis_index("tensor")
    g = lax.axis_index("dp") * cores + lax.axis_index("replica")
    rows = partial_ref.shape[0] // group
    own = rows // tensors
    plane = [lax.rem(g + k, group) for k in range(1, group)]
    line = [lax.rem(t + k, tensors) for k in range(1, tensors)]
    plane_ids = [{"dp": p // cores, "replica": lax.rem(p, cores)} for p in plane]
    line_ids = [{"tensor": p} for p in line]

    barrier = pltpu.get_barrier_semaphore()
    for device in plane_ids + line_ids:
        pl.semaphore_signal(barrier, inc=1, device_id=device, device_id_type=MESH)
    pl.semaphore_wait(barrier, group + tensors - 2)

    def exchange(pairs, ids, sends, recvs):
        copies = []
        for k, ((source, target), device) in enumerate(zip(pairs, ids)):
            copy = pltpu.make_async_remote_copy(
                src_ref=source, dst_ref=target, send_sem=sends.at[k], recv_sem=recvs.at[k],
                device_id=device, device_id_type=MESH,
            )
            copy.start()
            copies.append(copy)
        return copies

    first = exchange(
        [(partial_ref.at[pl.ds(p * rows, rows)], plane_buf.at[k]) for k, p in enumerate(plane)],
        plane_ids, send1, recv1,
    )
    total = partial_ref[pl.ds(g * rows, rows)]
    for k, copy in enumerate(first):
        copy.wait_recv()
        total = total + plane_buf[k]
    mine[...] = total
    second = exchange(
        [(mine.at[pl.ds(p * own, own)], line_buf.at[k]) for k, p in enumerate(line)],
        line_ids, send2, recv2,
    )
    grad = mine[pl.ds(t * own, own)]
    for k, copy in enumerate(second):
        copy.wait_recv()
        grad = grad + line_buf[k]
    square = jnp.sum(jnp.sum(grad * grad, axis=2, keepdims=True), axis=1, keepdims=True)
    count = partial_ref.shape[1] * partial_ref.shape[2]
    row = g * rows + t * own
    block = pl.ds(row, own)
    out_ref[block] = adversary_ref[block] + step_ref[0] * grad * lax.rsqrt(square / count + 1e-06)
    third = exchange([(out_ref.at[block], out_ref.at[block])] * len(line), line_ids, send3, recv3)
    for copy in third:
        copy.wait_recv()
    wide = pl.ds(g * rows, rows)
    fourth = exchange([(out_ref.at[wide], out_ref.at[wide])] * len(plane), plane_ids, send4, recv4)
    for copy in fourth:
        copy.wait_recv()
    for copy in first + second + third + fourth:
        copy.wait_send()


def apply_step(partial, adversary, step_size):
    tensors, chips, cores = (lax.axis_size(a) for a in ("tensor", "dp", "replica"))
    group = chips * cores
    count, width = partial.shape
    if count % (group * tensors) == 0 and width % 1024 == 0:
        shape = (count, 8, width // 8)
        rows = count // group
        own = rows // tensors
        dma = pltpu.SemaphoreType.DMA
        vmem = pl.BlockSpec(memory_space=pltpu.VMEM)
        result = pl.pallas_call(
            functools.partial(step_kernel, tensors, chips, cores),
            out_shape=jax.ShapeDtypeStruct(shape, jnp.float32),
            in_specs=[vmem, vmem, pl.BlockSpec(memory_space=pltpu.SMEM)],
            out_specs=vmem,
            scratch_shapes=[
                pltpu.VMEM((group - 1, rows) + shape[1:], jnp.float32),
                pltpu.VMEM((tensors - 1, own) + shape[1:], jnp.float32),
                pltpu.VMEM((rows,) + shape[1:], jnp.float32),
            ]
            + [dma((group - 1,))] * 2 + [dma((tensors - 1,))] * 4 + [dma((group - 1,))] * 2,
            compiler_params=pltpu.CompilerParams(
                collective_id=0, has_side_effects=True, vmem_limit_bytes=16 << 20
            ),
            cost_estimate=pl.CostEstimate(
                flops=20_000_000_000, bytes_accessed=3 * count * width * 4, transcendentals=0
            ),
            name="attack_step",
        )(partial.reshape(shape), adversary.reshape(shape), step_size)
        return result.reshape(count, width)
    grad = lax.psum(partial, ("tensor", "dp", "replica"))
    scale = lax.rsqrt(jnp.mean(grad * grad, axis=-1, keepdims=True) + 1e-06)
    return adversary + step_size[0] * grad * scale


def scalar_kernel(tensors, chips, cores, value_ref, out_ref, buf1, buf2, mine, send1, recv1, send2, recv2):
    group = chips * cores
    t = lax.axis_index("tensor")
    g = lax.axis_index("dp") * cores + lax.axis_index("replica")
    plane = [lax.rem(g + k, group) for k in range(1, group)]
    plane_ids = [{"dp": p // cores, "replica": lax.rem(p, cores)} for p in plane]
    line_ids = [{"tensor": lax.rem(t + k, tensors)} for k in range(1, tensors)]
    barrier = pltpu.get_barrier_semaphore()
    for device in plane_ids + line_ids:
        pl.semaphore_signal(barrier, inc=1, device_id=device, device_id_type=MESH)
    pl.semaphore_wait(barrier, group + tensors - 2)
    copies = []
    total = value_ref[...]
    source = value_ref
    for ids, buf, sends, recvs in ((plane_ids, buf1, send1, recv1), (line_ids, buf2, send2, recv2)):
        stage = []
        for k, device in enumerate(ids):
            copy = pltpu.make_async_remote_copy(
                src_ref=source, dst_ref=buf.at[k], send_sem=sends.at[k], recv_sem=recvs.at[k],
                device_id=device, device_id_type=MESH,
            )
            copy.start()
            stage.append(copy)
        for k, copy in enumerate(stage):
            copy.wait_recv()
            total = total + buf[k]
        copies += stage
        if buf is buf1:
            mine[...] = total
            source = mine
    out_ref[...] = total
    for copy in copies:
        copy.wait_send()


def sum_everywhere(value):
    tensors, chips, cores = (lax.axis_size(a) for a in ("tensor", "dp", "replica"))
    group = chips * cores
    if not 1 < tensors <= 8 or not 1 < group <= 16:
        return lax.psum(value, ("tensor", "dp", "replica"))
    dma = pltpu.SemaphoreType.DMA
    vmem = pl.BlockSpec(memory_space=pltpu.VMEM)
    return pl.pallas_call(
        functools.partial(scalar_kernel, tensors, chips, cores),
        out_shape=jax.ShapeDtypeStruct((8, 128), jnp.float32),
        in_specs=[vmem],
        out_specs=vmem,
        scratch_shapes=[
            pltpu.VMEM((group - 1, 8, 128), jnp.float32),
            pltpu.VMEM((tensors - 1, 8, 128), jnp.float32),
            pltpu.VMEM((8, 128), jnp.float32),
        ]
        + [dma((group - 1,))] * 2 + [dma((tensors - 1,))] * 2,
        compiler_params=pltpu.CompilerParams(
            collective_id=1, has_side_effects=True, vmem_limit_bytes=4 << 20
        ),
        name="scalar_sum",
    )(jnp.full((8, 128), value, jnp.float32))[0, 0]


def norm_kernel(start_ref, state_ref, parts_ref, gain_ref, out_ref):
    slots = parts_ref.shape[0] // 3
    tokens = state_ref.shape[1]
    shape = (tokens, 3 * slots)
    slot = lax.broadcasted_iota(jnp.int32, shape, 0) - start_ref[pl.program_id(0)]
    column = lax.rem(lax.broadcasted_iota(jnp.int32, shape, 1), slots)
    placed = jnp.dot(
        jnp.where(slot == column, 1.0, 0.0).astype(jnp.bfloat16), parts_ref[...],
        preferred_element_type=jnp.float32,
    )
    rows = state_ref[0].astype(jnp.float32) + placed
    scale = lax.rsqrt(jnp.mean(rows * rows, axis=-1, keepdims=True) + 1e-05)
    out_ref[0] = (rows * scale * gain_ref[...]).astype(jnp.bfloat16)


def normed_rows(starts, states, parts, gain):
    count, tokens, width = states.shape
    return pl.pallas_call(
        norm_kernel,
        out_shape=jax.ShapeDtypeStruct(states.shape, jnp.bfloat16),
        grid_spec=pltpu.PrefetchScalarGridSpec(
            num_scalar_prefetch=1,
            grid=(count,),
            in_specs=[
                pl.BlockSpec((1, tokens, width), lambda b, s: (b, 0, 0)),
                pl.BlockSpec(parts.shape, lambda b, s: (0, 0)),
                pl.BlockSpec((1, width), lambda b, s: (0, 0)),
            ],
            out_specs=pl.BlockSpec((1, tokens, width), lambda b, s: (b, 0, 0)),
        ),
        compiler_params=pltpu.CompilerParams(vmem_limit_bytes=48 << 20),
        cost_estimate=pl.CostEstimate(
            flops=count * tokens * width * 200, bytes_accessed=count * tokens * width * 4,
            transcendentals=0,
        ),
        name="normed_rows",
    )(starts, states, parts, gain.reshape(1, width)).reshape(count * tokens, width)


def per_device_general(states, norm_gain, gate_up, cotangent, prompt, step_sizes, insert_at, lengths):
    chips, cores = lax.axis_size("dp"), lax.axis_size("replica")
    chip, core = lax.axis_index("dp"), lax.axis_index("replica")
    half, _, shard_units = gate_up.shape
    units = shard_units // chips
    count = prompt.shape[0]
    tokens = states.shape[1]
    width = half * cores

    unit_slice = lax.dynamic_slice_in_dim(gate_up, chip * units, units, 2)
    weight_pair = lax.all_gather(
        unit_slice.reshape(half, 2 * units), "replica", axis=0, tiled=True
    )

    seq_states, seq_cotan, prompt_start = states[0], cotangent[0], insert_at[0]
    package = jnp.concatenate(
        [
            lax.dynamic_slice_in_dim(seq_states, prompt_start, count, 0),
            lax.dynamic_slice_in_dim(seq_cotan, prompt_start, count, 0),
            jnp.broadcast_to(insert_at.astype(jnp.bfloat16).reshape(1, 1), (count, 128)),
        ],
        axis=1,
    )
    package = lax.all_gather(package, "dp", axis=0, tiled=False)
    prompt_base = package[:, :, :width].astype(jnp.float32)
    prompt_cotan = (
        lax.dynamic_slice_in_dim(package, width + chip * units, units, 2)
        .reshape(chips * count, units)
        .astype(jnp.float32)
    )

    swap = [(i, (i + 1) % cores) for i in range(cores)]
    own_starts = package[:, 0, package.shape[2] - 1].astype(jnp.int32)
    seq_states, seq_cotan, _ = lax.optimization_barrier((seq_states, seq_cotan, weight_pair))
    own_states = lax.all_gather(seq_states, "dp", axis=0, tiled=False)
    other_starts = lax.ppermute(own_starts, "replica", swap)
    positions = lax.broadcasted_iota(jnp.int32, (tokens, 1), 0)
    live_cotan = jnp.where(positions < lengths[0], seq_cotan, jnp.zeros_like(seq_cotan))

    def shifted_perm(k):
        return [(i, (i + k) % chips) for i in range(chips)]

    cotan_blocks = []
    for k in range(chips):
        block = lax.dynamic_slice_in_dim(live_cotan, lax.rem(chip + k, chips) * units, units, 1)
        cotan_blocks.append(lax.ppermute(block, "dp", shifted_perm(k)) if k else block)
    stacked = jnp.stack(cotan_blocks)
    token_cotan = jnp.concatenate(
        [
            lax.dynamic_index_in_dim(stacked, lax.rem(chip - j + chips, chips), 0, keepdims=False)
            for j in range(chips)
        ],
        axis=0,
    )

    adversary = prompt.astype(jnp.float32)
    for attack_step in range(step_sizes.shape[0]):
        shifted = prompt_base + adversary[None]
        inverse_rms = row_scale(shifted)
        normalized = (shifted * inverse_rms * norm_gain).astype(jnp.bfloat16)
        unit_grads = hidden_grads(normalized.reshape(chips * count, width), weight_pair, prompt_cotan)
        feature_grad = lax.dot_general(
            unit_grads, weight_pair, (((1,), (1,)), ((), ())), preferred_element_type=jnp.float32
        ).reshape(chips, count, width)
        scaled = norm_gain * feature_grad
        feature_mean = jnp.mean(shifted * scaled, axis=-1, keepdims=True)
        partial = jnp.sum(
            inverse_rms * scaled - shifted * (inverse_rms * inverse_rms * inverse_rms) * feature_mean,
            axis=0,
        )
        adversary = apply_step(partial, adversary, step_sizes[attack_step : attack_step + 1])
        if attack_step == step_sizes.shape[0] - 2:
            own_states, adversary = lax.optimization_barrier((own_states, adversary))
            other_states = lax.ppermute(own_states, "replica", swap)

    high = lax.reduce_precision(adversary, 8, 7)
    middle = lax.reduce_precision(adversary - high, 8, 7)
    low = adversary - high - middle
    parts = jnp.concatenate([high, middle, low], axis=0).astype(jnp.bfloat16)
    own_normed = normed_rows(own_starts, own_states, parts, norm_gain)
    own_grads = hidden_grads(own_normed, weight_pair, token_cotan.astype(jnp.float32))
    other_grads = lax.ppermute(own_grads, "replica", swap)
    other_normed = normed_rows(other_starts, other_states, parts, norm_gain)

    block_width = width // (chips * cores)
    dims = (((0,), (0,)), ((), ()))
    squares = 0.0
    received = [None] * chips
    for k in [2 % chips, *[i for i in range(1, chips) if i != 2 % chips], 0] if chips > 2 else range(chips):
        start = (lax.rem(chip + k, chips) * cores + core) * block_width
        block = lax.dot_general(
            lax.dynamic_slice_in_dim(own_normed, start, block_width, 1), own_grads, dims,
            preferred_element_type=jnp.float32,
        ) + lax.dot_general(
            lax.dynamic_slice_in_dim(other_normed, start, block_width, 1), other_grads, dims,
            preferred_element_type=jnp.float32,
        )
        squares = squares + jnp.sum(block * block)
        sent = block.astype(jnp.bfloat16)
        received[k] = lax.ppermute(sent, "dp", shifted_perm(k)) if k else sent
    squares = sum_everywhere(squares)
    scale = lax.rsqrt(squares / (2 * D * FF) + 1e-06)
    stacked = jnp.stack(received)
    pieces = [
        lax.dynamic_index_in_dim(stacked, lax.rem(chip - j + chips, chips), 0, keepdims=False)
        for j in range(chips)
    ]
    weight_step = jnp.concatenate(
        [piece.reshape(block_width, 2, units) for piece in pieces], axis=2
    )
    weight_step = (weight_step.astype(jnp.float32) * scale).astype(jnp.bfloat16)
    column_count = width // lax.axis_size("tensor")
    prompt_final = lax.dynamic_slice_in_dim(
        adversary, lax.axis_index("tensor") * column_count, column_count, 1
    )
    return (prompt_final, weight_step)


def relative_devices(chip, core):
    pairs = []
    for m in range(4):
        other_chip = [chip, chip + 1 - 2 * lax.rem(chip, 2), lax.rem(chip + 2, 4), 3 - chip][m]
        for q in range(2):
            pairs.append((other_chip, core if q == 0 else 1 - core))
    return pairs


def main_kernel(
    tensors, steps,
    pair, normed, cot_ref, prompt_in, base_rows, base_cot, gain_ref, step_ref,
    adv_out, xp_out, g_all, x_all, gp_all,
    rows_v, w_buf, keep_v, send_v, got_v, g_v,
    base_buf, cot_buf, near_v, far_v, x_v, fg_v, inv_v, adv, part,
    send_a, send_b, recv_s, recv_a, recv_b, recv_c, gp_v,
    s_local, s_w, s_r, r_r, s_f, r_f, s_g, r_g, s_p, r_p, s_c, r_c, s_x, r_x, s_z, r_z,
    s_0, r_0, s_1, r_1, s_2, r_2, s_3, r_3, s_o, r_o,
):
    t = lax.axis_index("tensor")
    chip = lax.axis_index("dp")
    core = lax.axis_index("replica")
    me = chip * 2 + core
    lead = core == 0
    rel = relative_devices(chip, core)
    ids = [{"dp": a, "replica": b} for a, b in rel]
    place = [a * 2 + b for a, b in rel]
    wide = near_v.shape[2]
    half = pair.shape[1]
    units = pair.shape[2] // 4
    count, width = base_rows.shape
    block = width // 8
    base = normed.shape[0]

    def remote(src, dst, send, recv, device):
        return pltpu.make_async_remote_copy(
            src_ref=src, dst_ref=dst, send_sem=send, recv_sem=recv,
            device_id=device, device_id_type=MESH,
        )

    def w_copy(i):
        return pltpu.make_async_copy(pair.at[:, :, pl.ds(i * units, units)], w_buf.at[i % 2], s_w.at[i % 2])

    w_copies = [w_copy(0), w_copy(1)]
    for copy in w_copies:
        copy.start()
    near_half = pl.ds(pl.multiple_of(core * half, 128), half)
    far_half = pl.ds(pl.multiple_of((1 - core) * half, 128), half)
    rows_local = pltpu.make_async_copy(normed.at[:, near_half], rows_v.at[pl.ds(0, base)], s_local.at[0])
    rows_local.start()

    barrier = pltpu.get_barrier_semaphore()
    line_ids = [{"tensor": lax.rem(t + k, tensors)} for k in range(1, tensors)]
    for device in ids[1:] + line_ids:
        pl.semaphore_signal(barrier, inc=1, device_id=device, device_id_type=MESH)
    pl.semaphore_wait(barrier, 7 + tensors - 1)

    rows_far = remote(normed.at[:, far_half], rows_v.at[pl.ds(base, base)], s_r.at[0], r_r.at[0], ids[1])
    rows_far.start()
    rows_a = [remote(base_rows, base_buf.at[me], s_p.at[m], r_p.at[m], ids[2 * m]) for m in range(1, 4)]

    def first_unit(a, b):
        return pl.multiple_of(a * units + b * (units - wide), 128)

    cots = [None] + [
        remote(
            base_cot.at[:, pl.ds(first_unit(*rel[j]), wide)], cot_buf.at[me], s_c.at[j], r_c.at[j], ids[j]
        )
        for j in range(1, 8)
    ]
    w_far = remote(pair.at[:, :, pl.ds(first_unit(chip, 1 - core), wide)], far_v, s_r.at[1], r_r.at[1], ids[1])
    local = [
        pltpu.make_async_copy(base_rows, base_buf.at[me], s_local.at[1]),
        pltpu.make_async_copy(base_cot.at[:, pl.ds(first_unit(chip, core), wide)], cot_buf.at[me], s_local.at[2]),
        pltpu.make_async_copy(pair.at[:, :, pl.ds(first_unit(chip, core), wide)], near_v, s_local.at[3]),
    ]
    rows_b = [
        remote(base_buf.at[place[2 * m]], base_buf.at[place[2 * m]], s_p.at[4 + m], r_p.at[4 + m], ids[1])
        for m in range(4)
    ]
    quarter = block // tensors
    own_quarter = pl.ds(pl.multiple_of(t * quarter, 128), quarter)
    xs = [None]
    for j in range(1, 8):
        start = pl.multiple_of(place[j] * block, 128)
        if j == 1:
            src, dst = normed.at[:, pl.ds(start, block)], x_all.at[j]
        else:
            src = normed.at[:, pl.ds(pl.multiple_of(start + t * quarter, 128), quarter)]
            dst = x_all.at[j, :, own_quarter]
        xs.append(remote(src, dst, s_x.at[j], r_x.at[j], ids[j]))
    xz = [
        [
            remote(
                x_all.at[j, :, own_quarter], x_all.at[j, :, own_quarter],
                s_z.at[j, k], r_z.at[j, k], line_ids[k],
            )
            for k in range(tensors - 1)
        ]
        for j in range(2, 8)
    ]
    xzs = [copy for line in xz for copy in line]
    mine_block = pl.ds(pl.multiple_of(me * block, 128), block)
    xl = pltpu.make_async_copy(normed.at[:, mine_block], x_all.at[0], s_local.at[9])
    for copy in rows_a + cots[1:] + local + xs[1:] + [xl]:
        copy.start()

    def bulk(src, slot, i, k, device):
        return remote(src, g_all.at[slot, i], s_g.at[k], r_g.at[k], device)

    gx = [[bulk(g_v.at[i] if q == 0 else g_all.at[1, i], 2 + q, i, 4 * q + i, ids[2]) for i in range(4)] for q in range(2)]
    gy = [[bulk(g_v.at[i] if q == 0 else g_all.at[1, i], 4 + q, i, 8 + 4 * q + i, ids[4]) for i in range(4)] for q in range(2)]
    early = [bulk(g_v.at[0], 3, 0, 4, ids[3]), bulk(g_v.at[0], 5, 0, 12, ids[5])]
    gs = [bulk(g_v.at[i], 1, i, 16 + i, ids[1]) for i in range(4)]
    gl = [pltpu.make_async_copy(g_v.at[i], g_all.at[0, i], s_local.at[5 + i]) for i in range(4)]
    fd = [
        [bulk(g_all.at[(2 if i < 2 else 4) + q, i], 6 + q, i, 20 + 4 * q + i, ids[4 if i < 2 else 2]) for i in range(4)]
        for q in range(2)
    ]
    side = [[bulk(g_all.at[n, i], n + 1 - 2 * (n % 2), i, 28 + 4 * (n - 2) + i, ids[1]) for i in range(4)] for n in range(2, 8)]
    swaps = [remote(send_v.at[i % 2], got_v.at[i], s_f.at[i], r_f.at[i], ids[1]) for i in range(4)]

    def combine(i):
        swaps[i].wait_recv()
        gate = keep_v[i % 2, 0] + got_v[i, 0]
        up = keep_v[i % 2, 1] + got_v[i, 1]
        act, slope = silu_parts(gate)
        cot = cot_ref[:, i * units : (i + 1) * units].astype(jnp.float32)
        g_v[i, :, :units] = (cot * up * slope).astype(jnp.bfloat16)
        g_v[i, :, units:] = (cot * act).astype(jnp.bfloat16)
        gs[i].start()
        gl[i].start()

        @pl.when(lead)
        def _():
            gx[0][i].start()
            gy[0][i].start()
            for n in [i - 1] * (i > 0) + [i] * (i == 3):
                gs[n].wait_recv()
                if n:
                    gx[1][n].start()
                    gy[1][n].start()

        if i == 0:
            @pl.when(core == 1)
            def _():
                for copy in early:
                    copy.start()

    rows_local.wait()
    rows_far.wait_recv()
    for i in range(4):
        w_copies[i].wait()
        if i >= 2:
            swaps[i - 2].wait_send()
        for p in range(2):
            product = jnp.dot(rows_v[...], w_buf[i % 2, p], preferred_element_type=jnp.float32)
            keep_v[i % 2, p] = product[:base]
            send_v[i % 2, p] = product[base:]
        swaps[i].start()
        if i < 2:
            w_copies.append(w_copy(i + 2))
            w_copies[-1].start()
        if i == 0:
            local[0].wait()
            rows_b[0].start()
            w_far.start()
        else:
            combine(i - 1)
        if i == 1:
            for j in range(2, 8):
                xs[j].wait_recv()
                for copy in xz[j - 2]:
                    copy.start()
        if i == 2:
            for m in range(1, 4):
                rows_a[m - 1].wait_recv()
                rows_b[m].start()
    adv[...] = prompt_in[...].astype(jnp.float32)
    combine(3)
    for copy in rows_b + cots[1:] + [w_far]:
        copy.wait_recv()
    for copy in local[1:]:
        copy.wait()
    lane = lax.broadcasted_iota(jnp.int32, (count, wide), 1)
    keep = lane >= core * (2 * wide - units)

    def norm_rows():
        def one(b, _):
            shifted = base_buf[b].astype(jnp.float32) + adv[...]
            inverse = lax.rsqrt(jnp.mean(shifted * shifted, axis=-1, keepdims=True) + 1e-05)
            x_v[pl.ds(pl.multiple_of(b * count, count), count)] = (shifted * inverse * gain_ref[...]).astype(jnp.bfloat16)
            inv_v[b] = jnp.broadcast_to(inverse, (count, 128))
            return 0
        lax.fori_loop(0, 8, one, 0)

    def unit_grads():
        near = x_v[:, near_half]
        far = x_v[:, far_half]
        gate, up = [
            jnp.dot(near, near_v[p], preferred_element_type=jnp.float32)
            + jnp.dot(far, far_v[p], preferred_element_type=jnp.float32)
            for p in range(2)
        ]
        act, slope = silu_parts(gate)
        cot = jnp.concatenate(
            [jnp.where(keep, cot_buf[b].astype(jnp.float32), 0.0) for b in range(8)], axis=0
        )
        gp_v[:, pl.ds(0, wide)] = (cot * up * slope).astype(jnp.bfloat16)
        gp_v[:, pl.ds(wide, wide)] = (cot * act).astype(jnp.bfloat16)

    dims = (((1,), (1,)), ((), ()))
    chunk = 512

    def feature_grads():
        for source, start in ((near_v, core * half), (far_v, (1 - core) * half)):
            def one(i, _):
                rows = pl.ds(pl.multiple_of(i * chunk, chunk), chunk)
                fg_v[:, pl.ds(pl.multiple_of(start + i * chunk, chunk), chunk)] = lax.dot_general(
                    gp_v[:, pl.ds(0, wide)], source[0, rows], dims, preferred_element_type=jnp.float32
                ) + lax.dot_general(
                    gp_v[:, pl.ds(wide, wide)], source[1, rows], dims, preferred_element_type=jnp.float32
                )
                return 0
            lax.fori_loop(0, half // chunk, one, 0)

    def row_grads():
        part[...] = jnp.zeros_like(part)
        def one(b, _):
            shifted = base_buf[b].astype(jnp.float32) + adv[...]
            scaled = gain_ref[...] * fg_v[pl.ds(pl.multiple_of(b * count, count), count)]
            inverse = inv_v[b][:, :1]
            middle = jnp.mean(shifted * scaled, axis=-1, keepdims=True)
            part[...] += inverse * scaled - shifted * (inverse * inverse * inverse * middle)
            return 0
        lax.fori_loop(0, 8, one, 0)

    lead_waits, other_waits = [], []

    def exchange(k):
        for a in range(4):
            send_a[k, a] = part[:, 2 * a * block : 2 * (a + 1) * block].astype(jnp.bfloat16)
        sib = remote(send_a.at[k], recv_s.at[k], s_0.at[k], r_0.at[k], ids[1])
        first = [
            remote(send_b.at[k, rel[2 * m][0]], recv_a.at[k, m], s_1.at[k, m], r_1.at[k, m], ids[2 * m])
            for m in range(1, 4)
        ]
        second = [
            remote(recv_b.at[k, t], recv_b.at[k, t], s_2.at[k, j], r_2.at[k, j], line_ids[j])
            for j in range(tensors - 1)
        ]
        third = [
            remote(recv_c.at[k, chip], recv_c.at[k, chip], s_3.at[k, m], r_3.at[k, m], ids[2 * m])
            for m in range(1, 4)
        ]
        fourth = [
            remote(
                recv_c.at[k, rel[2 * m][0]], recv_c.at[k, rel[2 * m][0]],
                s_3.at[k, 4 + m], r_3.at[k, 4 + m], ids[1],
            )
            for m in range(4)
        ]

        @pl.when(lead)
        def _():
            sib.start()
            for copy in fourth:
                copy.wait_recv()

        @pl.when(core == 1)
        def _():
            sib.wait_recv()
            for a in range(4):
                send_b[k, a] = (
                    send_a[k, a].astype(jnp.float32) + recv_s[k, a].astype(jnp.float32)
                ).astype(jnp.bfloat16)
            for copy in first:
                copy.start()
            total = send_b[k, chip].astype(jnp.float32)
            for m in range(1, 4):
                first[m - 1].wait_recv()
                total = total + recv_a[k, m].astype(jnp.float32)
            recv_b[k, t] = total.astype(jnp.bfloat16)
            for copy in second:
                copy.start()
            for copy in second:
                copy.wait_recv()
            total = recv_b[k, 0].astype(jnp.float32)
            for j in range(1, tensors):
                total = total + recv_b[k, j].astype(jnp.float32)
            recv_c[k, chip] = total.astype(jnp.bfloat16)
            for copy in third + fourth[:1]:
                copy.start()
            for m in range(1, 4):
                third[m - 1].wait_recv()
                fourth[m].start()

        lead_waits.append(sib)
        other_waits.extend(first + second + third + fourth)
        square = jnp.zeros((count, 1), jnp.float32)
        for p in range(4):
            piece = recv_c[k, p].astype(jnp.float32)
            square = square + jnp.sum(piece * piece, axis=-1, keepdims=True)
        scale = step_ref[k] * lax.rsqrt(square / width + 1e-06)
        for p in range(4):
            at = slice(2 * p * block, 2 * (p + 1) * block)
            adv[:, at] = adv[:, at] + scale * recv_c[k, p].astype(jnp.float32)

    def pass_on(source, n, i):
        source.wait_recv()
        if n < 6 and (n < 4) == (i < 2):
            fd[n % 2][i].start()
        side[n - 2][i].start()

    def forward_some(pieces):
        @pl.when(lead)
        def _():
            for n, i in pieces:
                pass_on((gx, gy)[n // 2 - 1][n % 2][i], n, i)

    stages = [[], [(2, 0), (2, 1), (3, 0), (3, 1)], [(4, 2), (5, 2), (4, 3)], [(5, 3)]]
    rest = [(2, 2), (2, 3), (3, 2), (3, 3), (4, 0), (4, 1), (5, 0), (5, 1)]
    for k in range(steps):
        norm_rows()
        unit_grads()
        feature_grads()
        row_grads()
        exchange(k)
        if k + 1 < len(stages):
            forward_some(stages[k + 1])
    for k in range(steps, 3):
        forward_some(stages[k + 1])
    adv_out[...] = adv[...]
    norm_rows()
    unit_grads()
    xp_out[...] = x_v[:, mine_block]
    mid = 4 * count
    parts = [pl.ds(0, mid), pl.ds(mid, mid)]

    def hop(src, slot, h, k, device):
        source = gp_all.at[slot] if src is None else src
        return remote(source.at[parts[h]], gp_all.at[slot, parts[h]], s_o.at[k], r_o.at[k], device)

    os = remote(gp_v, gp_all.at[me], s_o.at[4], r_o.at[4], ids[1])
    ol = pltpu.make_async_copy(gp_v, gp_all.at[me], s_local.at[4])
    os.start()
    ol.start()
    ox = [[hop(gp_v if q == 0 else None, place[q], h, (0, 5)[q] + h, ids[2]) for h in range(2)] for q in range(2)]
    oy = [[hop(gp_v if q == 0 else None, place[q], h, (2, 7)[q] + h, ids[4]) for h in range(2)] for q in range(2)]
    od = [[hop(None, place[2 + q], 0, 9 + q, ids[4]) for q in range(2)], [hop(None, place[4 + q], 1, 11 + q, ids[2]) for q in range(2)]]
    back = [[hop(None, place[n], h, 13 + 2 * (n - 2) + h, ids[1]) for h in range(2)] for n in range(2, 8)]
    backs = [copy for two in back for copy in two]

    @pl.when(core == 1)
    def _():
        for copy in (ox[0][0], oy[0][1], ox[0][1], oy[0][0]):
            copy.start()
        os.wait_recv()
        for copy in (ox[1][0], oy[1][1], ox[1][1], oy[1][0]):
            copy.start()
        for q in range(2):
            ox[q][0].wait_recv()
            od[0][q].start()
            back[q][0].start()
            oy[q][1].wait_recv()
            od[1][q].start()
            back[2 + q][1].start()
        for q in range(2):
            ox[q][1].wait_recv()
            back[q][1].start()
            oy[q][0].wait_recv()
            back[2 + q][0].start()
        for q in range(2):
            for h in range(2):
                od[h][q].wait_recv()
                back[4 + q][h].start()
        for copy in gs:
            copy.wait_recv()
        for four in side:
            for copy in four:
                copy.wait_recv()
        for copy in other_waits + early + ox[0] + ox[1] + oy[0] + oy[1] + od[0] + od[1] + backs:
            copy.wait_send()

    @pl.when(lead)
    def _():
        for n, i in rest:
            pass_on((gx, gy)[n // 2 - 1][n % 2][i], n, i)
        for i in range(4):
            for q in range(2):
                pass_on(fd[q][i], 6 + q, i)
        os.wait_recv()
        for copy in backs:
            copy.wait_recv()
        for copy in lead_waits + gx[0] + gx[1][1:] + gy[0] + gy[1][1:] + fd[0] + fd[1]:
            copy.wait_send()
        for four in side:
            for copy in four:
                copy.wait_send()

    for copy in [xs[1]] + xzs:
        copy.wait_recv()
    for copy in gl + [ol, xl]:
        copy.wait()
    for copy in [rows_far, w_far, os] + rows_a + rows_b + cots[1:] + xs[1:] + xzs + swaps[2:] + gs:
        copy.wait_send()


def main_call(pair, normed, cot, prompt, base_rows, base_cot, gain, step_sizes):
    tensors = lax.axis_size("tensor")
    steps = step_sizes.shape[0]
    count, width = base_rows.shape
    half, shard = pair.shape[1:]
    units, wide = shard // 4, 512
    block = width // 8
    base = normed.shape[0]
    bf, f32 = jnp.bfloat16, jnp.float32
    dma = pltpu.SemaphoreType.DMA
    vmem = pl.BlockSpec(memory_space=pltpu.VMEM)
    hbm = pl.BlockSpec(memory_space=pl.ANY)
    return pl.pallas_call(
        functools.partial(main_kernel, tensors, steps),
        out_shape=[
            jax.ShapeDtypeStruct((count, width), f32),
            jax.ShapeDtypeStruct((8 * count, block), bf),
            jax.ShapeDtypeStruct((8, 4, base, 2 * units), bf),
            jax.ShapeDtypeStruct((8, base, block), bf),
            jax.ShapeDtypeStruct((8, 8 * count, 2 * wide), bf),
        ],
        in_specs=[hbm, hbm, vmem, vmem, hbm, hbm, vmem, pl.BlockSpec(memory_space=pltpu.SMEM)],
        out_specs=[vmem, vmem, hbm, hbm, hbm],
        scratch_shapes=[
            pltpu.VMEM((2 * base, half), bf),
            pltpu.VMEM((2, 2, half, units), bf),
            pltpu.VMEM((2, 2, base, units), f32),
            pltpu.VMEM((2, 2, base, units), f32),
            pltpu.VMEM((4, 2, base, units), f32),
            pltpu.VMEM((4, base, 2 * units), bf),
            pltpu.VMEM((8, count, width), bf),
            pltpu.VMEM((8, count, wide), bf),
            pltpu.VMEM((2, half, wide), bf),
            pltpu.VMEM((2, half, wide), bf),
            pltpu.VMEM((8 * count, width), bf),
            pltpu.VMEM((8 * count, width), f32),
            pltpu.VMEM((8, count, 128), f32),
            pltpu.VMEM((count, width), f32),
            pltpu.VMEM((count, width), f32),
            pltpu.VMEM((steps, 4, count, 2 * block), bf),
            pltpu.VMEM((steps, 4, count, 2 * block), bf),
            pltpu.VMEM((steps, 4, count, 2 * block), bf),
            pltpu.VMEM((steps, 4, count, 2 * block), bf),
            pltpu.VMEM((steps, tensors, count, 2 * block), bf),
            pltpu.VMEM((steps, 4, count, 2 * block), bf),
            pltpu.VMEM((8 * count, 2 * wide), bf),
        ]
        + [dma((10,))] + [dma((2,))] * 3 + [dma((4,))] * 2 + [dma((52,))] * 2 + [dma((8,))] * 6 + [dma((8, tensors))] * 2
        + [dma((steps,))] * 2 + [dma((steps, 4))] * 2 + [dma((steps, tensors))] * 2
        + [dma((steps, 8))] * 2 + [dma((25,))] * 2,
        compiler_params=pltpu.CompilerParams(
            collective_id=2, has_side_effects=True, vmem_limit_bytes=62 << 20
        ),
        cost_estimate=pl.CostEstimate(flops=100_000_000_000, bytes_accessed=100_000_000, transcendentals=0),
        name="attack_and_gather",
    )(pair, normed, cot, prompt, base_rows, base_cot, gain.reshape(1, width), step_sizes)


def grad_kernel(x_ref, xp_ref, g_ref, gp0_ref, gp1_ref, out_ref, sq_ref, xt_v, xpt_v):
    step = pl.program_id(0) * pl.num_programs(1) + pl.program_id(1)

    @pl.when(step == 0)
    def _():
        xt_v[...] = x_ref[...].T
        xpt_v[...] = xp_ref[...].T
        sq_ref[...] = jnp.zeros_like(sq_ref)

    extra = 2 * gp0_ref.shape[2] - out_ref.shape[2]
    rows = g_ref.shape[0] * g_ref.shape[2]
    gp = jnp.concatenate([gp0_ref[0], gp1_ref[0][:, extra:]], axis=1)
    block = jnp.dot(
        xt_v[...], g_ref[...].reshape(rows, g_ref.shape[3]), preferred_element_type=jnp.float32
    ) + jnp.dot(xpt_v[...], gp, preferred_element_type=jnp.float32)
    out_ref[0] = block
    sq_ref[...] += jnp.sum((block * block).reshape(-1, 8, block.shape[1]), axis=0)


def grad_call(x_all, xp, g_all, gp_all):
    eight, _, own_base, pair_units = g_all.shape
    cols = 4 * pair_units
    block = x_all.shape[2]
    wide = gp_all.shape[2] // 2
    shard = cols // 2
    units = shard // 4
    prompts = xp.shape[0]
    f32 = jnp.float32
    return pl.pallas_call(
        grad_kernel,
        out_shape=[
            jax.ShapeDtypeStruct((2, block, shard), f32),
            jax.ShapeDtypeStruct((8, units), f32),
        ],
        grid=(2, 4),
        in_specs=[
            pl.BlockSpec((eight * own_base, block), lambda p, j: (0, 0)),
            pl.BlockSpec((prompts, block), lambda p, j: (0, 0)),
            pl.BlockSpec((eight, 1, own_base, units), lambda p, j: (0, j, 0, p)),
            pl.BlockSpec((1, prompts, wide), lambda p, j: (2 * j, 0, p)),
            pl.BlockSpec((1, prompts, wide), lambda p, j: (2 * j + 1, 0, p)),
        ],
        out_specs=[
            pl.BlockSpec((1, block, units), lambda p, j: (p, 0, j)),
            pl.BlockSpec((8, units), lambda p, j: (0, 0)),
        ],
        scratch_shapes=[
            pltpu.VMEM((block, eight * own_base), jnp.bfloat16),
            pltpu.VMEM((block, prompts), jnp.bfloat16),
        ],
        compiler_params=pltpu.CompilerParams(vmem_limit_bytes=48 << 20),
        cost_estimate=pl.CostEstimate(
            flops=2 * block * cols * (eight * own_base + prompts), bytes_accessed=50_000_000, transcendentals=0
        ),
        name="weight_grad",
    )(x_all.reshape(eight * own_base, block), xp, g_all, gp_all, gp_all)


def result_kernel(scale_ref, grad_ref, out_ref):
    _, rows, cols = grad_ref.shape
    n = 128
    to = lax.broadcasted_iota(jnp.int32, (2 * n, 2 * n), 0)
    source = jnp.where(lax.rem(to, 2) == 0, to // 2, n + to // 2)
    order = jnp.where(lax.broadcasted_iota(jnp.int32, (2 * n, 2 * n), 1) == source, 1.0, 0.0).astype(jnp.bfloat16)
    for r in range(0, rows, n):
        both = jnp.concatenate(
            [(grad_ref[p, r : r + n] * scale_ref[0]).astype(jnp.bfloat16) for p in range(2)], axis=0
        )
        mixed = jnp.dot(order, both, preferred_element_type=jnp.float32).astype(jnp.bfloat16)
        out_ref[r : r + n] = mixed.reshape(n, 2, cols)


def result_call(scale, weight_grad):
    _, rows, shard = weight_grad.shape
    cols = 512
    return pl.pallas_call(
        result_kernel,
        out_shape=jax.ShapeDtypeStruct((rows, 2, shard), jnp.bfloat16),
        grid=(shard // cols,),
        in_specs=[
            pl.BlockSpec(memory_space=pltpu.SMEM),
            pl.BlockSpec((2, rows, cols), lambda j: (0, 0, j)),
        ],
        out_specs=pl.BlockSpec((rows, 2, cols), lambda j: (0, 0, j)),
        compiler_params=pltpu.CompilerParams(vmem_limit_bytes=48 << 20),
        name="scaled_result",
    )(scale.reshape(1), weight_grad)


def per_device(states, norm_gain, gate_up, cotangent, prompt, step_sizes, insert_at, lengths):
    chips, cores = lax.axis_size("dp"), lax.axis_size("replica")
    shard = gate_up.shape[2]
    count = prompt.shape[0]
    fits = (
        chips == 4 and cores == 2 and states.shape[2] % (1024 * lax.axis_size("tensor")) == 0 and states.shape[0] == 1 and shard % (chips * 128) == 0
        and shard // chips > 512 and shard // chips <= 1024 and shard % 512 == 0
        and gate_up.shape[0] % 1024 == 0 and count % 16 == 0 and (states.shape[1] - count) % 16 == 0
    )
    if not fits:
        return per_device_general(
            states, norm_gain, gate_up, cotangent, prompt, step_sizes, insert_at, lengths
        )
    chip, core = lax.axis_index("dp"), lax.axis_index("replica")
    half = gate_up.shape[0]
    width = half * cores
    tokens = states.shape[1]
    base = tokens - count
    units = shard // chips
    start = insert_at[0]

    pair = jnp.transpose(gate_up, (1, 0, 2))

    spot = lax.broadcasted_iota(jnp.int32, (base, 1), 0)
    ahead = spot < start
    position = jnp.where(ahead, spot, spot + count)
    rows = jnp.where(ahead, states[0, :base], states[0, count:]).astype(jnp.float32)
    cot = jnp.where(ahead, cotangent[0, :base], cotangent[0, count:])
    cot = jnp.where(position < lengths[0], cot, jnp.zeros_like(cot))
    normed = (rows * row_scale(rows) * norm_gain).astype(jnp.bfloat16)
    base_rows = lax.dynamic_slice_in_dim(states[0], start, count, 0)
    base_cot = lax.dynamic_slice_in_dim(cotangent[0], start, count, 0)

    adversary, xp, g_all, x_all, gp_all = main_call(
        pair, normed, cot, prompt, base_rows, base_cot, norm_gain, step_sizes
    )
    weight_grad, squares = grad_call(x_all, xp, g_all, gp_all)
    squares = sum_everywhere(jnp.sum(squares))
    scale = lax.rsqrt(squares / (2 * D * FF) + 1e-06)
    weight_step = result_call(scale, weight_grad)
    column_count = width // lax.axis_size("tensor")
    prompt_final = lax.dynamic_slice_in_dim(
        adversary, lax.axis_index("tensor") * column_count, column_count, 1
    )
    return (prompt_final, weight_step)


def solution(mesh):
    return jax.shard_map(
        per_device,
        mesh=mesh,
        in_specs=(
            P(("dp", "replica"), None, None),
            P(),
            P("replica", None, "tensor"),
            P(("dp", "replica"), None, "tensor"),
            P(),
            P(),
            P(("dp", "replica")),
            P(("dp", "replica")),
        ),
        out_specs=(P(None, "tensor"), P(("dp", "replica"), None, "tensor")),
        check_vma=False,
    )
```

```python
import functools

import jax
import jax.numpy as jnp
from jax import lax
from jax.experimental import pallas as pl
from jax.experimental.pallas import tpu as pltpu
from jax.sharding import PartitionSpec as P

D = 4096
FF = 14336
MESH = pl.DeviceIdType.MESH


def row_scale(feature_rows):
    return lax.rsqrt(jnp.mean(feature_rows * feature_rows, axis=-1, keepdims=True) + 1e-05)


def silu_parts(gate_values):
    sigmoid_value = jax.nn.sigmoid(gate_values)
    return (
        gate_values * sigmoid_value,
        sigmoid_value * (1.0 + gate_values * (1.0 - sigmoid_value)),
    )


def hidden_grads(normalized, weight_pair, cotan_rows):
    unit_count = weight_pair.shape[1] // 2
    projected = jnp.dot(normalized, weight_pair, preferred_element_type=jnp.float32)
    activated, derivative = silu_parts(projected[:, :unit_count])
    up_part = projected[:, unit_count:]
    return jnp.concatenate(
        [cotan_rows * up_part * derivative, cotan_rows * activated], axis=1
    ).astype(jnp.bfloat16)


def step_kernel(
    tensors, chips, cores, partial_ref, adversary_ref, step_ref, out_ref,
    plane_buf, line_buf, mine, send1, recv1, send2, recv2, send3, recv3, send4, recv4,
):
    group = chips * cores
    t = lax.axis_index("tensor")
    g = lax.axis_index("dp") * cores + lax.axis_index("replica")
    rows = partial_ref.shape[0] // group
    own = rows // tensors
    plane = [lax.rem(g + k, group) for k in range(1, group)]
    line = [lax.rem(t + k, tensors) for k in range(1, tensors)]
    plane_ids = [{"dp": p // cores, "replica": lax.rem(p, cores)} for p in plane]
    line_ids = [{"tensor": p} for p in line]

    barrier = pltpu.get_barrier_semaphore()
    for device in plane_ids + line_ids:
        pl.semaphore_signal(barrier, inc=1, device_id=device, device_id_type=MESH)
    pl.semaphore_wait(barrier, group + tensors - 2)

    def exchange(pairs, ids, sends, recvs):
        copies = []
        for k, ((source, target), device) in enumerate(zip(pairs, ids)):
            copy = pltpu.make_async_remote_copy(
                src_ref=source, dst_ref=target, send_sem=sends.at[k], recv_sem=recvs.at[k],
                device_id=device, device_id_type=MESH,
            )
            copy.start()
            copies.append(copy)
        return copies

    first = exchange(
        [(partial_ref.at[pl.ds(p * rows, rows)], plane_buf.at[k]) for k, p in enumerate(plane)],
        plane_ids, send1, recv1,
    )
    total = partial_ref[pl.ds(g * rows, rows)]
    for k, copy in enumerate(first):
        copy.wait_recv()
        total = total + plane_buf[k]
    mine[...] = total
    second = exchange(
        [(mine.at[pl.ds(p * own, own)], line_buf.at[k]) for k, p in enumerate(line)],
        line_ids, send2, recv2,
    )
    grad = mine[pl.ds(t * own, own)]
    for k, copy in enumerate(second):
        copy.wait_recv()
        grad = grad + line_buf[k]
    square = jnp.sum(jnp.sum(grad * grad, axis=2, keepdims=True), axis=1, keepdims=True)
    count = partial_ref.shape[1] * partial_ref.shape[2]
    row = g * rows + t * own
    block = pl.ds(row, own)
    out_ref[block] = adversary_ref[block] + step_ref[0] * grad * lax.rsqrt(square / count + 1e-06)
    third = exchange([(out_ref.at[block], out_ref.at[block])] * len(line), line_ids, send3, recv3)
    for copy in third:
        copy.wait_recv()
    wide = pl.ds(g * rows, rows)
    fourth = exchange([(out_ref.at[wide], out_ref.at[wide])] * len(plane), plane_ids, send4, recv4)
    for copy in fourth:
        copy.wait_recv()
    for copy in first + second + third + fourth:
        copy.wait_send()


def apply_step(partial, adversary, step_size):
    tensors, chips, cores = (lax.axis_size(a) for a in ("tensor", "dp", "replica"))
    group = chips * cores
    count, width = partial.shape
    if count % (group * tensors) == 0 and width % 1024 == 0:
        shape = (count, 8, width // 8)
        rows = count // group
        own = rows // tensors
        dma = pltpu.SemaphoreType.DMA
        vmem = pl.BlockSpec(memory_space=pltpu.VMEM)
        result = pl.pallas_call(
            functools.partial(step_kernel, tensors, chips, cores),
            out_shape=jax.ShapeDtypeStruct(shape, jnp.float32),
            in_specs=[vmem, vmem, pl.BlockSpec(memory_space=pltpu.SMEM)],
            out_specs=vmem,
            scratch_shapes=[
                pltpu.VMEM((group - 1, rows) + shape[1:], jnp.float32),
                pltpu.VMEM((tensors - 1, own) + shape[1:], jnp.float32),
                pltpu.VMEM((rows,) + shape[1:], jnp.float32),
            ]
            + [dma((group - 1,))] * 2 + [dma((tensors - 1,))] * 4 + [dma((group - 1,))] * 2,
            compiler_params=pltpu.CompilerParams(
                collective_id=0, has_side_effects=True, vmem_limit_bytes=16 << 20
            ),
            cost_estimate=pl.CostEstimate(
                flops=20_000_000_000, bytes_accessed=3 * count * width * 4, transcendentals=0
            ),
            name="attack_step",
        )(partial.reshape(shape), adversary.reshape(shape), step_size)
        return result.reshape(count, width)
    grad = lax.psum(partial, ("tensor", "dp", "replica"))
    scale = lax.rsqrt(jnp.mean(grad * grad, axis=-1, keepdims=True) + 1e-06)
    return adversary + step_size[0] * grad * scale


def scalar_kernel(tensors, chips, cores, value_ref, out_ref, buf1, buf2, mine, send1, recv1, send2, recv2):
    group = chips * cores
    t = lax.axis_index("tensor")
    g = lax.axis_index("dp") * cores + lax.axis_index("replica")
    plane = [lax.rem(g + k, group) for k in range(1, group)]
    plane_ids = [{"dp": p // cores, "replica": lax.rem(p, cores)} for p in plane]
    line_ids = [{"tensor": lax.rem(t + k, tensors)} for k in range(1, tensors)]
    barrier = pltpu.get_barrier_semaphore()
    for device in plane_ids + line_ids:
        pl.semaphore_signal(barrier, inc=1, device_id=device, device_id_type=MESH)
    pl.semaphore_wait(barrier, group + tensors - 2)
    copies = []
    total = value_ref[...]
    source = value_ref
    for ids, buf, sends, recvs in ((plane_ids, buf1, send1, recv1), (line_ids, buf2, send2, recv2)):
        stage = []
        for k, device in enumerate(ids):
            copy = pltpu.make_async_remote_copy(
                src_ref=source, dst_ref=buf.at[k], send_sem=sends.at[k], recv_sem=recvs.at[k],
                device_id=device, device_id_type=MESH,
            )
            copy.start()
            stage.append(copy)
        for k, copy in enumerate(stage):
            copy.wait_recv()
            total = total + buf[k]
        copies += stage
        if buf is buf1:
            mine[...] = total
            source = mine
    out_ref[...] = total
    for copy in copies:
        copy.wait_send()


def sum_everywhere(value):
    tensors, chips, cores = (lax.axis_size(a) for a in ("tensor", "dp", "replica"))
    group = chips * cores
    if not 1 < tensors <= 8 or not 1 < group <= 16:
        return lax.psum(value, ("tensor", "dp", "replica"))
    dma = pltpu.SemaphoreType.DMA
    vmem = pl.BlockSpec(memory_space=pltpu.VMEM)
    return pl.pallas_call(
        functools.partial(scalar_kernel, tensors, chips, cores),
        out_shape=jax.ShapeDtypeStruct((8, 128), jnp.float32),
        in_specs=[vmem],
        out_specs=vmem,
        scratch_shapes=[
            pltpu.VMEM((group - 1, 8, 128), jnp.float32),
            pltpu.VMEM((tensors - 1, 8, 128), jnp.float32),
            pltpu.VMEM((8, 128), jnp.float32),
        ]
        + [dma((group - 1,))] * 2 + [dma((tensors - 1,))] * 2,
        compiler_params=pltpu.CompilerParams(
            collective_id=1, has_side_effects=True, vmem_limit_bytes=4 << 20
        ),
        name="scalar_sum",
    )(jnp.full((8, 128), value, jnp.float32))[0, 0]


def norm_kernel(start_ref, state_ref, parts_ref, gain_ref, out_ref):
    slots = parts_ref.shape[0] // 3
    tokens = state_ref.shape[1]
    shape = (tokens, 3 * slots)
    slot = lax.broadcasted_iota(jnp.int32, shape, 0) - start_ref[pl.program_id(0)]
    column = lax.rem(lax.broadcasted_iota(jnp.int32, shape, 1), slots)
    placed = jnp.dot(
        jnp.where(slot == column, 1.0, 0.0).astype(jnp.bfloat16), parts_ref[...],
        preferred_element_type=jnp.float32,
    )
    rows = state_ref[0].astype(jnp.float32) + placed
    scale = lax.rsqrt(jnp.mean(rows * rows, axis=-1, keepdims=True) + 1e-05)
    out_ref[0] = (rows * scale * gain_ref[...]).astype(jnp.bfloat16)


def normed_rows(starts, states, parts, gain):
    count, tokens, width = states.shape
    return pl.pallas_call(
        norm_kernel,
        out_shape=jax.ShapeDtypeStruct(states.shape, jnp.bfloat16),
        grid_spec=pltpu.PrefetchScalarGridSpec(
            num_scalar_prefetch=1,
            grid=(count,),
            in_specs=[
                pl.BlockSpec((1, tokens, width), lambda b, s: (b, 0, 0)),
                pl.BlockSpec(parts.shape, lambda b, s: (0, 0)),
                pl.BlockSpec((1, width), lambda b, s: (0, 0)),
            ],
            out_specs=pl.BlockSpec((1, tokens, width), lambda b, s: (b, 0, 0)),
        ),
        compiler_params=pltpu.CompilerParams(vmem_limit_bytes=48 << 20),
        cost_estimate=pl.CostEstimate(
            flops=count * tokens * width * 200, bytes_accessed=count * tokens * width * 4,
            transcendentals=0,
        ),
        name="normed_rows",
    )(starts, states, parts, gain.reshape(1, width)).reshape(count * tokens, width)


def per_device_general(states, norm_gain, gate_up, cotangent, prompt, step_sizes, insert_at, lengths):
    chips, cores = lax.axis_size("dp"), lax.axis_size("replica")
    chip, core = lax.axis_index("dp"), lax.axis_index("replica")
    half, _, shard_units = gate_up.shape
    units = shard_units // chips
    count = prompt.shape[0]
    tokens = states.shape[1]
    width = half * cores

    unit_slice = lax.dynamic_slice_in_dim(gate_up, chip * units, units, 2)
    weight_pair = lax.all_gather(
        unit_slice.reshape(half, 2 * units), "replica", axis=0, tiled=True
    )

    seq_states, seq_cotan, prompt_start = states[0], cotangent[0], insert_at[0]
    package = jnp.concatenate(
        [
            lax.dynamic_slice_in_dim(seq_states, prompt_start, count, 0),
            lax.dynamic_slice_in_dim(seq_cotan, prompt_start, count, 0),
            jnp.broadcast_to(insert_at.astype(jnp.bfloat16).reshape(1, 1), (count, 128)),
        ],
        axis=1,
    )
    package = lax.all_gather(package, "dp", axis=0, tiled=False)
    prompt_base = package[:, :, :width].astype(jnp.float32)
    prompt_cotan = (
        lax.dynamic_slice_in_dim(package, width + chip * units, units, 2)
        .reshape(chips * count, units)
        .astype(jnp.float32)
    )

    swap = [(i, (i + 1) % cores) for i in range(cores)]
    own_starts = package[:, 0, package.shape[2] - 1].astype(jnp.int32)
    seq_states, seq_cotan, _ = lax.optimization_barrier((seq_states, seq_cotan, weight_pair))
    own_states = lax.all_gather(seq_states, "dp", axis=0, tiled=False)
    other_starts = lax.ppermute(own_starts, "replica", swap)
    positions = lax.broadcasted_iota(jnp.int32, (tokens, 1), 0)
    live_cotan = jnp.where(positions < lengths[0], seq_cotan, jnp.zeros_like(seq_cotan))

    def shifted_perm(k):
        return [(i, (i + k) % chips) for i in range(chips)]

    cotan_blocks = []
    for k in range(chips):
        block = lax.dynamic_slice_in_dim(live_cotan, lax.rem(chip + k, chips) * units, units, 1)
        cotan_blocks.append(lax.ppermute(block, "dp", shifted_perm(k)) if k else block)
    stacked = jnp.stack(cotan_blocks)
    token_cotan = jnp.concatenate(
        [
            lax.dynamic_index_in_dim(stacked, lax.rem(chip - j + chips, chips), 0, keepdims=False)
            for j in range(chips)
        ],
        axis=0,
    )

    adversary = prompt.astype(jnp.float32)
    for attack_step in range(step_sizes.shape[0]):
        shifted = prompt_base + adversary[None]
        inverse_rms = row_scale(shifted)
        normalized = (shifted * inverse_rms * norm_gain).astype(jnp.bfloat16)
        unit_grads = hidden_grads(normalized.reshape(chips * count, width), weight_pair, prompt_cotan)
        feature_grad = lax.dot_general(
            unit_grads, weight_pair, (((1,), (1,)), ((), ())), preferred_element_type=jnp.float32
        ).reshape(chips, count, width)
        scaled = norm_gain * feature_grad
        feature_mean = jnp.mean(shifted * scaled, axis=-1, keepdims=True)
        partial = jnp.sum(
            inverse_rms * scaled - shifted * (inverse_rms * inverse_rms * inverse_rms) * feature_mean,
            axis=0,
        )
        adversary = apply_step(partial, adversary, step_sizes[attack_step : attack_step + 1])
        if attack_step == step_sizes.shape[0] - 2:
            own_states, adversary = lax.optimization_barrier((own_states, adversary))
            other_states = lax.ppermute(own_states, "replica", swap)

    high = lax.reduce_precision(adversary, 8, 7)
    middle = lax.reduce_precision(adversary - high, 8, 7)
    low = adversary - high - middle
    parts = jnp.concatenate([high, middle, low], axis=0).astype(jnp.bfloat16)
    own_normed = normed_rows(own_starts, own_states, parts, norm_gain)
    own_grads = hidden_grads(own_normed, weight_pair, token_cotan.astype(jnp.float32))
    other_grads = lax.ppermute(own_grads, "replica", swap)
    other_normed = normed_rows(other_starts, other_states, parts, norm_gain)

    block_width = width // (chips * cores)
    dims = (((0,), (0,)), ((), ()))
    squares = 0.0
    received = [None] * chips
    for k in [2 % chips, *[i for i in range(1, chips) if i != 2 % chips], 0] if chips > 2 else range(chips):
        start = (lax.rem(chip + k, chips) * cores + core) * block_width
        block = lax.dot_general(
            lax.dynamic_slice_in_dim(own_normed, start, block_width, 1), own_grads, dims,
            preferred_element_type=jnp.float32,
        ) + lax.dot_general(
            lax.dynamic_slice_in_dim(other_normed, start, block_width, 1), other_grads, dims,
            preferred_element_type=jnp.float32,
        )
        squares = squares + jnp.sum(block * block)
        sent = block.astype(jnp.bfloat16)
        received[k] = lax.ppermute(sent, "dp", shifted_perm(k)) if k else sent
    squares = sum_everywhere(squares)
    scale = lax.rsqrt(squares / (2 * D * FF) + 1e-06)
    stacked = jnp.stack(received)
    pieces = [
        lax.dynamic_index_in_dim(stacked, lax.rem(chip - j + chips, chips), 0, keepdims=False)
        for j in range(chips)
    ]
    weight_step = jnp.concatenate(
        [piece.reshape(block_width, 2, units) for piece in pieces], axis=2
    )
    weight_step = (weight_step.astype(jnp.float32) * scale).astype(jnp.bfloat16)
    column_count = width // lax.axis_size("tensor")
    prompt_final = lax.dynamic_slice_in_dim(
        adversary, lax.axis_index("tensor") * column_count, column_count, 1
    )
    return (prompt_final, weight_step)


def relative_devices(chip, core):
    pairs = []
    for m in range(4):
        other_chip = [chip, chip + 1 - 2 * lax.rem(chip, 2), lax.rem(chip + 2, 4), 3 - chip][m]
        for q in range(2):
            pairs.append((other_chip, core if q == 0 else 1 - core))
    return pairs


def main_kernel(
    tensors, steps,
    pair, normed, cot_ref, prompt_in, base_rows, base_cot, gain_ref, step_ref,
    adv_out, xp_out, g_all, x_all, gp_all, early_grad,
    rows_v, w_buf, keep_v, send_v, got_v, g_v,
    base_buf, cot_buf, near_v, far_v, x_v, fg_v, inv_v, adv, part,
    send_a, send_b, recv_s, recv_a, recv_b, recv_c, gp_v, xt_v,
    s_local, s_w, s_r, r_r, s_f, r_f, s_g, r_g, s_p, r_p, s_c, r_c, s_x, r_x, s_z, r_z, s_q, s_e,
    s_0, r_0, s_1, r_1, s_2, r_2, s_3, r_3, s_o, r_o,
):
    t = lax.axis_index("tensor")
    chip = lax.axis_index("dp")
    core = lax.axis_index("replica")
    me = chip * 2 + core
    lead = core == 0
    rel = relative_devices(chip, core)
    ids = [{"dp": a, "replica": b} for a, b in rel]
    place = [a * 2 + b for a, b in rel]
    wide = near_v.shape[2]
    half = pair.shape[1]
    units = pair.shape[2] // 4
    count, width = base_rows.shape
    block = width // 8
    base = normed.shape[0]

    def remote(src, dst, send, recv, device):
        return pltpu.make_async_remote_copy(
            src_ref=src, dst_ref=dst, send_sem=send, recv_sem=recv,
            device_id=device, device_id_type=MESH,
        )

    def w_copy(i):
        return pltpu.make_async_copy(pair.at[:, :, pl.ds(i * units, units)], w_buf.at[i % 2], s_w.at[i % 2])

    w_copies = [w_copy(0), w_copy(1)]
    for copy in w_copies:
        copy.start()
    near_half = pl.ds(pl.multiple_of(core * half, 128), half)
    far_half = pl.ds(pl.multiple_of((1 - core) * half, 128), half)
    rows_local = pltpu.make_async_copy(normed.at[:, near_half], rows_v.at[pl.ds(0, base)], s_local.at[0])
    rows_local.start()

    barrier = pltpu.get_barrier_semaphore()
    line_ids = [{"tensor": lax.rem(t + k, tensors)} for k in range(1, tensors)]
    for device in ids[1:] + line_ids:
        pl.semaphore_signal(barrier, inc=1, device_id=device, device_id_type=MESH)
    pl.semaphore_wait(barrier, 7 + tensors - 1)

    rows_far = remote(normed.at[:, far_half], rows_v.at[pl.ds(base, base)], s_r.at[0], r_r.at[0], ids[1])
    rows_far.start()
    rows_a = [remote(base_rows, base_buf.at[me], s_p.at[m], r_p.at[m], ids[2 * m]) for m in range(1, 4)]

    def first_unit(a, b):
        return pl.multiple_of(a * units + b * (units - wide), 128)

    cots = [None] + [
        remote(
            base_cot.at[:, pl.ds(first_unit(*rel[j]), wide)], cot_buf.at[me], s_c.at[j], r_c.at[j], ids[j]
        )
        for j in range(1, 8)
    ]
    w_far = remote(pair.at[:, :, pl.ds(first_unit(chip, 1 - core), wide)], far_v, s_r.at[1], r_r.at[1], ids[1])
    local = [
        pltpu.make_async_copy(base_rows, base_buf.at[me], s_local.at[1]),
        pltpu.make_async_copy(base_cot.at[:, pl.ds(first_unit(chip, core), wide)], cot_buf.at[me], s_local.at[2]),
        pltpu.make_async_copy(pair.at[:, :, pl.ds(first_unit(chip, core), wide)], near_v, s_local.at[3]),
    ]
    rows_b = [
        remote(base_buf.at[place[2 * m]], base_buf.at[place[2 * m]], s_p.at[4 + m], r_p.at[4 + m], ids[1])
        for m in range(4)
    ]
    quarter = block // tensors
    own_quarter = pl.ds(pl.multiple_of(t * quarter, 128), quarter)
    xs = [None]
    for j in range(1, 8):
        start = pl.multiple_of(place[j] * block, 128)
        if j == 1:
            src, dst = normed.at[:, pl.ds(start, block)], x_all.at[j]
        else:
            src = normed.at[:, pl.ds(pl.multiple_of(start + t * quarter, 128), quarter)]
            dst = x_all.at[j, :, own_quarter]
        xs.append(remote(src, dst, s_x.at[j], r_x.at[j], ids[j]))
    xz = [
        [
            remote(
                x_all.at[j, :, own_quarter], x_all.at[j, :, own_quarter],
                s_z.at[j, k], r_z.at[j, k], line_ids[k],
            )
            for k in range(tensors - 1)
        ]
        for j in range(2, 8)
    ]
    xzs = [copy for line in xz for copy in line]
    mine_block = pl.ds(pl.multiple_of(me * block, 128), block)
    xl = pltpu.make_async_copy(normed.at[:, mine_block], x_all.at[0], s_local.at[9])
    for copy in rows_a + cots[1:] + local + xs[1:] + [xl]:
        copy.start()

    def bulk(src, slot, i, k, device):
        return remote(src, g_all.at[slot, i], s_g.at[k], r_g.at[k], device)

    gx = [[bulk(g_v.at[i] if q == 0 else g_all.at[1, i], 2 + q, i, 4 * q + i, ids[2]) for i in range(4)] for q in range(2)]
    gy = [[bulk(g_v.at[i] if q == 0 else g_all.at[1, i], 4 + q, i, 8 + 4 * q + i, ids[4]) for i in range(4)] for q in range(2)]
    early = [bulk(g_v.at[0], 3, 0, 4, ids[3]), bulk(g_v.at[0], 5, 0, 12, ids[5])]
    gs = [bulk(g_v.at[i], 1, i, 16 + i, ids[1]) for i in range(4)]
    gl = [pltpu.make_async_copy(g_v.at[i], g_all.at[0, i], s_local.at[5 + i]) for i in range(4)]
    fd = [
        [bulk(g_all.at[(2 if i < 2 else 4) + q, i], 6 + q, i, 20 + 4 * q + i, ids[4 if i < 2 else 2]) for i in range(4)]
        for q in range(2)
    ]
    side = [[bulk(g_all.at[n, i], n + 1 - 2 * (n % 2), i, 28 + 4 * (n - 2) + i, ids[1]) for i in range(4)] for n in range(2, 8)]
    swaps = [remote(send_v.at[i % 2], got_v.at[i], s_f.at[i], r_f.at[i], ids[1]) for i in range(4)]

    def combine(i):
        swaps[i].wait_recv()
        gate = keep_v[i % 2, 0] + got_v[i, 0]
        up = keep_v[i % 2, 1] + got_v[i, 1]
        act, slope = silu_parts(gate)
        cot = cot_ref[:, i * units : (i + 1) * units].astype(jnp.float32)
        g_v[i, :, :units] = (cot * up * slope).astype(jnp.bfloat16)
        g_v[i, :, units:] = (cot * act).astype(jnp.bfloat16)
        gs[i].start()
        gl[i].start()

        @pl.when(lead)
        def _():
            gx[0][i].start()
            gy[0][i].start()
            for n in [i - 1] * (i > 0) + [i] * (i == 3):
                gs[n].wait_recv()
                if n:
                    gx[1][n].start()
                    gy[1][n].start()

        if i == 0:
            @pl.when(core == 1)
            def _():
                for copy in early:
                    copy.start()

    rows_local.wait()
    rows_far.wait_recv()
    for i in range(4):
        w_copies[i].wait()
        if i >= 2:
            swaps[i - 2].wait_send()
        for p in range(2):
            product = jnp.dot(rows_v[...], w_buf[i % 2, p], preferred_element_type=jnp.float32)
            keep_v[i % 2, p] = product[:base]
            send_v[i % 2, p] = product[base:]
        swaps[i].start()
        if i < 2:
            w_copies.append(w_copy(i + 2))
            w_copies[-1].start()
        if i == 0:
            local[0].wait()
            rows_b[0].start()
            w_far.start()
        else:
            combine(i - 1)
        if i == 1:
            for j in range(2, 8):
                xs[j].wait_recv()
                for copy in xz[j - 2]:
                    copy.start()
        if i == 2:
            for m in range(1, 4):
                rows_a[m - 1].wait_recv()
                rows_b[m].start()
    adv[...] = prompt_in[...].astype(jnp.float32)
    combine(3)
    for copy in rows_b + cots[1:] + [w_far]:
        copy.wait_recv()
    for copy in local[1:]:
        copy.wait()
    lane = lax.broadcasted_iota(jnp.int32, (count, wide), 1)
    keep = lane >= core * (2 * wide - units)

    def norm_rows():
        def one(b, _):
            shifted = base_buf[b].astype(jnp.float32) + adv[...]
            inverse = lax.rsqrt(jnp.mean(shifted * shifted, axis=-1, keepdims=True) + 1e-05)
            x_v[pl.ds(pl.multiple_of(b * count, count), count)] = (shifted * inverse * gain_ref[...]).astype(jnp.bfloat16)
            inv_v[b] = jnp.broadcast_to(inverse, (count, 128))
            return 0
        lax.fori_loop(0, 8, one, 0)

    def unit_grads():
        near = x_v[:, near_half]
        far = x_v[:, far_half]
        gate, up = [
            jnp.dot(near, near_v[p], preferred_element_type=jnp.float32)
            + jnp.dot(far, far_v[p], preferred_element_type=jnp.float32)
            for p in range(2)
        ]
        act, slope = silu_parts(gate)
        cot = jnp.concatenate(
            [jnp.where(keep, cot_buf[b].astype(jnp.float32), 0.0) for b in range(8)], axis=0
        )
        gp_v[:, pl.ds(0, wide)] = (cot * up * slope).astype(jnp.bfloat16)
        gp_v[:, pl.ds(wide, wide)] = (cot * act).astype(jnp.bfloat16)

    dims = (((1,), (1,)), ((), ()))
    chunk = 512

    def feature_grads():
        for source, start in ((near_v, core * half), (far_v, (1 - core) * half)):
            def one(i, _):
                rows = pl.ds(pl.multiple_of(i * chunk, chunk), chunk)
                fg_v[:, pl.ds(pl.multiple_of(start + i * chunk, chunk), chunk)] = lax.dot_general(
                    gp_v[:, pl.ds(0, wide)], source[0, rows], dims, preferred_element_type=jnp.float32
                ) + lax.dot_general(
                    gp_v[:, pl.ds(wide, wide)], source[1, rows], dims, preferred_element_type=jnp.float32
                )
                return 0
            lax.fori_loop(0, half // chunk, one, 0)

    def row_grads():
        part[...] = jnp.zeros_like(part)
        def one(b, _):
            shifted = base_buf[b].astype(jnp.float32) + adv[...]
            scaled = gain_ref[...] * fg_v[pl.ds(pl.multiple_of(b * count, count), count)]
            inverse = inv_v[b][:, :1]
            middle = jnp.mean(shifted * scaled, axis=-1, keepdims=True)
            part[...] += inverse * scaled - shifted * (inverse * inverse * inverse * middle)
            return 0
        lax.fori_loop(0, 8, one, 0)

    lead_waits, other_waits = [], []

    def exchange(k):
        for a in range(4):
            send_a[k, a] = part[:, 2 * a * block : 2 * (a + 1) * block].astype(jnp.bfloat16)
        sib = remote(send_a.at[k], recv_s.at[k], s_0.at[k], r_0.at[k], ids[1])
        first = [
            remote(send_b.at[k, rel[2 * m][0]], recv_a.at[k, m], s_1.at[k, m], r_1.at[k, m], ids[2 * m])
            for m in range(1, 4)
        ]
        second = [
            remote(recv_b.at[k, t], recv_b.at[k, t], s_2.at[k, j], r_2.at[k, j], line_ids[j])
            for j in range(tensors - 1)
        ]
        third = [
            remote(recv_c.at[k, chip], recv_c.at[k, chip], s_3.at[k, m], r_3.at[k, m], ids[2 * m])
            for m in range(1, 4)
        ]
        fourth = [
            remote(
                recv_c.at[k, rel[2 * m][0]], recv_c.at[k, rel[2 * m][0]],
                s_3.at[k, 4 + m], r_3.at[k, 4 + m], ids[1],
            )
            for m in range(4)
        ]

        @pl.when(lead)
        def _():
            sib.start()
            for copy in fourth:
                copy.wait_recv()

        @pl.when(core == 1)
        def _():
            sib.wait_recv()
            for a in range(4):
                send_b[k, a] = (
                    send_a[k, a].astype(jnp.float32) + recv_s[k, a].astype(jnp.float32)
                ).astype(jnp.bfloat16)
            for copy in first:
                copy.start()
            total = send_b[k, chip].astype(jnp.float32)
            for m in range(1, 4):
                first[m - 1].wait_recv()
                total = total + recv_a[k, m].astype(jnp.float32)
            recv_b[k, t] = total.astype(jnp.bfloat16)
            for copy in second:
                copy.start()
            for copy in second:
                copy.wait_recv()
            total = recv_b[k, 0].astype(jnp.float32)
            for j in range(1, tensors):
                total = total + recv_b[k, j].astype(jnp.float32)
            recv_c[k, chip] = total.astype(jnp.bfloat16)
            for copy in third + fourth[:1]:
                copy.start()
            for m in range(1, 4):
                third[m - 1].wait_recv()
                fourth[m].start()

        lead_waits.append(sib)
        other_waits.extend(first + second + third + fourth)
        square = jnp.zeros((count, 1), jnp.float32)
        for p in range(4):
            piece = recv_c[k, p].astype(jnp.float32)
            square = square + jnp.sum(piece * piece, axis=-1, keepdims=True)
        scale = step_ref[k] * lax.rsqrt(square / width + 1e-06)
        for p in range(4):
            at = slice(2 * p * block, 2 * (p + 1) * block)
            adv[:, at] = adv[:, at] + scale * recv_c[k, p].astype(jnp.float32)

    def pass_on(source, n, i):
        source.wait_recv()
        if n < 6 and (n < 4) == (i < 2):
            fd[n % 2][i].start()
        side[n - 2][i].start()

    def forward_some(pieces):
        @pl.when(lead)
        def _():
            for n, i in pieces:
                pass_on((gx, gy)[n // 2 - 1][n % 2][i], n, i)

    stages = [[], [(2, 0), (2, 1), (3, 0), (3, 1)], [(4, 2), (5, 2), (4, 3)], [(5, 3)]]
    rest = [(2, 2), (2, 3), (3, 2), (3, 3), (4, 0), (4, 1), (5, 0), (5, 1)]
    for k in range(steps):
        norm_rows()
        unit_grads()
        feature_grads()
        row_grads()
        exchange(k)
        if k + 1 < len(stages):
            forward_some(stages[k + 1])
    for k in range(steps, 3):
        forward_some(stages[k + 1])
    adv_out[...] = adv[...]
    norm_rows()
    unit_grads()
    xp_out[...] = x_v[:, mine_block]
    mid = 4 * count
    parts = [pl.ds(0, mid), pl.ds(mid, mid)]

    def hop(src, slot, h, k, device):
        source = gp_all.at[slot] if src is None else src
        return remote(source.at[parts[h]], gp_all.at[slot, parts[h]], s_o.at[k], r_o.at[k], device)

    os = remote(gp_v, gp_all.at[me], s_o.at[4], r_o.at[4], ids[1])
    ol = pltpu.make_async_copy(gp_v, gp_all.at[me], s_local.at[4])
    os.start()
    ol.start()
    ox = [[hop(gp_v if q == 0 else None, place[q], h, (0, 5)[q] + h, ids[2]) for h in range(2)] for q in range(2)]
    oy = [[hop(gp_v if q == 0 else None, place[q], h, (2, 7)[q] + h, ids[4]) for h in range(2)] for q in range(2)]
    od = [[hop(None, place[2 + q], 0, 9 + q, ids[4]) for q in range(2)], [hop(None, place[4 + q], 1, 11 + q, ids[2]) for q in range(2)]]
    back = [[hop(None, place[n], h, 13 + 2 * (n - 2) + h, ids[1]) for h in range(2)] for n in range(2, 8)]
    backs = [copy for two in back for copy in two]

    def early_loads(i):
        return [
            pltpu.make_async_copy(
                g_all.at[n, i, :, pl.ds(p * units, units)], w_buf.at[i % 2, p, pl.ds(n * base, base)],
                s_w.at[i % 2],
            )
            for n in range(6) for p in range(2)
        ]

    def early_stores(i, p):
        return [
            pltpu.make_async_copy(
                fg_v.at[:, pl.ds((2 * p + h) * units, units)],
                early_grad.at[p, pl.ds(h * (block // 2), block // 2), pl.ds(i * units, units)],
                s_e.at[p, h],
            )
            for h in range(2)
        ]

    def early_whole(i):
        return pltpu.make_async_copy(
            w_buf.at[i % 2, :, pl.ds(0, 6 * base)], w_buf.at[i % 2, :, pl.ds(0, 6 * base)], s_w.at[i % 2]
        )

    def early_begin():
        for j in range(6):
            pltpu.make_async_copy(x_all.at[j], x_v.at[pl.ds(0, base), pl.ds(j * block, block)], s_q.at[j]).start()
        for i in range(2):
            for copy in early_loads(i):
                copy.start()
        for j in range(6):
            pltpu.make_async_copy(x_all.at[j], x_v.at[pl.ds(0, base), pl.ds(j * block, block)], s_q.at[j]).wait()
        xt_v[...] = jnp.concatenate(
            [x_v[:base, j * block : (j + 1) * block] for j in range(6)], axis=0
        ).T

    def early_chunk(i):
        early_whole(i).wait()
        for p in range(2):
            if i:
                for copy in early_stores(i - 1, p):
                    copy.wait()
            tile = jnp.dot(xt_v[...], w_buf[i % 2, p, : 6 * base], preferred_element_type=jnp.float32)
            fg_v[:, 2 * p * units : (2 * p + 1) * units] = tile[: block // 2]
            fg_v[:, (2 * p + 1) * units : (2 * p + 2) * units] = tile[block // 2 :]
            for copy in early_stores(i, p):
                copy.start()
        if i < 2:
            for copy in early_loads(i + 2):
                copy.start()
        if i == 3:
            for p in range(2):
                for copy in early_stores(i, p):
                    copy.wait()

    for copy in [xs[1]] + xzs:
        copy.wait_recv()
    for copy in gl + [xl]:
        copy.wait()

    @pl.when(core == 1)
    def _():
        for copy in (ox[0][0], oy[0][1], ox[0][1], oy[0][0]):
            copy.start()
        os.wait_recv()
        for copy in (ox[1][0], oy[1][1], ox[1][1], oy[1][0]):
            copy.start()
        for copy in gs:
            copy.wait_recv()
        for four in side[:4]:
            for copy in four:
                copy.wait_recv()
        early_begin()
        early_chunk(0)
        for q in range(2):
            ox[q][0].wait_recv()
            od[0][q].start()
            back[q][0].start()
            oy[q][1].wait_recv()
            od[1][q].start()
            back[2 + q][1].start()
        early_chunk(1)
        early_chunk(2)
        for q in range(2):
            ox[q][1].wait_recv()
            back[q][1].start()
            oy[q][0].wait_recv()
            back[2 + q][0].start()
        early_chunk(3)
        for q in range(2):
            for h in range(2):
                od[h][q].wait_recv()
                back[4 + q][h].start()
        for four in side[4:]:
            for copy in four:
                copy.wait_recv()
        for copy in other_waits + early + ox[0] + ox[1] + oy[0] + oy[1] + od[0] + od[1] + backs:
            copy.wait_send()

    @pl.when(lead)
    def _():
        for n, i in rest:
            pass_on((gx, gy)[n // 2 - 1][n % 2][i], n, i)
        early_begin()
        for i in range(4):
            early_chunk(i)
            for q in range(2):
                pass_on(fd[q][i], 6 + q, i)
        os.wait_recv()
        for copy in backs:
            copy.wait_recv()
        for copy in lead_waits + gx[0] + gx[1][1:] + gy[0] + gy[1][1:] + fd[0] + fd[1]:
            copy.wait_send()
        for four in side:
            for copy in four:
                copy.wait_send()

    ol.wait()
    for copy in [rows_far, w_far, os] + rows_a + rows_b + cots[1:] + xs[1:] + xzs + swaps[2:] + gs:
        copy.wait_send()


def main_call(pair, normed, cot, prompt, base_rows, base_cot, gain, step_sizes):
    tensors = lax.axis_size("tensor")
    steps = step_sizes.shape[0]
    count, width = base_rows.shape
    half, shard = pair.shape[1:]
    units, wide = shard // 4, 512
    block = width // 8
    base = normed.shape[0]
    bf, f32 = jnp.bfloat16, jnp.float32
    dma = pltpu.SemaphoreType.DMA
    vmem = pl.BlockSpec(memory_space=pltpu.VMEM)
    hbm = pl.BlockSpec(memory_space=pl.ANY)
    return pl.pallas_call(
        functools.partial(main_kernel, tensors, steps),
        out_shape=[
            jax.ShapeDtypeStruct((count, width), f32),
            jax.ShapeDtypeStruct((8 * count, block), bf),
            jax.ShapeDtypeStruct((8, 4, base, 2 * units), bf),
            jax.ShapeDtypeStruct((8, base, block), bf),
            jax.ShapeDtypeStruct((8, 8 * count, 2 * wide), bf),
            jax.ShapeDtypeStruct((2, block, shard), f32),
        ],
        in_specs=[hbm, hbm, vmem, vmem, hbm, hbm, vmem, pl.BlockSpec(memory_space=pltpu.SMEM)],
        out_specs=[vmem, vmem, hbm, hbm, hbm, hbm],
        scratch_shapes=[
            pltpu.VMEM((2 * base, half), bf),
            pltpu.VMEM((2, 2, half, units), bf),
            pltpu.VMEM((2, 2, base, units), f32),
            pltpu.VMEM((2, 2, base, units), f32),
            pltpu.VMEM((4, 2, base, units), f32),
            pltpu.VMEM((4, base, 2 * units), bf),
            pltpu.VMEM((8, count, width), bf),
            pltpu.VMEM((8, count, wide), bf),
            pltpu.VMEM((2, half, wide), bf),
            pltpu.VMEM((2, half, wide), bf),
            pltpu.VMEM((8 * count, width), bf),
            pltpu.VMEM((8 * count, width), f32),
            pltpu.VMEM((8, count, 128), f32),
            pltpu.VMEM((count, width), f32),
            pltpu.VMEM((count, width), f32),
            pltpu.VMEM((steps, 4, count, 2 * block), bf),
            pltpu.VMEM((steps, 4, count, 2 * block), bf),
            pltpu.VMEM((steps, 4, count, 2 * block), bf),
            pltpu.VMEM((steps, 4, count, 2 * block), bf),
            pltpu.VMEM((steps, tensors, count, 2 * block), bf),
            pltpu.VMEM((steps, 4, count, 2 * block), bf),
            pltpu.VMEM((8 * count, 2 * wide), bf),
            pltpu.VMEM((block, 6 * base), bf),
        ]
        + [dma((10,))] + [dma((2,))] * 3 + [dma((4,))] * 2 + [dma((52,))] * 2 + [dma((8,))] * 6 + [dma((8, tensors))] * 2 + [dma((8,)), dma((2, 2))]
        + [dma((steps,))] * 2 + [dma((steps, 4))] * 2 + [dma((steps, tensors))] * 2
        + [dma((steps, 8))] * 2 + [dma((25,))] * 2,
        compiler_params=pltpu.CompilerParams(
            collective_id=2, has_side_effects=True, vmem_limit_bytes=62 << 20
        ),
        cost_estimate=pl.CostEstimate(flops=100_000_000_000, bytes_accessed=100_000_000, transcendentals=0),
        name="attack_and_gather",
    )(pair, normed, cot, prompt, base_rows, base_cot, gain.reshape(1, width), step_sizes)


def grad_kernel(x_ref, xp_ref, g_ref, gp0_ref, gp1_ref, early_ref, out_ref, sq_ref, xt_v, xpt_v):
    step = pl.program_id(0) * pl.num_programs(1) + pl.program_id(1)

    @pl.when(step == 0)
    def _():
        xt_v[...] = x_ref[...].T
        xpt_v[...] = xp_ref[...].T
        sq_ref[...] = jnp.zeros_like(sq_ref)

    extra = 2 * gp0_ref.shape[2] - out_ref.shape[2]
    rows = g_ref.shape[0] * g_ref.shape[2]
    gp = jnp.concatenate([gp0_ref[0], gp1_ref[0][:, extra:]], axis=1)
    block = early_ref[0] + jnp.dot(
        xt_v[...], g_ref[...].reshape(rows, g_ref.shape[3]), preferred_element_type=jnp.float32
    ) + jnp.dot(xpt_v[...], gp, preferred_element_type=jnp.float32)
    out_ref[0] = block
    sq_ref[...] += jnp.sum((block * block).reshape(-1, 8, block.shape[1]), axis=0)


def grad_call(x_all, xp, g_all, gp_all, early_grad):
    eight, _, own_base, pair_units = g_all.shape
    cols = 4 * pair_units
    block = x_all.shape[2]
    wide = gp_all.shape[2] // 2
    shard = cols // 2
    units = shard // 4
    prompts = xp.shape[0]
    f32 = jnp.float32
    return pl.pallas_call(
        grad_kernel,
        out_shape=[
            jax.ShapeDtypeStruct((2, block, shard), f32),
            jax.ShapeDtypeStruct((8, units), f32),
        ],
        grid=(2, 4),
        in_specs=[
            pl.BlockSpec((2 * own_base, block), lambda p, j: (3, 0)),
            pl.BlockSpec((prompts, block), lambda p, j: (0, 0)),
            pl.BlockSpec((2, 1, own_base, units), lambda p, j: (3, j, 0, p)),
            pl.BlockSpec((1, prompts, wide), lambda p, j: (2 * j, 0, p)),
            pl.BlockSpec((1, prompts, wide), lambda p, j: (2 * j + 1, 0, p)),
            pl.BlockSpec((1, block, units), lambda p, j: (p, 0, j)),
        ],
        out_specs=[
            pl.BlockSpec((1, block, units), lambda p, j: (p, 0, j)),
            pl.BlockSpec((8, units), lambda p, j: (0, 0)),
        ],
        scratch_shapes=[
            pltpu.VMEM((block, 2 * own_base), jnp.bfloat16),
            pltpu.VMEM((block, prompts), jnp.bfloat16),
        ],
        compiler_params=pltpu.CompilerParams(vmem_limit_bytes=48 << 20),
        cost_estimate=pl.CostEstimate(
            flops=2 * block * cols * (eight * own_base + prompts), bytes_accessed=50_000_000, transcendentals=0
        ),
        name="weight_grad",
    )(x_all.reshape(eight * own_base, block), xp, g_all, gp_all, gp_all, early_grad)


def result_kernel(scale_ref, grad_ref, out_ref):
    _, rows, cols = grad_ref.shape
    n = 128
    to = lax.broadcasted_iota(jnp.int32, (2 * n, 2 * n), 0)
    source = jnp.where(lax.rem(to, 2) == 0, to // 2, n + to // 2)
    order = jnp.where(lax.broadcasted_iota(jnp.int32, (2 * n, 2 * n), 1) == source, 1.0, 0.0).astype(jnp.bfloat16)
    for r in range(0, rows, n):
        both = jnp.concatenate(
            [(grad_ref[p, r : r + n] * scale_ref[0]).astype(jnp.bfloat16) for p in range(2)], axis=0
        )
        mixed = jnp.dot(order, both, preferred_element_type=jnp.float32).astype(jnp.bfloat16)
        out_ref[r : r + n] = mixed.reshape(n, 2, cols)


def result_call(scale, weight_grad):
    _, rows, shard = weight_grad.shape
    cols = 512
    return pl.pallas_call(
        result_kernel,
        out_shape=jax.ShapeDtypeStruct((rows, 2, shard), jnp.bfloat16),
        grid=(shard // cols,),
        in_specs=[
            pl.BlockSpec(memory_space=pltpu.SMEM),
            pl.BlockSpec((2, rows, cols), lambda j: (0, 0, j)),
        ],
        out_specs=pl.BlockSpec((rows, 2, cols), lambda j: (0, 0, j)),
        compiler_params=pltpu.CompilerParams(vmem_limit_bytes=48 << 20),
        name="scaled_result",
    )(scale.reshape(1), weight_grad)


def per_device(states, norm_gain, gate_up, cotangent, prompt, step_sizes, insert_at, lengths):
    chips, cores = lax.axis_size("dp"), lax.axis_size("replica")
    shard = gate_up.shape[2]
    count = prompt.shape[0]
    fits = (
        chips == 4 and cores == 2 and states.shape[2] % (1024 * lax.axis_size("tensor")) == 0 and states.shape[0] == 1 and shard % (chips * 128) == 0
        and shard // chips > 512 and shard // chips <= 1024 and shard % 512 == 0
        and gate_up.shape[0] % 1024 == 0 and count % 16 == 0 and (states.shape[1] - count) % 16 == 0
    )
    if not fits:
        return per_device_general(
            states, norm_gain, gate_up, cotangent, prompt, step_sizes, insert_at, lengths
        )
    chip, core = lax.axis_index("dp"), lax.axis_index("replica")
    half = gate_up.shape[0]
    width = half * cores
    tokens = states.shape[1]
    base = tokens - count
    units = shard // chips
    start = insert_at[0]

    pair = jnp.transpose(gate_up, (1, 0, 2))

    spot = lax.broadcasted_iota(jnp.int32, (base, 1), 0)
    ahead = spot < start
    position = jnp.where(ahead, spot, spot + count)
    rows = jnp.where(ahead, states[0, :base], states[0, count:]).astype(jnp.float32)
    cot = jnp.where(ahead, cotangent[0, :base], cotangent[0, count:])
    cot = jnp.where(position < lengths[0], cot, jnp.zeros_like(cot))
    normed = (rows * row_scale(rows) * norm_gain).astype(jnp.bfloat16)
    base_rows = lax.dynamic_slice_in_dim(states[0], start, count, 0)
    base_cot = lax.dynamic_slice_in_dim(cotangent[0], start, count, 0)

    adversary, xp, g_all, x_all, gp_all, early_grad = main_call(
        pair, normed, cot, prompt, base_rows, base_cot, norm_gain, step_sizes
    )
    weight_grad, squares = grad_call(x_all, xp, g_all, gp_all, early_grad)
    squares = sum_everywhere(jnp.sum(squares))
    scale = lax.rsqrt(squares / (2 * D * FF) + 1e-06)
    weight_step = result_call(scale, weight_grad)
    column_count = width // lax.axis_size("tensor")
    prompt_final = lax.dynamic_slice_in_dim(
        adversary, lax.axis_index("tensor") * column_count, column_count, 1
    )
    return (prompt_final, weight_step)


def solution(mesh):
    return jax.shard_map(
        per_device,
        mesh=mesh,
        in_specs=(
            P(("dp", "replica"), None, None),
            P(),
            P("replica", None, "tensor"),
            P(("dp", "replica"), None, "tensor"),
            P(),
            P(),
            P(("dp", "replica")),
            P(("dp", "replica")),
        ),
        out_specs=(P(None, "tensor"), P(("dp", "replica"), None, "tensor")),
        check_vma=False,
    )
```

```python
import functools

import jax
import jax.numpy as jnp
from jax import lax
from jax.experimental import pallas as pl
from jax.experimental.pallas import tpu as pltpu
from jax.sharding import PartitionSpec as P

D = 4096
FF = 14336
MESH = pl.DeviceIdType.MESH


def row_scale(feature_rows):
    return lax.rsqrt(jnp.mean(feature_rows * feature_rows, axis=-1, keepdims=True) + 1e-05)


def silu_parts(gate_values):
    sigmoid_value = jax.nn.sigmoid(gate_values)
    return (
        gate_values * sigmoid_value,
        sigmoid_value * (1.0 + gate_values * (1.0 - sigmoid_value)),
    )


def hidden_grads(normalized, weight_pair, cotan_rows):
    unit_count = weight_pair.shape[1] // 2
    projected = jnp.dot(normalized, weight_pair, preferred_element_type=jnp.float32)
    activated, derivative = silu_parts(projected[:, :unit_count])
    up_part = projected[:, unit_count:]
    return jnp.concatenate(
        [cotan_rows * up_part * derivative, cotan_rows * activated], axis=1
    ).astype(jnp.bfloat16)


def step_kernel(
    tensors, chips, cores, partial_ref, adversary_ref, step_ref, out_ref,
    plane_buf, line_buf, mine, send1, recv1, send2, recv2, send3, recv3, send4, recv4,
):
    group = chips * cores
    t = lax.axis_index("tensor")
    g = lax.axis_index("dp") * cores + lax.axis_index("replica")
    rows = partial_ref.shape[0] // group
    own = rows // tensors
    plane = [lax.rem(g + k, group) for k in range(1, group)]
    line = [lax.rem(t + k, tensors) for k in range(1, tensors)]
    plane_ids = [{"dp": p // cores, "replica": lax.rem(p, cores)} for p in plane]
    line_ids = [{"tensor": p} for p in line]

    barrier = pltpu.get_barrier_semaphore()
    for device in plane_ids + line_ids:
        pl.semaphore_signal(barrier, inc=1, device_id=device, device_id_type=MESH)
    pl.semaphore_wait(barrier, group + tensors - 2)

    def exchange(pairs, ids, sends, recvs):
        copies = []
        for k, ((source, target), device) in enumerate(zip(pairs, ids)):
            copy = pltpu.make_async_remote_copy(
                src_ref=source, dst_ref=target, send_sem=sends.at[k], recv_sem=recvs.at[k],
                device_id=device, device_id_type=MESH,
            )
            copy.start()
            copies.append(copy)
        return copies

    first = exchange(
        [(partial_ref.at[pl.ds(p * rows, rows)], plane_buf.at[k]) for k, p in enumerate(plane)],
        plane_ids, send1, recv1,
    )
    total = partial_ref[pl.ds(g * rows, rows)]
    for k, copy in enumerate(first):
        copy.wait_recv()
        total = total + plane_buf[k]
    mine[...] = total
    second = exchange(
        [(mine.at[pl.ds(p * own, own)], line_buf.at[k]) for k, p in enumerate(line)],
        line_ids, send2, recv2,
    )
    grad = mine[pl.ds(t * own, own)]
    for k, copy in enumerate(second):
        copy.wait_recv()
        grad = grad + line_buf[k]
    square = jnp.sum(jnp.sum(grad * grad, axis=2, keepdims=True), axis=1, keepdims=True)
    count = partial_ref.shape[1] * partial_ref.shape[2]
    row = g * rows + t * own
    block = pl.ds(row, own)
    out_ref[block] = adversary_ref[block] + step_ref[0] * grad * lax.rsqrt(square / count + 1e-06)
    third = exchange([(out_ref.at[block], out_ref.at[block])] * len(line), line_ids, send3, recv3)
    for copy in third:
        copy.wait_recv()
    wide = pl.ds(g * rows, rows)
    fourth = exchange([(out_ref.at[wide], out_ref.at[wide])] * len(plane), plane_ids, send4, recv4)
    for copy in fourth:
        copy.wait_recv()
    for copy in first + second + third + fourth:
        copy.wait_send()


def apply_step(partial, adversary, step_size):
    tensors, chips, cores = (lax.axis_size(a) for a in ("tensor", "dp", "replica"))
    group = chips * cores
    count, width = partial.shape
    if count % (group * tensors) == 0 and width % 1024 == 0:
        shape = (count, 8, width // 8)
        rows = count // group
        own = rows // tensors
        dma = pltpu.SemaphoreType.DMA
        vmem = pl.BlockSpec(memory_space=pltpu.VMEM)
        result = pl.pallas_call(
            functools.partial(step_kernel, tensors, chips, cores),
            out_shape=jax.ShapeDtypeStruct(shape, jnp.float32),
            in_specs=[vmem, vmem, pl.BlockSpec(memory_space=pltpu.SMEM)],
            out_specs=vmem,
            scratch_shapes=[
                pltpu.VMEM((group - 1, rows) + shape[1:], jnp.float32),
                pltpu.VMEM((tensors - 1, own) + shape[1:], jnp.float32),
                pltpu.VMEM((rows,) + shape[1:], jnp.float32),
            ]
            + [dma((group - 1,))] * 2 + [dma((tensors - 1,))] * 4 + [dma((group - 1,))] * 2,
            compiler_params=pltpu.CompilerParams(
                collective_id=0, has_side_effects=True, vmem_limit_bytes=16 << 20
            ),
            cost_estimate=pl.CostEstimate(
                flops=20_000_000_000, bytes_accessed=3 * count * width * 4, transcendentals=0
            ),
            name="attack_step",
        )(partial.reshape(shape), adversary.reshape(shape), step_size)
        return result.reshape(count, width)
    grad = lax.psum(partial, ("tensor", "dp", "replica"))
    scale = lax.rsqrt(jnp.mean(grad * grad, axis=-1, keepdims=True) + 1e-06)
    return adversary + step_size[0] * grad * scale


def scalar_kernel(tensors, chips, cores, value_ref, out_ref, buf1, buf2, mine, send1, recv1, send2, recv2):
    group = chips * cores
    t = lax.axis_index("tensor")
    g = lax.axis_index("dp") * cores + lax.axis_index("replica")
    plane = [lax.rem(g + k, group) for k in range(1, group)]
    plane_ids = [{"dp": p // cores, "replica": lax.rem(p, cores)} for p in plane]
    line_ids = [{"tensor": lax.rem(t + k, tensors)} for k in range(1, tensors)]
    barrier = pltpu.get_barrier_semaphore()
    for device in plane_ids + line_ids:
        pl.semaphore_signal(barrier, inc=1, device_id=device, device_id_type=MESH)
    pl.semaphore_wait(barrier, group + tensors - 2)
    copies = []
    total = value_ref[...]
    source = value_ref
    for ids, buf, sends, recvs in ((plane_ids, buf1, send1, recv1), (line_ids, buf2, send2, recv2)):
        stage = []
        for k, device in enumerate(ids):
            copy = pltpu.make_async_remote_copy(
                src_ref=source, dst_ref=buf.at[k], send_sem=sends.at[k], recv_sem=recvs.at[k],
                device_id=device, device_id_type=MESH,
            )
            copy.start()
            stage.append(copy)
        for k, copy in enumerate(stage):
            copy.wait_recv()
            total = total + buf[k]
        copies += stage
        if buf is buf1:
            mine[...] = total
            source = mine
    out_ref[...] = total
    for copy in copies:
        copy.wait_send()


def sum_everywhere(value):
    tensors, chips, cores = (lax.axis_size(a) for a in ("tensor", "dp", "replica"))
    group = chips * cores
    if not 1 < tensors <= 8 or not 1 < group <= 16:
        return lax.psum(value, ("tensor", "dp", "replica"))
    dma = pltpu.SemaphoreType.DMA
    vmem = pl.BlockSpec(memory_space=pltpu.VMEM)
    return pl.pallas_call(
        functools.partial(scalar_kernel, tensors, chips, cores),
        out_shape=jax.ShapeDtypeStruct((8, 128), jnp.float32),
        in_specs=[vmem],
        out_specs=vmem,
        scratch_shapes=[
            pltpu.VMEM((group - 1, 8, 128), jnp.float32),
            pltpu.VMEM((tensors - 1, 8, 128), jnp.float32),
            pltpu.VMEM((8, 128), jnp.float32),
        ]
        + [dma((group - 1,))] * 2 + [dma((tensors - 1,))] * 2,
        compiler_params=pltpu.CompilerParams(
            collective_id=1, has_side_effects=True, vmem_limit_bytes=4 << 20
        ),
        name="scalar_sum",
    )(jnp.full((8, 128), value, jnp.float32))[0, 0]


def norm_kernel(start_ref, state_ref, parts_ref, gain_ref, out_ref):
    slots = parts_ref.shape[0] // 3
    tokens = state_ref.shape[1]
    shape = (tokens, 3 * slots)
    slot = lax.broadcasted_iota(jnp.int32, shape, 0) - start_ref[pl.program_id(0)]
    column = lax.rem(lax.broadcasted_iota(jnp.int32, shape, 1), slots)
    placed = jnp.dot(
        jnp.where(slot == column, 1.0, 0.0).astype(jnp.bfloat16), parts_ref[...],
        preferred_element_type=jnp.float32,
    )
    rows = state_ref[0].astype(jnp.float32) + placed
    scale = lax.rsqrt(jnp.mean(rows * rows, axis=-1, keepdims=True) + 1e-05)
    out_ref[0] = (rows * scale * gain_ref[...]).astype(jnp.bfloat16)


def normed_rows(starts, states, parts, gain):
    count, tokens, width = states.shape
    return pl.pallas_call(
        norm_kernel,
        out_shape=jax.ShapeDtypeStruct(states.shape, jnp.bfloat16),
        grid_spec=pltpu.PrefetchScalarGridSpec(
            num_scalar_prefetch=1,
            grid=(count,),
            in_specs=[
                pl.BlockSpec((1, tokens, width), lambda b, s: (b, 0, 0)),
                pl.BlockSpec(parts.shape, lambda b, s: (0, 0)),
                pl.BlockSpec((1, width), lambda b, s: (0, 0)),
            ],
            out_specs=pl.BlockSpec((1, tokens, width), lambda b, s: (b, 0, 0)),
        ),
        compiler_params=pltpu.CompilerParams(vmem_limit_bytes=48 << 20),
        cost_estimate=pl.CostEstimate(
            flops=count * tokens * width * 200, bytes_accessed=count * tokens * width * 4,
            transcendentals=0,
        ),
        name="normed_rows",
    )(starts, states, parts, gain.reshape(1, width)).reshape(count * tokens, width)


def per_device_general(states, norm_gain, gate_up, cotangent, prompt, step_sizes, insert_at, lengths):
    chips, cores = lax.axis_size("dp"), lax.axis_size("replica")
    chip, core = lax.axis_index("dp"), lax.axis_index("replica")
    half, _, shard_units = gate_up.shape
    units = shard_units // chips
    count = prompt.shape[0]
    tokens = states.shape[1]
    width = half * cores

    unit_slice = lax.dynamic_slice_in_dim(gate_up, chip * units, units, 2)
    weight_pair = lax.all_gather(
        unit_slice.reshape(half, 2 * units), "replica", axis=0, tiled=True
    )

    seq_states, seq_cotan, prompt_start = states[0], cotangent[0], insert_at[0]
    package = jnp.concatenate(
        [
            lax.dynamic_slice_in_dim(seq_states, prompt_start, count, 0),
            lax.dynamic_slice_in_dim(seq_cotan, prompt_start, count, 0),
            jnp.broadcast_to(insert_at.astype(jnp.bfloat16).reshape(1, 1), (count, 128)),
        ],
        axis=1,
    )
    package = lax.all_gather(package, "dp", axis=0, tiled=False)
    prompt_base = package[:, :, :width].astype(jnp.float32)
    prompt_cotan = (
        lax.dynamic_slice_in_dim(package, width + chip * units, units, 2)
        .reshape(chips * count, units)
        .astype(jnp.float32)
    )

    swap = [(i, (i + 1) % cores) for i in range(cores)]
    own_starts = package[:, 0, package.shape[2] - 1].astype(jnp.int32)
    seq_states, seq_cotan, _ = lax.optimization_barrier((seq_states, seq_cotan, weight_pair))
    own_states = lax.all_gather(seq_states, "dp", axis=0, tiled=False)
    other_starts = lax.ppermute(own_starts, "replica", swap)
    positions = lax.broadcasted_iota(jnp.int32, (tokens, 1), 0)
    live_cotan = jnp.where(positions < lengths[0], seq_cotan, jnp.zeros_like(seq_cotan))

    def shifted_perm(k):
        return [(i, (i + k) % chips) for i in range(chips)]

    cotan_blocks = []
    for k in range(chips):
        block = lax.dynamic_slice_in_dim(live_cotan, lax.rem(chip + k, chips) * units, units, 1)
        cotan_blocks.append(lax.ppermute(block, "dp", shifted_perm(k)) if k else block)
    stacked = jnp.stack(cotan_blocks)
    token_cotan = jnp.concatenate(
        [
            lax.dynamic_index_in_dim(stacked, lax.rem(chip - j + chips, chips), 0, keepdims=False)
            for j in range(chips)
        ],
        axis=0,
    )

    adversary = prompt.astype(jnp.float32)
    for attack_step in range(step_sizes.shape[0]):
        shifted = prompt_base + adversary[None]
        inverse_rms = row_scale(shifted)
        normalized = (shifted * inverse_rms * norm_gain).astype(jnp.bfloat16)
        unit_grads = hidden_grads(normalized.reshape(chips * count, width), weight_pair, prompt_cotan)
        feature_grad = lax.dot_general(
            unit_grads, weight_pair, (((1,), (1,)), ((), ())), preferred_element_type=jnp.float32
        ).reshape(chips, count, width)
        scaled = norm_gain * feature_grad
        feature_mean = jnp.mean(shifted * scaled, axis=-1, keepdims=True)
        partial = jnp.sum(
            inverse_rms * scaled - shifted * (inverse_rms * inverse_rms * inverse_rms) * feature_mean,
            axis=0,
        )
        adversary = apply_step(partial, adversary, step_sizes[attack_step : attack_step + 1])
        if attack_step == step_sizes.shape[0] - 2:
            own_states, adversary = lax.optimization_barrier((own_states, adversary))
            other_states = lax.ppermute(own_states, "replica", swap)

    high = lax.reduce_precision(adversary, 8, 7)
    middle = lax.reduce_precision(adversary - high, 8, 7)
    low = adversary - high - middle
    parts = jnp.concatenate([high, middle, low], axis=0).astype(jnp.bfloat16)
    own_normed = normed_rows(own_starts, own_states, parts, norm_gain)
    own_grads = hidden_grads(own_normed, weight_pair, token_cotan.astype(jnp.float32))
    other_grads = lax.ppermute(own_grads, "replica", swap)
    other_normed = normed_rows(other_starts, other_states, parts, norm_gain)

    block_width = width // (chips * cores)
    dims = (((0,), (0,)), ((), ()))
    squares = 0.0
    received = [None] * chips
    for k in [2 % chips, *[i for i in range(1, chips) if i != 2 % chips], 0] if chips > 2 else range(chips):
        start = (lax.rem(chip + k, chips) * cores + core) * block_width
        block = lax.dot_general(
            lax.dynamic_slice_in_dim(own_normed, start, block_width, 1), own_grads, dims,
            preferred_element_type=jnp.float32,
        ) + lax.dot_general(
            lax.dynamic_slice_in_dim(other_normed, start, block_width, 1), other_grads, dims,
            preferred_element_type=jnp.float32,
        )
        squares = squares + jnp.sum(block * block)
        sent = block.astype(jnp.bfloat16)
        received[k] = lax.ppermute(sent, "dp", shifted_perm(k)) if k else sent
    squares = sum_everywhere(squares)
    scale = lax.rsqrt(squares / (2 * D * FF) + 1e-06)
    stacked = jnp.stack(received)
    pieces = [
        lax.dynamic_index_in_dim(stacked, lax.rem(chip - j + chips, chips), 0, keepdims=False)
        for j in range(chips)
    ]
    weight_step = jnp.concatenate(
        [piece.reshape(block_width, 2, units) for piece in pieces], axis=2
    )
    weight_step = (weight_step.astype(jnp.float32) * scale).astype(jnp.bfloat16)
    column_count = width // lax.axis_size("tensor")
    prompt_final = lax.dynamic_slice_in_dim(
        adversary, lax.axis_index("tensor") * column_count, column_count, 1
    )
    return (prompt_final, weight_step)


def relative_devices(chip, core):
    pairs = []
    for m in range(4):
        other_chip = [chip, chip + 1 - 2 * lax.rem(chip, 2), lax.rem(chip + 2, 4), 3 - chip][m]
        for q in range(2):
            pairs.append((other_chip, core if q == 0 else 1 - core))
    return pairs


def main_kernel(
    tensors, steps,
    pair, normed, cot_ref, prompt_in, base_rows, rows_1, rows_2, rows_3, base_cot, gain_ref, step_ref,
    adv_out, xp_out, g_all, x_all, gp_all,
    rows_v, w_buf, keep_v, send_v, got_v, g_v,
    base_buf, cot_buf, near_v, far_v, x_v, fg_v, inv_v, adv, part,
    send_a, send_b, recv_s, recv_a, recv_b, recv_c, gp_v,
    s_local, s_w, s_r, r_r, s_f, r_f, s_g, r_g, s_p, r_p, s_c, r_c, s_x, r_x, s_z, r_z,
    s_0, r_0, s_1, r_1, s_2, r_2, s_3, r_3, s_o, r_o,
):
    t = lax.axis_index("tensor")
    chip = lax.axis_index("dp")
    core = lax.axis_index("replica")
    me = chip * 2 + core
    lead = core == 0
    rel = relative_devices(chip, core)
    ids = [{"dp": a, "replica": b} for a, b in rel]
    place = [a * 2 + b for a, b in rel]
    wide = near_v.shape[2]
    half = pair.shape[1]
    units = pair.shape[2] // 4
    count, width = base_rows.shape
    block = width // 8
    base = normed.shape[0]

    def remote(src, dst, send, recv, device):
        return pltpu.make_async_remote_copy(
            src_ref=src, dst_ref=dst, send_sem=send, recv_sem=recv,
            device_id=device, device_id_type=MESH,
        )

    def w_copy(i):
        return pltpu.make_async_copy(pair.at[:, :, pl.ds(i * units, units)], w_buf.at[i % 2], s_w.at[i % 2])

    w_copies = [w_copy(0), w_copy(1)]
    for copy in w_copies:
        copy.start()
    near_half = pl.ds(pl.multiple_of(core * half, 128), half)
    far_half = pl.ds(pl.multiple_of((1 - core) * half, 128), half)
    rows_local = pltpu.make_async_copy(normed.at[:, near_half], rows_v.at[pl.ds(0, base)], s_local.at[0])
    rows_local.start()

    barrier = pltpu.get_barrier_semaphore()
    line_ids = [{"tensor": lax.rem(t + k, tensors)} for k in range(1, tensors)]
    for device in ids[1:] + line_ids:
        pl.semaphore_signal(barrier, inc=1, device_id=device, device_id_type=MESH)
    pl.semaphore_wait(barrier, 7 + tensors - 1)

    rows_far = remote(normed.at[:, far_half], rows_v.at[pl.ds(base, base)], s_r.at[0], r_r.at[0], ids[1])
    rows_far.start()
    rows_a = [
        pltpu.make_async_copy(source, base_buf.at[place[2 * m]], s_p.at[m])
        for m, source in ((1, rows_1), (2, rows_2), (3, rows_3))
    ]

    def first_unit(a, b):
        return pl.multiple_of(a * units + b * (units - wide), 128)

    cots = [None] + [
        remote(
            base_cot.at[:, pl.ds(first_unit(*rel[j]), wide)], cot_buf.at[me], s_c.at[j], r_c.at[j], ids[j]
        )
        for j in range(1, 8)
    ]
    w_far = remote(pair.at[:, :, pl.ds(first_unit(chip, 1 - core), wide)], far_v, s_r.at[1], r_r.at[1], ids[1])
    local = [
        pltpu.make_async_copy(base_rows, base_buf.at[me], s_local.at[1]),
        pltpu.make_async_copy(base_cot.at[:, pl.ds(first_unit(chip, core), wide)], cot_buf.at[me], s_local.at[2]),
        pltpu.make_async_copy(pair.at[:, :, pl.ds(first_unit(chip, core), wide)], near_v, s_local.at[3]),
    ]
    rows_b = [
        remote(base_buf.at[place[2 * m]], base_buf.at[place[2 * m]], s_p.at[4 + m], r_p.at[4 + m], ids[1])
        for m in range(4)
    ]
    quarter = block // tensors
    own_quarter = pl.ds(pl.multiple_of(t * quarter, 128), quarter)
    xs = [None]
    for j in range(1, 8):
        start = pl.multiple_of(place[j] * block, 128)
        if j == 1:
            src, dst = normed.at[:, pl.ds(start, block)], x_all.at[j]
        else:
            src = normed.at[:, pl.ds(pl.multiple_of(start + t * quarter, 128), quarter)]
            dst = x_all.at[j, :, own_quarter]
        xs.append(remote(src, dst, s_x.at[j], r_x.at[j], ids[j]))
    xz = [
        [
            remote(
                x_all.at[j, :, own_quarter], x_all.at[j, :, own_quarter],
                s_z.at[j, k], r_z.at[j, k], line_ids[k],
            )
            for k in range(tensors - 1)
        ]
        for j in range(2, 8)
    ]
    xzs = [copy for line in xz for copy in line]
    mine_block = pl.ds(pl.multiple_of(me * block, 128), block)
    xl = pltpu.make_async_copy(normed.at[:, mine_block], x_all.at[0], s_local.at[9])
    for copy in rows_a + cots[1:] + local + xs[1:] + [xl]:
        copy.start()

    def bulk(src, slot, i, k, device):
        return remote(src, g_all.at[slot, i], s_g.at[k], r_g.at[k], device)

    gx = [[bulk(g_v.at[i] if q == 0 else g_all.at[1, i], 2 + q, i, 4 * q + i, ids[2]) for i in range(4)] for q in range(2)]
    gy = [[bulk(g_v.at[i] if q == 0 else g_all.at[1, i], 4 + q, i, 8 + 4 * q + i, ids[4]) for i in range(4)] for q in range(2)]
    early = [bulk(g_v.at[0], 3, 0, 4, ids[3]), bulk(g_v.at[0], 5, 0, 12, ids[5])]
    gs = [bulk(g_v.at[i], 1, i, 16 + i, ids[1]) for i in range(4)]
    gl = [pltpu.make_async_copy(g_v.at[i], g_all.at[0, i], s_local.at[5 + i]) for i in range(4)]
    fd = [
        [bulk(g_all.at[(2 if i < 2 else 4) + q, i], 6 + q, i, 20 + 4 * q + i, ids[4 if i < 2 else 2]) for i in range(4)]
        for q in range(2)
    ]
    side = [[bulk(g_all.at[n, i], n + 1 - 2 * (n % 2), i, 28 + 4 * (n - 2) + i, ids[1]) for i in range(4)] for n in range(2, 8)]
    swaps = [remote(send_v.at[i % 2], got_v.at[i], s_f.at[i], r_f.at[i], ids[1]) for i in range(4)]

    def combine(i):
        swaps[i].wait_recv()
        gate = keep_v[i % 2, 0] + got_v[i, 0]
        up = keep_v[i % 2, 1] + got_v[i, 1]
        act, slope = silu_parts(gate)
        cot = cot_ref[:, i * units : (i + 1) * units].astype(jnp.float32)
        g_v[i, :, :units] = (cot * up * slope).astype(jnp.bfloat16)
        g_v[i, :, units:] = (cot * act).astype(jnp.bfloat16)
        gs[i].start()
        gl[i].start()

        @pl.when(lead)
        def _():
            gx[0][i].start()
            gy[0][i].start()
            for n in [i - 1] * (i > 0) + [i] * (i == 3):
                gs[n].wait_recv()
                if n:
                    gx[1][n].start()
                    gy[1][n].start()

        if i == 0:
            @pl.when(core == 1)
            def _():
                for copy in early:
                    copy.start()

    rows_local.wait()
    rows_far.wait_recv()
    for i in range(4):
        w_copies[i].wait()
        if i >= 2:
            swaps[i - 2].wait_send()
        for p in range(2):
            product = jnp.dot(rows_v[...], w_buf[i % 2, p], preferred_element_type=jnp.float32)
            keep_v[i % 2, p] = product[:base]
            send_v[i % 2, p] = product[base:]
        swaps[i].start()
        if i < 2:
            w_copies.append(w_copy(i + 2))
            w_copies[-1].start()
        if i == 0:
            local[0].wait()
            rows_b[0].start()
            w_far.start()
        else:
            combine(i - 1)
        if i == 1:
            for j in range(2, 8):
                xs[j].wait_recv()
                for copy in xz[j - 2]:
                    copy.start()
        if i == 2:
            for m in range(1, 4):
                rows_a[m - 1].wait()
                rows_b[m].start()
    adv[...] = prompt_in[...].astype(jnp.float32)
    combine(3)
    for copy in rows_b + cots[1:] + [w_far]:
        copy.wait_recv()
    for copy in local[1:]:
        copy.wait()
    lane = lax.broadcasted_iota(jnp.int32, (count, wide), 1)
    keep = lane >= core * (2 * wide - units)

    def norm_rows():
        def one(b, _):
            shifted = base_buf[b].astype(jnp.float32) + adv[...]
            inverse = lax.rsqrt(jnp.mean(shifted * shifted, axis=-1, keepdims=True) + 1e-05)
            x_v[pl.ds(pl.multiple_of(b * count, count), count)] = (shifted * inverse * gain_ref[...]).astype(jnp.bfloat16)
            inv_v[b] = jnp.broadcast_to(inverse, (count, 128))
            return 0
        lax.fori_loop(0, 8, one, 0)

    def unit_grads():
        near = x_v[:, near_half]
        far = x_v[:, far_half]
        gate, up = [
            jnp.dot(near, near_v[p], preferred_element_type=jnp.float32)
            + jnp.dot(far, far_v[p], preferred_element_type=jnp.float32)
            for p in range(2)
        ]
        act, slope = silu_parts(gate)
        cot = jnp.concatenate(
            [jnp.where(keep, cot_buf[b].astype(jnp.float32), 0.0) for b in range(8)], axis=0
        )
        gp_v[:, pl.ds(0, wide)] = (cot * up * slope).astype(jnp.bfloat16)
        gp_v[:, pl.ds(wide, wide)] = (cot * act).astype(jnp.bfloat16)

    dims = (((1,), (1,)), ((), ()))
    chunk = 512

    def feature_grads():
        for source, start in ((near_v, core * half), (far_v, (1 - core) * half)):
            def one(i, _):
                rows = pl.ds(pl.multiple_of(i * chunk, chunk), chunk)
                fg_v[:, pl.ds(pl.multiple_of(start + i * chunk, chunk), chunk)] = lax.dot_general(
                    gp_v[:, pl.ds(0, wide)], source[0, rows], dims, preferred_element_type=jnp.float32
                ) + lax.dot_general(
                    gp_v[:, pl.ds(wide, wide)], source[1, rows], dims, preferred_element_type=jnp.float32
                )
                return 0
            lax.fori_loop(0, half // chunk, one, 0)

    def row_grads():
        part[...] = jnp.zeros_like(part)
        def one(b, _):
            shifted = base_buf[b].astype(jnp.float32) + adv[...]
            scaled = gain_ref[...] * fg_v[pl.ds(pl.multiple_of(b * count, count), count)]
            inverse = inv_v[b][:, :1]
            middle = jnp.mean(shifted * scaled, axis=-1, keepdims=True)
            part[...] += inverse * scaled - shifted * (inverse * inverse * inverse * middle)
            return 0
        lax.fori_loop(0, 8, one, 0)

    lead_waits, other_waits = [], []

    def exchange(k):
        for a in range(4):
            send_a[k, a] = part[:, 2 * a * block : 2 * (a + 1) * block].astype(jnp.bfloat16)
        sib = remote(send_a.at[k], recv_s.at[k], s_0.at[k], r_0.at[k], ids[1])
        first = [
            remote(send_b.at[k, rel[2 * m][0]], recv_a.at[k, m], s_1.at[k, m], r_1.at[k, m], ids[2 * m])
            for m in range(1, 4)
        ]
        second = [
            remote(recv_b.at[k, t], recv_b.at[k, t], s_2.at[k, j], r_2.at[k, j], line_ids[j])
            for j in range(tensors - 1)
        ]
        third = [
            remote(recv_c.at[k, chip], recv_c.at[k, chip], s_3.at[k, m], r_3.at[k, m], ids[2 * m])
            for m in range(1, 4)
        ]
        fourth = [
            remote(
                recv_c.at[k, rel[2 * m][0]], recv_c.at[k, rel[2 * m][0]],
                s_3.at[k, 4 + m], r_3.at[k, 4 + m], ids[1],
            )
            for m in range(4)
        ]

        @pl.when(lead)
        def _():
            sib.start()
            for copy in fourth:
                copy.wait_recv()

        @pl.when(core == 1)
        def _():
            sib.wait_recv()
            for a in range(4):
                send_b[k, a] = (
                    send_a[k, a].astype(jnp.float32) + recv_s[k, a].astype(jnp.float32)
                ).astype(jnp.bfloat16)
            for copy in first:
                copy.start()
            total = send_b[k, chip].astype(jnp.float32)
            for m in range(1, 4):
                first[m - 1].wait_recv()
                total = total + recv_a[k, m].astype(jnp.float32)
            recv_b[k, t] = total.astype(jnp.bfloat16)
            for copy in second:
                copy.start()
            for copy in second:
                copy.wait_recv()
            total = recv_b[k, 0].astype(jnp.float32)
            for j in range(1, tensors):
                total = total + recv_b[k, j].astype(jnp.float32)
            recv_c[k, chip] = total.astype(jnp.bfloat16)
            for copy in third + fourth[:1]:
                copy.start()
            for m in range(1, 4):
                third[m - 1].wait_recv()
                fourth[m].start()

        lead_waits.append(sib)
        other_waits.extend(first + second + third + fourth)
        square = jnp.zeros((count, 1), jnp.float32)
        for p in range(4):
            piece = recv_c[k, p].astype(jnp.float32)
            square = square + jnp.sum(piece * piece, axis=-1, keepdims=True)
        scale = step_ref[k] * lax.rsqrt(square / width + 1e-06)
        for p in range(4):
            at = slice(2 * p * block, 2 * (p + 1) * block)
            adv[:, at] = adv[:, at] + scale * recv_c[k, p].astype(jnp.float32)

    def pass_on(source, n, i):
        source.wait_recv()
        if n < 6 and (n < 4) == (i < 2):
            fd[n % 2][i].start()
        side[n - 2][i].start()

    def forward_some(pieces):
        @pl.when(lead)
        def _():
            for n, i in pieces:
                pass_on((gx, gy)[n // 2 - 1][n % 2][i], n, i)

    stages = [[], [(2, 0), (2, 1), (3, 0), (3, 1)], [(4, 2), (5, 2), (4, 3)], [(5, 3)]]
    rest = [(2, 2), (2, 3), (3, 2), (3, 3), (4, 0), (4, 1), (5, 0), (5, 1)]
    for k in range(steps):
        norm_rows()
        unit_grads()
        feature_grads()
        row_grads()
        exchange(k)
        if k + 1 < len(stages):
            forward_some(stages[k + 1])
    for k in range(steps, 3):
        forward_some(stages[k + 1])
    adv_out[...] = adv[...]
    norm_rows()
    unit_grads()
    xp_out[...] = x_v[:, mine_block]
    mid = 4 * count
    parts = [pl.ds(0, mid), pl.ds(mid, mid)]

    def hop(src, slot, h, k, device):
        source = gp_all.at[slot] if src is None else src
        return remote(source.at[parts[h]], gp_all.at[slot, parts[h]], s_o.at[k], r_o.at[k], device)

    os = remote(gp_v, gp_all.at[me], s_o.at[4], r_o.at[4], ids[1])
    ol = pltpu.make_async_copy(gp_v, gp_all.at[me], s_local.at[4])
    os.start()
    ol.start()
    ox = [[hop(gp_v if q == 0 else None, place[q], h, (0, 5)[q] + h, ids[2]) for h in range(2)] for q in range(2)]
    oy = [[hop(gp_v if q == 0 else None, place[q], h, (2, 7)[q] + h, ids[4]) for h in range(2)] for q in range(2)]
    od = [[hop(None, place[2 + q], 0, 9 + q, ids[4]) for q in range(2)], [hop(None, place[4 + q], 1, 11 + q, ids[2]) for q in range(2)]]
    back = [[hop(None, place[n], h, 13 + 2 * (n - 2) + h, ids[1]) for h in range(2)] for n in range(2, 8)]
    backs = [copy for two in back for copy in two]

    @pl.when(core == 1)
    def _():
        for copy in (ox[0][0], oy[0][1], ox[0][1], oy[0][0]):
            copy.start()
        os.wait_recv()
        for copy in (ox[1][0], oy[1][1], ox[1][1], oy[1][0]):
            copy.start()
        for q in range(2):
            ox[q][0].wait_recv()
            od[0][q].start()
            back[q][0].start()
            oy[q][1].wait_recv()
            od[1][q].start()
            back[2 + q][1].start()
        for q in range(2):
            ox[q][1].wait_recv()
            back[q][1].start()
            oy[q][0].wait_recv()
            back[2 + q][0].start()
        for q in range(2):
            for h in range(2):
                od[h][q].wait_recv()
                back[4 + q][h].start()
        for copy in gs:
            copy.wait_recv()
        for four in side:
            for copy in four:
                copy.wait_recv()
        for copy in other_waits + early + ox[0] + ox[1] + oy[0] + oy[1] + od[0] + od[1] + backs:
            copy.wait_send()

    @pl.when(lead)
    def _():
        for n, i in rest:
            pass_on((gx, gy)[n // 2 - 1][n % 2][i], n, i)
        for i in range(4):
            for q in range(2):
                pass_on(fd[q][i], 6 + q, i)
        os.wait_recv()
        for copy in backs:
            copy.wait_recv()
        for copy in lead_waits + gx[0] + gx[1][1:] + gy[0] + gy[1][1:] + fd[0] + fd[1]:
            copy.wait_send()
        for four in side:
            for copy in four:
                copy.wait_send()

    for copy in [xs[1]] + xzs:
        copy.wait_recv()
    for copy in gl + [ol, xl]:
        copy.wait()
    for copy in [rows_far, w_far, os] + rows_b + cots[1:] + xs[1:] + xzs + swaps[2:] + gs:
        copy.wait_send()


def main_call(pair, normed, cot, prompt, base_rows, other_rows, base_cot, gain, step_sizes):
    tensors = lax.axis_size("tensor")
    steps = step_sizes.shape[0]
    count, width = base_rows.shape
    half, shard = pair.shape[1:]
    units, wide = shard // 4, 512
    block = width // 8
    base = normed.shape[0]
    bf, f32 = jnp.bfloat16, jnp.float32
    dma = pltpu.SemaphoreType.DMA
    vmem = pl.BlockSpec(memory_space=pltpu.VMEM)
    hbm = pl.BlockSpec(memory_space=pl.ANY)
    return pl.pallas_call(
        functools.partial(main_kernel, tensors, steps),
        out_shape=[
            jax.ShapeDtypeStruct((count, width), f32),
            jax.ShapeDtypeStruct((8 * count, block), bf),
            jax.ShapeDtypeStruct((8, 4, base, 2 * units), bf),
            jax.ShapeDtypeStruct((8, base, block), bf),
            jax.ShapeDtypeStruct((8, 8 * count, 2 * wide), bf),
        ],
        in_specs=[hbm, hbm, vmem, vmem, hbm, hbm, hbm, hbm, hbm, vmem, pl.BlockSpec(memory_space=pltpu.SMEM)],
        out_specs=[vmem, vmem, hbm, hbm, hbm],
        scratch_shapes=[
            pltpu.VMEM((2 * base, half), bf),
            pltpu.VMEM((2, 2, half, units), bf),
            pltpu.VMEM((2, 2, base, units), f32),
            pltpu.VMEM((2, 2, base, units), f32),
            pltpu.VMEM((4, 2, base, units), f32),
            pltpu.VMEM((4, base, 2 * units), bf),
            pltpu.VMEM((8, count, width), bf),
            pltpu.VMEM((8, count, wide), bf),
            pltpu.VMEM((2, half, wide), bf),
            pltpu.VMEM((2, half, wide), bf),
            pltpu.VMEM((8 * count, width), bf),
            pltpu.VMEM((8 * count, width), f32),
            pltpu.VMEM((8, count, 128), f32),
            pltpu.VMEM((count, width), f32),
            pltpu.VMEM((count, width), f32),
            pltpu.VMEM((steps, 4, count, 2 * block), bf),
            pltpu.VMEM((steps, 4, count, 2 * block), bf),
            pltpu.VMEM((steps, 4, count, 2 * block), bf),
            pltpu.VMEM((steps, 4, count, 2 * block), bf),
            pltpu.VMEM((steps, tensors, count, 2 * block), bf),
            pltpu.VMEM((steps, 4, count, 2 * block), bf),
            pltpu.VMEM((8 * count, 2 * wide), bf),
        ]
        + [dma((10,))] + [dma((2,))] * 3 + [dma((4,))] * 2 + [dma((52,))] * 2 + [dma((8,))] * 6 + [dma((8, tensors))] * 2
        + [dma((steps,))] * 2 + [dma((steps, 4))] * 2 + [dma((steps, tensors))] * 2
        + [dma((steps, 8))] * 2 + [dma((25,))] * 2,
        compiler_params=pltpu.CompilerParams(
            collective_id=2, has_side_effects=True, vmem_limit_bytes=62 << 20
        ),
        cost_estimate=pl.CostEstimate(flops=100_000_000_000, bytes_accessed=100_000_000, transcendentals=0),
        name="attack_and_gather",
    )(pair, normed, cot, prompt, base_rows, *other_rows, base_cot, gain.reshape(1, width), step_sizes)


def grad_kernel(
    tensors, x_ref, xp_ref, g_ref, gp0_ref, gp1_ref, out_ref, total_ref,
    xt_v, xpt_v, sq_v, mine, buf1, buf2, send1, recv1, send2, recv2,
):
    step = pl.program_id(0) * pl.num_programs(1) + pl.program_id(1)
    t = lax.axis_index("tensor")
    plane_ids = [
        {"dp": a, "replica": b} for a, b in relative_devices(lax.axis_index("dp"), lax.axis_index("replica"))[1:]
    ]
    line_ids = [{"tensor": lax.rem(t + k, tensors)} for k in range(1, tensors)]
    barrier = pltpu.get_barrier_semaphore()

    @pl.when(step == 0)
    def _():
        for device in plane_ids + line_ids:
            pl.semaphore_signal(barrier, inc=1, device_id=device, device_id_type=MESH)
        xt_v[...] = x_ref[...].T
        xpt_v[...] = xp_ref[...].T
        sq_v[...] = jnp.zeros_like(sq_v)

    extra = 2 * gp0_ref.shape[2] - out_ref.shape[2]
    rows = g_ref.shape[0] * g_ref.shape[2]
    gp = jnp.concatenate([gp0_ref[0], gp1_ref[0][:, extra:]], axis=1)
    block = jnp.dot(
        xt_v[...], g_ref[...].reshape(rows, g_ref.shape[3]), preferred_element_type=jnp.float32
    ) + jnp.dot(xpt_v[...], gp, preferred_element_type=jnp.float32)
    out_ref[0] = block
    sq_v[...] += jnp.sum((block * block).reshape(-1, 8, block.shape[1]), axis=0)

    @pl.when(step == pl.num_programs(0) * pl.num_programs(1) - 1)
    def _():
        pl.semaphore_wait(barrier, 7 + tensors - 1)
        total = jnp.full((8, 128), jnp.sum(sq_v[...]), jnp.float32)
        copies = []
        for n, (ids, buf, sends, recvs) in enumerate(((plane_ids, buf1, send1, recv1), (line_ids, buf2, send2, recv2))):
            mine[n] = total
            stage = [
                pltpu.make_async_remote_copy(
                    src_ref=mine.at[n], dst_ref=buf.at[k], send_sem=sends.at[k], recv_sem=recvs.at[k],
                    device_id=device, device_id_type=MESH,
                )
                for k, device in enumerate(ids)
            ]
            for copy in stage:
                copy.start()
            for k, copy in enumerate(stage):
                copy.wait_recv()
                total = total + buf[k]
            copies += stage
        total_ref[...] = total
        for copy in copies:
            copy.wait_send()


def grad_call(x_all, xp, g_all, gp_all):
    eight, _, own_base, pair_units = g_all.shape
    cols = 4 * pair_units
    block = x_all.shape[2]
    wide = gp_all.shape[2] // 2
    shard = cols // 2
    units = shard // 4
    prompts = xp.shape[0]
    f32 = jnp.float32
    tensors = lax.axis_size("tensor")
    dma = pltpu.SemaphoreType.DMA
    return pl.pallas_call(
        functools.partial(grad_kernel, tensors),
        out_shape=[
            jax.ShapeDtypeStruct((2, block, shard), f32),
            jax.ShapeDtypeStruct((8, 128), f32),
        ],
        grid=(2, 4),
        in_specs=[
            pl.BlockSpec((eight * own_base, block), lambda p, j: (0, 0)),
            pl.BlockSpec((prompts, block), lambda p, j: (0, 0)),
            pl.BlockSpec((eight, 1, own_base, units), lambda p, j: (0, j, 0, p)),
            pl.BlockSpec((1, prompts, wide), lambda p, j: (2 * j, 0, p)),
            pl.BlockSpec((1, prompts, wide), lambda p, j: (2 * j + 1, 0, p)),
        ],
        out_specs=[
            pl.BlockSpec((1, block, units), lambda p, j: (p, 0, j)),
            pl.BlockSpec((8, 128), lambda p, j: (0, 0)),
        ],
        scratch_shapes=[
            pltpu.VMEM((block, eight * own_base), jnp.bfloat16),
            pltpu.VMEM((block, prompts), jnp.bfloat16),
            pltpu.VMEM((8, units), f32),
            pltpu.VMEM((2, 8, 128), f32),
            pltpu.VMEM((7, 8, 128), f32),
            pltpu.VMEM((tensors - 1, 8, 128), f32),
        ]
        + [dma((7,))] * 2 + [dma((tensors - 1,))] * 2,
        compiler_params=pltpu.CompilerParams(
            collective_id=3, has_side_effects=True, vmem_limit_bytes=60 << 20
        ),
        cost_estimate=pl.CostEstimate(
            flops=2 * block * cols * (eight * own_base + prompts), bytes_accessed=50_000_000, transcendentals=0
        ),
        name="weight_grad",
    )(x_all.reshape(eight * own_base, block), xp, g_all, gp_all, gp_all)


def result_kernel(total_ref, grad_ref, out_ref):
    _, rows, cols = grad_ref.shape
    scale = lax.rsqrt(total_ref[:1, :1] / (2 * D * FF) + 1e-06)
    n = 128
    to = lax.broadcasted_iota(jnp.int32, (2 * n, 2 * n), 0)
    source = jnp.where(lax.rem(to, 2) == 0, to // 2, n + to // 2)
    order = jnp.where(lax.broadcasted_iota(jnp.int32, (2 * n, 2 * n), 1) == source, 1.0, 0.0).astype(jnp.bfloat16)
    for r in range(0, rows, n):
        both = jnp.concatenate(
            [(grad_ref[p, r : r + n] * scale).astype(jnp.bfloat16) for p in range(2)], axis=0
        )
        mixed = jnp.dot(order, both, preferred_element_type=jnp.float32).astype(jnp.bfloat16)
        out_ref[r : r + n] = mixed.reshape(n, 2, cols)


def result_call(total, weight_grad):
    _, rows, shard = weight_grad.shape
    cols = 512
    return pl.pallas_call(
        result_kernel,
        out_shape=jax.ShapeDtypeStruct((rows, 2, shard), jnp.bfloat16),
        grid=(shard // cols,),
        in_specs=[
            pl.BlockSpec(total.shape, lambda j: (0, 0)),
            pl.BlockSpec((2, rows, cols), lambda j: (0, 0, j)),
        ],
        out_specs=pl.BlockSpec((rows, 2, cols), lambda j: (0, 0, j)),
        compiler_params=pltpu.CompilerParams(vmem_limit_bytes=48 << 20),
        name="scaled_result",
    )(total, weight_grad)


def per_device(states, norm_gain, gate_up, cotangent, prompt, step_sizes, insert_at, lengths):
    chips, cores = lax.axis_size("dp"), lax.axis_size("replica")
    shard = gate_up.shape[2]
    count = prompt.shape[0]
    fits = (
        chips == 4 and cores == 2 and 1 < lax.axis_size("tensor") <= 8 and states.shape[2] % (1024 * lax.axis_size("tensor")) == 0 and states.shape[0] == 1 and shard % (chips * 128) == 0
        and shard // chips > 512 and shard // chips <= 1024 and shard % 512 == 0
        and gate_up.shape[0] % 1024 == 0 and count % 16 == 0 and (states.shape[1] - count) % 16 == 0
    )
    if not fits:
        return per_device_general(
            states, norm_gain, gate_up, cotangent, prompt, step_sizes, insert_at, lengths
        )
    chip, core = lax.axis_index("dp"), lax.axis_index("replica")
    half = gate_up.shape[0]
    width = half * cores
    tokens = states.shape[1]
    base = tokens - count
    units = shard // chips
    start = insert_at[0]

    pair = jnp.transpose(gate_up, (1, 0, 2))

    spot = lax.broadcasted_iota(jnp.int32, (base, 1), 0)
    ahead = spot < start
    position = jnp.where(ahead, spot, spot + count)
    rows = jnp.where(ahead, states[0, :base], states[0, count:]).astype(jnp.float32)
    cot = jnp.where(ahead, cotangent[0, :base], cotangent[0, count:])
    cot = jnp.where(position < lengths[0], cot, jnp.zeros_like(cot))
    normed = (rows * row_scale(rows) * norm_gain).astype(jnp.bfloat16)
    base_rows = lax.dynamic_slice_in_dim(states[0], start, count, 0)
    base_cot = lax.dynamic_slice_in_dim(cotangent[0], start, count, 0)
    other_rows = [lax.ppermute(base_rows, "dp", [(i, i ^ m) for i in range(4)]) for m in range(1, 4)]

    adversary, xp, g_all, x_all, gp_all = main_call(
        pair, normed, cot, prompt, base_rows, other_rows, base_cot, norm_gain, step_sizes
    )
    weight_grad, total = grad_call(x_all, xp, g_all, gp_all)
    weight_step = result_call(total, weight_grad)
    column_count = width // lax.axis_size("tensor")
    prompt_final = lax.dynamic_slice_in_dim(
        adversary, lax.axis_index("tensor") * column_count, column_count, 1
    )
    return (prompt_final, weight_step)


def solution(mesh):
    return jax.shard_map(
        per_device,
        mesh=mesh,
        in_specs=(
            P(("dp", "replica"), None, None),
            P(),
            P("replica", None, "tensor"),
            P(("dp", "replica"), None, "tensor"),
            P(),
            P(),
            P(("dp", "replica")),
            P(("dp", "replica")),
        ),
        out_specs=(P(None, "tensor"), P(("dp", "replica"), None, "tensor")),
        check_vma=False,
    )
```

```python
import functools

import jax
import jax.numpy as jnp
from jax import lax
from jax.experimental import pallas as pl
from jax.experimental.pallas import tpu as pltpu
from jax.sharding import PartitionSpec as P

D = 4096
FF = 14336
MESH = pl.DeviceIdType.MESH


def row_scale(feature_rows):
    return lax.rsqrt(jnp.mean(feature_rows * feature_rows, axis=-1, keepdims=True) + 1e-05)


def silu_parts(gate_values):
    sigmoid_value = jax.nn.sigmoid(gate_values)
    return (
        gate_values * sigmoid_value,
        sigmoid_value * (1.0 + gate_values * (1.0 - sigmoid_value)),
    )


def hidden_grads(normalized, weight_pair, cotan_rows):
    unit_count = weight_pair.shape[1] // 2
    projected = jnp.dot(normalized, weight_pair, preferred_element_type=jnp.float32)
    activated, derivative = silu_parts(projected[:, :unit_count])
    up_part = projected[:, unit_count:]
    return jnp.concatenate(
        [cotan_rows * up_part * derivative, cotan_rows * activated], axis=1
    ).astype(jnp.bfloat16)


def step_kernel(
    tensors, chips, cores, partial_ref, adversary_ref, step_ref, out_ref,
    plane_buf, line_buf, mine, send1, recv1, send2, recv2, send3, recv3, send4, recv4,
):
    group = chips * cores
    t = lax.axis_index("tensor")
    g = lax.axis_index("dp") * cores + lax.axis_index("replica")
    rows = partial_ref.shape[0] // group
    own = rows // tensors
    plane = [lax.rem(g + k, group) for k in range(1, group)]
    line = [lax.rem(t + k, tensors) for k in range(1, tensors)]
    plane_ids = [{"dp": p // cores, "replica": lax.rem(p, cores)} for p in plane]
    line_ids = [{"tensor": p} for p in line]

    barrier = pltpu.get_barrier_semaphore()
    for device in plane_ids + line_ids:
        pl.semaphore_signal(barrier, inc=1, device_id=device, device_id_type=MESH)
    pl.semaphore_wait(barrier, group + tensors - 2)

    def exchange(pairs, ids, sends, recvs):
        copies = []
        for k, ((source, target), device) in enumerate(zip(pairs, ids)):
            copy = pltpu.make_async_remote_copy(
                src_ref=source, dst_ref=target, send_sem=sends.at[k], recv_sem=recvs.at[k],
                device_id=device, device_id_type=MESH,
            )
            copy.start()
            copies.append(copy)
        return copies

    first = exchange(
        [(partial_ref.at[pl.ds(p * rows, rows)], plane_buf.at[k]) for k, p in enumerate(plane)],
        plane_ids, send1, recv1,
    )
    total = partial_ref[pl.ds(g * rows, rows)]
    for k, copy in enumerate(first):
        copy.wait_recv()
        total = total + plane_buf[k]
    mine[...] = total
    second = exchange(
        [(mine.at[pl.ds(p * own, own)], line_buf.at[k]) for k, p in enumerate(line)],
        line_ids, send2, recv2,
    )
    grad = mine[pl.ds(t * own, own)]
    for k, copy in enumerate(second):
        copy.wait_recv()
        grad = grad + line_buf[k]
    square = jnp.sum(jnp.sum(grad * grad, axis=2, keepdims=True), axis=1, keepdims=True)
    count = partial_ref.shape[1] * partial_ref.shape[2]
    row = g * rows + t * own
    block = pl.ds(row, own)
    out_ref[block] = adversary_ref[block] + step_ref[0] * grad * lax.rsqrt(square / count + 1e-06)
    third = exchange([(out_ref.at[block], out_ref.at[block])] * len(line), line_ids, send3, recv3)
    for copy in third:
        copy.wait_recv()
    wide = pl.ds(g * rows, rows)
    fourth = exchange([(out_ref.at[wide], out_ref.at[wide])] * len(plane), plane_ids, send4, recv4)
    for copy in fourth:
        copy.wait_recv()
    for copy in first + second + third + fourth:
        copy.wait_send()


def apply_step(partial, adversary, step_size):
    tensors, chips, cores = (lax.axis_size(a) for a in ("tensor", "dp", "replica"))
    group = chips * cores
    count, width = partial.shape
    if count % (group * tensors) == 0 and width % 1024 == 0:
        shape = (count, 8, width // 8)
        rows = count // group
        own = rows // tensors
        dma = pltpu.SemaphoreType.DMA
        vmem = pl.BlockSpec(memory_space=pltpu.VMEM)
        result = pl.pallas_call(
            functools.partial(step_kernel, tensors, chips, cores),
            out_shape=jax.ShapeDtypeStruct(shape, jnp.float32),
            in_specs=[vmem, vmem, pl.BlockSpec(memory_space=pltpu.SMEM)],
            out_specs=vmem,
            scratch_shapes=[
                pltpu.VMEM((group - 1, rows) + shape[1:], jnp.float32),
                pltpu.VMEM((tensors - 1, own) + shape[1:], jnp.float32),
                pltpu.VMEM((rows,) + shape[1:], jnp.float32),
            ]
            + [dma((group - 1,))] * 2 + [dma((tensors - 1,))] * 4 + [dma((group - 1,))] * 2,
            compiler_params=pltpu.CompilerParams(
                collective_id=0, has_side_effects=True, vmem_limit_bytes=16 << 20
            ),
            cost_estimate=pl.CostEstimate(
                flops=20_000_000_000, bytes_accessed=3 * count * width * 4, transcendentals=0
            ),
            name="attack_step",
        )(partial.reshape(shape), adversary.reshape(shape), step_size)
        return result.reshape(count, width)
    grad = lax.psum(partial, ("tensor", "dp", "replica"))
    scale = lax.rsqrt(jnp.mean(grad * grad, axis=-1, keepdims=True) + 1e-06)
    return adversary + step_size[0] * grad * scale


def scalar_kernel(tensors, chips, cores, value_ref, out_ref, buf1, buf2, mine, send1, recv1, send2, recv2):
    group = chips * cores
    t = lax.axis_index("tensor")
    g = lax.axis_index("dp") * cores + lax.axis_index("replica")
    plane = [lax.rem(g + k, group) for k in range(1, group)]
    plane_ids = [{"dp": p // cores, "replica": lax.rem(p, cores)} for p in plane]
    line_ids = [{"tensor": lax.rem(t + k, tensors)} for k in range(1, tensors)]
    barrier = pltpu.get_barrier_semaphore()
    for device in plane_ids + line_ids:
        pl.semaphore_signal(barrier, inc=1, device_id=device, device_id_type=MESH)
    pl.semaphore_wait(barrier, group + tensors - 2)
    copies = []
    total = value_ref[...]
    source = value_ref
    for ids, buf, sends, recvs in ((plane_ids, buf1, send1, recv1), (line_ids, buf2, send2, recv2)):
        stage = []
        for k, device in enumerate(ids):
            copy = pltpu.make_async_remote_copy(
                src_ref=source, dst_ref=buf.at[k], send_sem=sends.at[k], recv_sem=recvs.at[k],
                device_id=device, device_id_type=MESH,
            )
            copy.start()
            stage.append(copy)
        for k, copy in enumerate(stage):
            copy.wait_recv()
            total = total + buf[k]
        copies += stage
        if buf is buf1:
            mine[...] = total
            source = mine
    out_ref[...] = total
    for copy in copies:
        copy.wait_send()


def sum_everywhere(value):
    tensors, chips, cores = (lax.axis_size(a) for a in ("tensor", "dp", "replica"))
    group = chips * cores
    if not 1 < tensors <= 8 or not 1 < group <= 16:
        return lax.psum(value, ("tensor", "dp", "replica"))
    dma = pltpu.SemaphoreType.DMA
    vmem = pl.BlockSpec(memory_space=pltpu.VMEM)
    return pl.pallas_call(
        functools.partial(scalar_kernel, tensors, chips, cores),
        out_shape=jax.ShapeDtypeStruct((8, 128), jnp.float32),
        in_specs=[vmem],
        out_specs=vmem,
        scratch_shapes=[
            pltpu.VMEM((group - 1, 8, 128), jnp.float32),
            pltpu.VMEM((tensors - 1, 8, 128), jnp.float32),
            pltpu.VMEM((8, 128), jnp.float32),
        ]
        + [dma((group - 1,))] * 2 + [dma((tensors - 1,))] * 2,
        compiler_params=pltpu.CompilerParams(
            collective_id=1, has_side_effects=True, vmem_limit_bytes=4 << 20
        ),
        name="scalar_sum",
    )(jnp.full((8, 128), value, jnp.float32))[0, 0]


def norm_kernel(start_ref, state_ref, parts_ref, gain_ref, out_ref):
    slots = parts_ref.shape[0] // 3
    tokens = state_ref.shape[1]
    shape = (tokens, 3 * slots)
    slot = lax.broadcasted_iota(jnp.int32, shape, 0) - start_ref[pl.program_id(0)]
    column = lax.rem(lax.broadcasted_iota(jnp.int32, shape, 1), slots)
    placed = jnp.dot(
        jnp.where(slot == column, 1.0, 0.0).astype(jnp.bfloat16), parts_ref[...],
        preferred_element_type=jnp.float32,
    )
    rows = state_ref[0].astype(jnp.float32) + placed
    scale = lax.rsqrt(jnp.mean(rows * rows, axis=-1, keepdims=True) + 1e-05)
    out_ref[0] = (rows * scale * gain_ref[...]).astype(jnp.bfloat16)


def normed_rows(starts, states, parts, gain):
    count, tokens, width = states.shape
    return pl.pallas_call(
        norm_kernel,
        out_shape=jax.ShapeDtypeStruct(states.shape, jnp.bfloat16),
        grid_spec=pltpu.PrefetchScalarGridSpec(
            num_scalar_prefetch=1,
            grid=(count,),
            in_specs=[
                pl.BlockSpec((1, tokens, width), lambda b, s: (b, 0, 0)),
                pl.BlockSpec(parts.shape, lambda b, s: (0, 0)),
                pl.BlockSpec((1, width), lambda b, s: (0, 0)),
            ],
            out_specs=pl.BlockSpec((1, tokens, width), lambda b, s: (b, 0, 0)),
        ),
        compiler_params=pltpu.CompilerParams(vmem_limit_bytes=48 << 20),
        cost_estimate=pl.CostEstimate(
            flops=count * tokens * width * 200, bytes_accessed=count * tokens * width * 4,
            transcendentals=0,
        ),
        name="normed_rows",
    )(starts, states, parts, gain.reshape(1, width)).reshape(count * tokens, width)


def per_device_general(states, norm_gain, gate_up, cotangent, prompt, step_sizes, insert_at, lengths):
    chips, cores = lax.axis_size("dp"), lax.axis_size("replica")
    chip, core = lax.axis_index("dp"), lax.axis_index("replica")
    half, _, shard_units = gate_up.shape
    units = shard_units // chips
    count = prompt.shape[0]
    tokens = states.shape[1]
    width = half * cores

    unit_slice = lax.dynamic_slice_in_dim(gate_up, chip * units, units, 2)
    weight_pair = lax.all_gather(
        unit_slice.reshape(half, 2 * units), "replica", axis=0, tiled=True
    )

    seq_states, seq_cotan, prompt_start = states[0], cotangent[0], insert_at[0]
    package = jnp.concatenate(
        [
            lax.dynamic_slice_in_dim(seq_states, prompt_start, count, 0),
            lax.dynamic_slice_in_dim(seq_cotan, prompt_start, count, 0),
            jnp.broadcast_to(insert_at.astype(jnp.bfloat16).reshape(1, 1), (count, 128)),
        ],
        axis=1,
    )
    package = lax.all_gather(package, "dp", axis=0, tiled=False)
    prompt_base = package[:, :, :width].astype(jnp.float32)
    prompt_cotan = (
        lax.dynamic_slice_in_dim(package, width + chip * units, units, 2)
        .reshape(chips * count, units)
        .astype(jnp.float32)
    )

    swap = [(i, (i + 1) % cores) for i in range(cores)]
    own_starts = package[:, 0, package.shape[2] - 1].astype(jnp.int32)
    seq_states, seq_cotan, _ = lax.optimization_barrier((seq_states, seq_cotan, weight_pair))
    own_states = lax.all_gather(seq_states, "dp", axis=0, tiled=False)
    other_starts = lax.ppermute(own_starts, "replica", swap)
    positions = lax.broadcasted_iota(jnp.int32, (tokens, 1), 0)
    live_cotan = jnp.where(positions < lengths[0], seq_cotan, jnp.zeros_like(seq_cotan))

    def shifted_perm(k):
        return [(i, (i + k) % chips) for i in range(chips)]

    cotan_blocks = []
    for k in range(chips):
        block = lax.dynamic_slice_in_dim(live_cotan, lax.rem(chip + k, chips) * units, units, 1)
        cotan_blocks.append(lax.ppermute(block, "dp", shifted_perm(k)) if k else block)
    stacked = jnp.stack(cotan_blocks)
    token_cotan = jnp.concatenate(
        [
            lax.dynamic_index_in_dim(stacked, lax.rem(chip - j + chips, chips), 0, keepdims=False)
            for j in range(chips)
        ],
        axis=0,
    )

    adversary = prompt.astype(jnp.float32)
    for attack_step in range(step_sizes.shape[0]):
        shifted = prompt_base + adversary[None]
        inverse_rms = row_scale(shifted)
        normalized = (shifted * inverse_rms * norm_gain).astype(jnp.bfloat16)
        unit_grads = hidden_grads(normalized.reshape(chips * count, width), weight_pair, prompt_cotan)
        feature_grad = lax.dot_general(
            unit_grads, weight_pair, (((1,), (1,)), ((), ())), preferred_element_type=jnp.float32
        ).reshape(chips, count, width)
        scaled = norm_gain * feature_grad
        feature_mean = jnp.mean(shifted * scaled, axis=-1, keepdims=True)
        partial = jnp.sum(
            inverse_rms * scaled - shifted * (inverse_rms * inverse_rms * inverse_rms) * feature_mean,
            axis=0,
        )
        adversary = apply_step(partial, adversary, step_sizes[attack_step : attack_step + 1])
        if attack_step == step_sizes.shape[0] - 2:
            own_states, adversary = lax.optimization_barrier((own_states, adversary))
            other_states = lax.ppermute(own_states, "replica", swap)

    high = lax.reduce_precision(adversary, 8, 7)
    middle = lax.reduce_precision(adversary - high, 8, 7)
    low = adversary - high - middle
    parts = jnp.concatenate([high, middle, low], axis=0).astype(jnp.bfloat16)
    own_normed = normed_rows(own_starts, own_states, parts, norm_gain)
    own_grads = hidden_grads(own_normed, weight_pair, token_cotan.astype(jnp.float32))
    other_grads = lax.ppermute(own_grads, "replica", swap)
    other_normed = normed_rows(other_starts, other_states, parts, norm_gain)

    block_width = width // (chips * cores)
    dims = (((0,), (0,)), ((), ()))
    squares = 0.0
    received = [None] * chips
    for k in [2 % chips, *[i for i in range(1, chips) if i != 2 % chips], 0] if chips > 2 else range(chips):
        start = (lax.rem(chip + k, chips) * cores + core) * block_width
        block = lax.dot_general(
            lax.dynamic_slice_in_dim(own_normed, start, block_width, 1), own_grads, dims,
            preferred_element_type=jnp.float32,
        ) + lax.dot_general(
            lax.dynamic_slice_in_dim(other_normed, start, block_width, 1), other_grads, dims,
            preferred_element_type=jnp.float32,
        )
        squares = squares + jnp.sum(block * block)
        sent = block.astype(jnp.bfloat16)
        received[k] = lax.ppermute(sent, "dp", shifted_perm(k)) if k else sent
    squares = sum_everywhere(squares)
    scale = lax.rsqrt(squares / (2 * D * FF) + 1e-06)
    stacked = jnp.stack(received)
    pieces = [
        lax.dynamic_index_in_dim(stacked, lax.rem(chip - j + chips, chips), 0, keepdims=False)
        for j in range(chips)
    ]
    weight_step = jnp.concatenate(
        [piece.reshape(block_width, 2, units) for piece in pieces], axis=2
    )
    weight_step = (weight_step.astype(jnp.float32) * scale).astype(jnp.bfloat16)
    column_count = width // lax.axis_size("tensor")
    prompt_final = lax.dynamic_slice_in_dim(
        adversary, lax.axis_index("tensor") * column_count, column_count, 1
    )
    return (prompt_final, weight_step)


def relative_devices(chip, core):
    pairs = []
    for m in range(4):
        other_chip = [chip, chip + 1 - 2 * lax.rem(chip, 2), lax.rem(chip + 2, 4), 3 - chip][m]
        for q in range(2):
            pairs.append((other_chip, core if q == 0 else 1 - core))
    return pairs


def main_kernel(
    tensors, steps,
    pair, normed, cot_ref, prompt_in, base_rows, rows_1, rows_2, rows_3, base_cot, gain_ref, step_ref,
    adv_out, xp_out, g_all, x_all, gp_all,
    rows_v, w_buf, keep_v, send_v, got_v, g_v,
    base_buf, cot_buf, near_v, far_v, x_v, fg_v, inv_v, adv, part,
    send_a, send_b, recv_s, recv_a, recv_b, recv_c, gp_v,
    s_local, s_w, s_r, r_r, s_f, r_f, s_g, r_g, s_p, r_p, s_c, r_c, s_x, r_x, s_z, r_z,
    s_0, r_0, s_1, r_1, s_2, r_2, s_3, r_3, s_o, r_o,
):
    t = lax.axis_index("tensor")
    chip = lax.axis_index("dp")
    core = lax.axis_index("replica")
    me = chip * 2 + core
    lead = core == 0
    rel = relative_devices(chip, core)
    ids = [{"dp": a, "replica": b} for a, b in rel]
    place = [a * 2 + b for a, b in rel]
    wide = near_v.shape[2]
    half = pair.shape[1]
    units = pair.shape[2] // 4
    count, width = base_rows.shape
    block = width // 8
    base = normed.shape[0]

    def remote(src, dst, send, recv, device):
        return pltpu.make_async_remote_copy(
            src_ref=src, dst_ref=dst, send_sem=send, recv_sem=recv,
            device_id=device, device_id_type=MESH,
        )

    def w_copy(i):
        return pltpu.make_async_copy(pair.at[:, :, pl.ds(i * units, units)], w_buf.at[i % 2], s_w.at[i % 2])

    w_copies = [w_copy(0), w_copy(1)]
    for copy in w_copies:
        copy.start()
    near_half = pl.ds(pl.multiple_of(core * half, 128), half)
    far_half = pl.ds(pl.multiple_of((1 - core) * half, 128), half)
    rows_local = pltpu.make_async_copy(normed.at[:, near_half], rows_v.at[pl.ds(0, base)], s_local.at[0])
    rows_local.start()

    barrier = pltpu.get_barrier_semaphore()
    line_ids = [{"tensor": lax.rem(t + k, tensors)} for k in range(1, tensors)]
    for device in ids[1:] + line_ids:
        pl.semaphore_signal(barrier, inc=1, device_id=device, device_id_type=MESH)
    pl.semaphore_wait(barrier, 7 + tensors - 1)

    rows_far = remote(normed.at[:, far_half], rows_v.at[pl.ds(base, base)], s_r.at[0], r_r.at[0], ids[1])
    rows_far.start()
    rows_a = [
        pltpu.make_async_copy(source, base_buf.at[place[2 * m]], s_p.at[m])
        for m, source in ((1, rows_1), (2, rows_2), (3, rows_3))
    ]

    def first_unit(a, b):
        return pl.multiple_of(a * units + b * (units - wide), 128)

    cots = [None] + [
        remote(
            base_cot.at[:, pl.ds(first_unit(*rel[j]), wide)], cot_buf.at[me], s_c.at[j], r_c.at[j], ids[j]
        )
        for j in range(1, 8)
    ]
    w_far = remote(pair.at[:, :, pl.ds(first_unit(chip, 1 - core), wide)], far_v, s_r.at[1], r_r.at[1], ids[1])
    local = [
        pltpu.make_async_copy(base_rows, base_buf.at[me], s_local.at[1]),
        pltpu.make_async_copy(base_cot.at[:, pl.ds(first_unit(chip, core), wide)], cot_buf.at[me], s_local.at[2]),
        pltpu.make_async_copy(pair.at[:, :, pl.ds(first_unit(chip, core), wide)], near_v, s_local.at[3]),
    ]
    rows_b = [
        remote(base_buf.at[place[2 * m]], base_buf.at[place[2 * m]], s_p.at[4 + m], r_p.at[4 + m], ids[1])
        for m in range(4)
    ]
    quarter = block // tensors
    own_quarter = pl.ds(pl.multiple_of(t * quarter, 128), quarter)
    xs = [None]
    for j in range(1, 8):
        start = pl.multiple_of(place[j] * block, 128)
        if j == 1:
            src, dst = normed.at[:, pl.ds(start, block)], x_all.at[j]
        else:
            src = normed.at[:, pl.ds(pl.multiple_of(start + t * quarter, 128), quarter)]
            dst = x_all.at[j, :, own_quarter]
        xs.append(remote(src, dst, s_x.at[j], r_x.at[j], ids[j]))
    xz = [
        [
            remote(
                x_all.at[j, :, own_quarter], x_all.at[j, :, own_quarter],
                s_z.at[j, k], r_z.at[j, k], line_ids[k],
            )
            for k in range(tensors - 1)
        ]
        for j in range(2, 8)
    ]
    xzs = [copy for line in xz for copy in line]
    mine_block = pl.ds(pl.multiple_of(me * block, 128), block)
    xl = pltpu.make_async_copy(normed.at[:, mine_block], x_all.at[0], s_local.at[9])
    for copy in rows_a + cots[1:] + local + xs[1:] + [xl]:
        copy.start()

    def bulk(src, slot, i, k, device):
        return remote(src, g_all.at[slot, i], s_g.at[k], r_g.at[k], device)

    gx = [[bulk(g_v.at[i] if q == 0 else g_all.at[1, i], 2 + q, i, 4 * q + i, ids[2]) for i in range(4)] for q in range(2)]
    gy = [[bulk(g_v.at[i] if q == 0 else g_all.at[1, i], 4 + q, i, 8 + 4 * q + i, ids[4]) for i in range(4)] for q in range(2)]
    early = [bulk(g_v.at[0], 3, 0, 4, ids[3]), bulk(g_v.at[0], 5, 0, 12, ids[5])]
    gs = [bulk(g_v.at[i], 1, i, 16 + i, ids[1]) for i in range(4)]
    gl = [pltpu.make_async_copy(g_v.at[i], g_all.at[0, i], s_local.at[5 + i]) for i in range(4)]
    fd = [
        [bulk(g_all.at[(2 if i < 2 else 4) + q, i], 6 + q, i, 20 + 4 * q + i, ids[4 if i < 2 else 2]) for i in range(4)]
        for q in range(2)
    ]
    side = [[bulk(g_all.at[n, i], n + 1 - 2 * (n % 2), i, 28 + 4 * (n - 2) + i, ids[1]) for i in range(4)] for n in range(2, 8)]
    swaps = [remote(send_v.at[i % 2], got_v.at[i], s_f.at[i], r_f.at[i], ids[1]) for i in range(4)]

    def combine(i):
        swaps[i].wait_recv()
        gate = keep_v[i % 2, 0] + got_v[i, 0]
        up = keep_v[i % 2, 1] + got_v[i, 1]
        act, slope = silu_parts(gate)
        cot = cot_ref[:, i * units : (i + 1) * units].astype(jnp.float32)
        g_v[i, :, :units] = (cot * up * slope).astype(jnp.bfloat16)
        g_v[i, :, units:] = (cot * act).astype(jnp.bfloat16)
        gs[i].start()
        gl[i].start()

        @pl.when(lead)
        def _():
            gx[0][i].start()
            gy[0][i].start()
            for n in [i - 1] * (i > 0) + [i] * (i == 3):
                gs[n].wait_recv()
                if n:
                    gx[1][n].start()
                    gy[1][n].start()

        if i == 0:
            @pl.when(core == 1)
            def _():
                for copy in early:
                    copy.start()

    rows_local.wait()
    rows_far.wait_recv()
    for i in range(4):
        w_copies[i].wait()
        if i >= 2:
            swaps[i - 2].wait_send()
        for p in range(2):
            product = jnp.dot(rows_v[...], w_buf[i % 2, p], preferred_element_type=jnp.float32)
            keep_v[i % 2, p] = product[:base]
            send_v[i % 2, p] = product[base:]
        swaps[i].start()
        if i < 2:
            w_copies.append(w_copy(i + 2))
            w_copies[-1].start()
        if i == 0:
            local[0].wait()
            rows_b[0].start()
            w_far.start()
        else:
            combine(i - 1)
        if i == 1:
            for j in range(2, 8):
                xs[j].wait_recv()
                for copy in xz[j - 2]:
                    copy.start()
        if i == 2:
            for m in range(1, 4):
                rows_a[m - 1].wait()
                rows_b[m].start()
    adv[...] = prompt_in[...].astype(jnp.float32)
    combine(3)
    for copy in rows_b + cots[1:] + [w_far]:
        copy.wait_recv()
    for copy in local[1:]:
        copy.wait()
    lane = lax.broadcasted_iota(jnp.int32, (count, wide), 1)
    keep = lane >= core * (2 * wide - units)

    def norm_rows():
        def one(b, _):
            shifted = base_buf[b].astype(jnp.float32) + adv[...]
            inverse = lax.rsqrt(jnp.mean(shifted * shifted, axis=-1, keepdims=True) + 1e-05)
            x_v[pl.ds(pl.multiple_of(b * count, count), count)] = (shifted * inverse * gain_ref[...]).astype(jnp.bfloat16)
            inv_v[b] = jnp.broadcast_to(inverse, (count, 128))
            return 0
        lax.fori_loop(0, 8, one, 0)

    def unit_grads():
        near = x_v[:, near_half]
        far = x_v[:, far_half]
        gate, up = [
            jnp.dot(near, near_v[p], preferred_element_type=jnp.float32)
            + jnp.dot(far, far_v[p], preferred_element_type=jnp.float32)
            for p in range(2)
        ]
        act, slope = silu_parts(gate)
        cot = jnp.concatenate(
            [jnp.where(keep, cot_buf[b].astype(jnp.float32), 0.0) for b in range(8)], axis=0
        )
        gp_v[:, pl.ds(0, wide)] = (cot * up * slope).astype(jnp.bfloat16)
        gp_v[:, pl.ds(wide, wide)] = (cot * act).astype(jnp.bfloat16)

    dims = (((1,), (1,)), ((), ()))
    chunk = 512

    def feature_grads():
        for source, start in ((near_v, core * half), (far_v, (1 - core) * half)):
            def one(i, _):
                rows = pl.ds(pl.multiple_of(i * chunk, chunk), chunk)
                fg_v[:, pl.ds(pl.multiple_of(start + i * chunk, chunk), chunk)] = lax.dot_general(
                    gp_v[:, pl.ds(0, wide)], source[0, rows], dims, preferred_element_type=jnp.float32
                ) + lax.dot_general(
                    gp_v[:, pl.ds(wide, wide)], source[1, rows], dims, preferred_element_type=jnp.float32
                )
                return 0
            lax.fori_loop(0, half // chunk, one, 0)

    def row_grads():
        part[...] = jnp.zeros_like(part)
        def one(b, _):
            shifted = base_buf[b].astype(jnp.float32) + adv[...]
            scaled = gain_ref[...] * fg_v[pl.ds(pl.multiple_of(b * count, count), count)]
            inverse = inv_v[b][:, :1]
            middle = jnp.mean(shifted * scaled, axis=-1, keepdims=True)
            part[...] += inverse * scaled - shifted * (inverse * inverse * inverse * middle)
            return 0
        lax.fori_loop(0, 8, one, 0)

    lead_waits, other_waits = [], []

    def exchange(k):
        for a in range(4):
            send_a[k, a] = part[:, 2 * a * block : 2 * (a + 1) * block].astype(jnp.bfloat16)
        sib = remote(send_a.at[k], recv_s.at[k], s_0.at[k], r_0.at[k], ids[1])
        first = [
            remote(send_b.at[k, rel[2 * m][0]], recv_a.at[k, m], s_1.at[k, m], r_1.at[k, m], ids[2 * m])
            for m in range(1, 4)
        ]
        second = [
            remote(recv_b.at[k, t], recv_b.at[k, t], s_2.at[k, j], r_2.at[k, j], line_ids[j])
            for j in range(tensors - 1)
        ]
        third = [
            remote(recv_c.at[k, chip], recv_c.at[k, chip], s_3.at[k, m], r_3.at[k, m], ids[2 * m])
            for m in range(1, 4)
        ]
        fourth = [
            remote(
                recv_c.at[k, rel[2 * m][0]], recv_c.at[k, rel[2 * m][0]],
                s_3.at[k, 4 + m], r_3.at[k, 4 + m], ids[1],
            )
            for m in range(4)
        ]

        @pl.when(lead)
        def _():
            sib.start()
            for copy in fourth:
                copy.wait_recv()

        @pl.when(core == 1)
        def _():
            sib.wait_recv()
            for a in range(4):
                send_b[k, a] = (
                    send_a[k, a].astype(jnp.float32) + recv_s[k, a].astype(jnp.float32)
                ).astype(jnp.bfloat16)
            for copy in first:
                copy.start()
            total = send_b[k, chip].astype(jnp.float32)
            for m in range(1, 4):
                first[m - 1].wait_recv()
                total = total + recv_a[k, m].astype(jnp.float32)
            recv_b[k, t] = total.astype(jnp.bfloat16)
            for copy in second:
                copy.start()
            for copy in second:
                copy.wait_recv()
            total = recv_b[k, 0].astype(jnp.float32)
            for j in range(1, tensors):
                total = total + recv_b[k, j].astype(jnp.float32)
            recv_c[k, chip] = total.astype(jnp.bfloat16)
            for copy in third + fourth[:1]:
                copy.start()
            for m in range(1, 4):
                third[m - 1].wait_recv()
                fourth[m].start()

        lead_waits.append(sib)
        other_waits.extend(first + second + third + fourth)
        square = jnp.zeros((count, 1), jnp.float32)
        for p in range(4):
            piece = recv_c[k, p].astype(jnp.float32)
            square = square + jnp.sum(piece * piece, axis=-1, keepdims=True)
        scale = step_ref[k] * lax.rsqrt(square / width + 1e-06)
        for p in range(4):
            at = slice(2 * p * block, 2 * (p + 1) * block)
            adv[:, at] = adv[:, at] + scale * recv_c[k, p].astype(jnp.float32)

    def pass_on(source, n, i):
        source.wait_recv()
        if n < 6 and (n < 4) == (i < 2):
            fd[n % 2][i].start()
        side[n - 2][i].start()

    def forward_some(pieces):
        @pl.when(lead)
        def _():
            for n, i in pieces:
                pass_on((gx, gy)[n // 2 - 1][n % 2][i], n, i)

    stages = [[], [(2, 0), (2, 1), (3, 0), (3, 1)], [(4, 2), (5, 2), (4, 3)], [(5, 3)]]
    rest = [(2, 2), (2, 3), (3, 2), (3, 3), (4, 0), (4, 1), (5, 0), (5, 1)]
    for k in range(steps):
        norm_rows()
        unit_grads()
        feature_grads()
        row_grads()
        exchange(k)
        if k + 1 < len(stages):
            forward_some(stages[k + 1])
    for k in range(steps, 3):
        forward_some(stages[k + 1])
    adv_out[...] = adv[...]
    norm_rows()
    unit_grads()
    xp_out[...] = x_v[:, mine_block]
    mid = 4 * count
    parts = [pl.ds(0, mid), pl.ds(mid, mid)]

    def hop(src, slot, h, k, device):
        source = gp_all.at[slot] if src is None else src
        return remote(source.at[parts[h]], gp_all.at[slot, parts[h]], s_o.at[k], r_o.at[k], device)

    os = remote(gp_v, gp_all.at[me], s_o.at[4], r_o.at[4], ids[1])
    ol = pltpu.make_async_copy(gp_v, gp_all.at[me], s_local.at[4])
    os.start()
    ol.start()
    ox = [[hop(gp_v if q == 0 else None, place[q], h, (0, 5)[q] + h, ids[2]) for h in range(2)] for q in range(2)]
    oy = [[hop(gp_v if q == 0 else None, place[q], h, (2, 7)[q] + h, ids[4]) for h in range(2)] for q in range(2)]
    od = [[hop(None, place[2 + q], 0, 9 + q, ids[4]) for q in range(2)], [hop(None, place[4 + q], 1, 11 + q, ids[2]) for q in range(2)]]
    back = [[hop(None, place[n], h, 13 + 2 * (n - 2) + h, ids[1]) for h in range(2)] for n in range(2, 8)]
    backs = [copy for two in back for copy in two]

    @pl.when(core == 1)
    def _():
        for copy in (ox[0][0], oy[0][1], ox[0][1], oy[0][0]):
            copy.start()
        os.wait_recv()
        for copy in (ox[1][0], oy[1][1], ox[1][1], oy[1][0]):
            copy.start()
        for q in range(2):
            ox[q][0].wait_recv()
            od[0][q].start()
            back[q][0].start()
            oy[q][1].wait_recv()
            od[1][q].start()
            back[2 + q][1].start()
        for q in range(2):
            ox[q][1].wait_recv()
            back[q][1].start()
            oy[q][0].wait_recv()
            back[2 + q][0].start()
        for q in range(2):
            for h in range(2):
                od[h][q].wait_recv()
                back[4 + q][h].start()
        for copy in gs:
            copy.wait_recv()
        for four in side:
            for copy in four:
                copy.wait_recv()
        for copy in other_waits + early + ox[0] + ox[1] + oy[0] + oy[1] + od[0] + od[1] + backs:
            copy.wait_send()

    @pl.when(lead)
    def _():
        for n, i in rest:
            pass_on((gx, gy)[n // 2 - 1][n % 2][i], n, i)
        for i in range(4):
            for q in range(2):
                pass_on(fd[q][i], 6 + q, i)
        os.wait_recv()
        for copy in backs:
            copy.wait_recv()
        for copy in lead_waits + gx[0] + gx[1][1:] + gy[0] + gy[1][1:] + fd[0] + fd[1]:
            copy.wait_send()
        for four in side:
            for copy in four:
                copy.wait_send()

    for copy in [xs[1]] + xzs:
        copy.wait_recv()
    for copy in gl + [ol, xl]:
        copy.wait()
    for copy in [rows_far, w_far, os] + rows_b + cots[1:] + xs[1:] + xzs + swaps[2:] + gs:
        copy.wait_send()


def main_call(pair, normed, cot, prompt, base_rows, other_rows, base_cot, gain, step_sizes):
    tensors = lax.axis_size("tensor")
    steps = step_sizes.shape[0]
    count, width = base_rows.shape
    half, shard = pair.shape[1:]
    units, wide = shard // 4, 512
    block = width // 8
    base = normed.shape[0]
    bf, f32 = jnp.bfloat16, jnp.float32
    dma = pltpu.SemaphoreType.DMA
    vmem = pl.BlockSpec(memory_space=pltpu.VMEM)
    hbm = pl.BlockSpec(memory_space=pl.ANY)
    return pl.pallas_call(
        functools.partial(main_kernel, tensors, steps),
        out_shape=[
            jax.ShapeDtypeStruct((count, width), f32),
            jax.ShapeDtypeStruct((8 * count, block), bf),
            jax.ShapeDtypeStruct((8, 4, base, 2 * units), bf),
            jax.ShapeDtypeStruct((8, base, block), bf),
            jax.ShapeDtypeStruct((8, 8 * count, 2 * wide), bf),
        ],
        in_specs=[hbm, hbm, vmem, vmem, hbm, hbm, hbm, hbm, hbm, vmem, pl.BlockSpec(memory_space=pltpu.SMEM)],
        out_specs=[vmem, vmem, hbm, hbm, hbm],
        scratch_shapes=[
            pltpu.VMEM((2 * base, half), bf),
            pltpu.VMEM((2, 2, half, units), bf),
            pltpu.VMEM((2, 2, base, units), f32),
            pltpu.VMEM((2, 2, base, units), f32),
            pltpu.VMEM((4, 2, base, units), f32),
            pltpu.VMEM((4, base, 2 * units), bf),
            pltpu.VMEM((8, count, width), bf),
            pltpu.VMEM((8, count, wide), bf),
            pltpu.VMEM((2, half, wide), bf),
            pltpu.VMEM((2, half, wide), bf),
            pltpu.VMEM((8 * count, width), bf),
            pltpu.VMEM((8 * count, width), f32),
            pltpu.VMEM((8, count, 128), f32),
            pltpu.VMEM((count, width), f32),
            pltpu.VMEM((count, width), f32),
            pltpu.VMEM((steps, 4, count, 2 * block), bf),
            pltpu.VMEM((steps, 4, count, 2 * block), bf),
            pltpu.VMEM((steps, 4, count, 2 * block), bf),
            pltpu.VMEM((steps, 4, count, 2 * block), bf),
            pltpu.VMEM((steps, tensors, count, 2 * block), bf),
            pltpu.VMEM((steps, 4, count, 2 * block), bf),
            pltpu.VMEM((8 * count, 2 * wide), bf),
        ]
        + [dma((10,))] + [dma((2,))] * 3 + [dma((4,))] * 2 + [dma((52,))] * 2 + [dma((8,))] * 6 + [dma((8, tensors))] * 2
        + [dma((steps,))] * 2 + [dma((steps, 4))] * 2 + [dma((steps, tensors))] * 2
        + [dma((steps, 8))] * 2 + [dma((25,))] * 2,
        compiler_params=pltpu.CompilerParams(
            collective_id=2, has_side_effects=True, vmem_limit_bytes=62 << 20
        ),
        cost_estimate=pl.CostEstimate(flops=100_000_000_000, bytes_accessed=100_000_000, transcendentals=0),
        name="attack_and_gather",
    )(pair, normed, cot, prompt, base_rows, *other_rows, base_cot, gain.reshape(1, width), step_sizes)


def grad_kernel(
    tensors, x_ref, xp_ref, g_ref, gp0_ref, gp1_ref, out_ref, total_ref,
    xt_v, xpt_v, sq_v, mine, buf1, buf2, send1, recv1, send2, recv2,
):
    step = pl.program_id(0) * pl.num_programs(1) + pl.program_id(1)
    t = lax.axis_index("tensor")
    plane_ids = [
        {"dp": a, "replica": b} for a, b in relative_devices(lax.axis_index("dp"), lax.axis_index("replica"))[1:]
    ]
    line_ids = [{"tensor": lax.rem(t + k, tensors)} for k in range(1, tensors)]
    barrier = pltpu.get_barrier_semaphore()

    @pl.when(step == 0)
    def _():
        for device in plane_ids + line_ids:
            pl.semaphore_signal(barrier, inc=1, device_id=device, device_id_type=MESH)
        xt_v[...] = x_ref[...].T
        xpt_v[...] = xp_ref[...].T
        sq_v[...] = jnp.zeros_like(sq_v)

    extra = 2 * gp0_ref.shape[2] - out_ref.shape[2]
    rows = g_ref.shape[0] * g_ref.shape[2]
    gp = jnp.concatenate([gp0_ref[0], gp1_ref[0][:, extra:]], axis=1)
    block = jnp.dot(
        xt_v[...], g_ref[...].reshape(rows, g_ref.shape[3]), preferred_element_type=jnp.float32
    ) + jnp.dot(xpt_v[...], gp, preferred_element_type=jnp.float32)
    out_ref[0] = block.astype(jnp.bfloat16)
    sq_v[...] += jnp.sum((block * block).reshape(-1, 8, block.shape[1]), axis=0)

    @pl.when(step == pl.num_programs(0) * pl.num_programs(1) - 1)
    def _():
        pl.semaphore_wait(barrier, 7 + tensors - 1)
        total = jnp.full((8, 128), jnp.sum(sq_v[...]), jnp.float32)
        copies = []
        for n, (ids, buf, sends, recvs) in enumerate(((plane_ids, buf1, send1, recv1), (line_ids, buf2, send2, recv2))):
            mine[n] = total
            stage = [
                pltpu.make_async_remote_copy(
                    src_ref=mine.at[n], dst_ref=buf.at[k], send_sem=sends.at[k], recv_sem=recvs.at[k],
                    device_id=device, device_id_type=MESH,
                )
                for k, device in enumerate(ids)
            ]
            for copy in stage:
                copy.start()
            for k, copy in enumerate(stage):
                copy.wait_recv()
                total = total + buf[k]
            copies += stage
        total_ref[...] = total
        for copy in copies:
            copy.wait_send()


def grad_call(x_all, xp, g_all, gp_all):
    eight, _, own_base, pair_units = g_all.shape
    cols = 4 * pair_units
    block = x_all.shape[2]
    wide = gp_all.shape[2] // 2
    shard = cols // 2
    units = shard // 4
    prompts = xp.shape[0]
    f32 = jnp.float32
    tensors = lax.axis_size("tensor")
    dma = pltpu.SemaphoreType.DMA
    return pl.pallas_call(
        functools.partial(grad_kernel, tensors),
        out_shape=[
            jax.ShapeDtypeStruct((2, block, shard), jnp.bfloat16),
            jax.ShapeDtypeStruct((8, 128), f32),
        ],
        grid=(2, 4),
        in_specs=[
            pl.BlockSpec((eight * own_base, block), lambda p, j: (0, 0)),
            pl.BlockSpec((prompts, block), lambda p, j: (0, 0)),
            pl.BlockSpec((eight, 1, own_base, units), lambda p, j: (0, j, 0, p)),
            pl.BlockSpec((1, prompts, wide), lambda p, j: (2 * j, 0, p)),
            pl.BlockSpec((1, prompts, wide), lambda p, j: (2 * j + 1, 0, p)),
        ],
        out_specs=[
            pl.BlockSpec((1, block, units), lambda p, j: (p, 0, j)),
            pl.BlockSpec((8, 128), lambda p, j: (0, 0)),
        ],
        scratch_shapes=[
            pltpu.VMEM((block, eight * own_base), jnp.bfloat16),
            pltpu.VMEM((block, prompts), jnp.bfloat16),
            pltpu.VMEM((8, units), f32),
            pltpu.VMEM((2, 8, 128), f32),
            pltpu.VMEM((7, 8, 128), f32),
            pltpu.VMEM((tensors - 1, 8, 128), f32),
        ]
        + [dma((7,))] * 2 + [dma((tensors - 1,))] * 2,
        compiler_params=pltpu.CompilerParams(
            collective_id=3, has_side_effects=True, vmem_limit_bytes=60 << 20
        ),
        cost_estimate=pl.CostEstimate(
            flops=2 * block * cols * (eight * own_base + prompts), bytes_accessed=50_000_000, transcendentals=0
        ),
        name="weight_grad",
    )(x_all.reshape(eight * own_base, block), xp, g_all, gp_all, gp_all)


def result_kernel(total_ref, grad_ref, out_ref):
    _, rows, cols = grad_ref.shape
    scale = lax.rsqrt(total_ref[:1, :1] / (2 * D * FF) + 1e-06)
    n = 128
    to = lax.broadcasted_iota(jnp.int32, (2 * n, 2 * n), 0)
    source = jnp.where(lax.rem(to, 2) == 0, to // 2, n + to // 2)
    order = jnp.where(lax.broadcasted_iota(jnp.int32, (2 * n, 2 * n), 1) == source, 1.0, 0.0).astype(jnp.bfloat16)
    for r in range(0, rows, n):
        both = jnp.concatenate(
            [grad_ref[p, r : r + n] for p in range(2)], axis=0
        )
        mixed = (jnp.dot(order, both, preferred_element_type=jnp.float32) * scale).astype(jnp.bfloat16)
        out_ref[r : r + n] = mixed.reshape(n, 2, cols)


def result_call(total, weight_grad):
    _, rows, shard = weight_grad.shape
    cols = 512
    return pl.pallas_call(
        result_kernel,
        out_shape=jax.ShapeDtypeStruct((rows, 2, shard), jnp.bfloat16),
        grid=(shard // cols,),
        in_specs=[
            pl.BlockSpec(total.shape, lambda j: (0, 0)),
            pl.BlockSpec((2, rows, cols), lambda j: (0, 0, j)),
        ],
        out_specs=pl.BlockSpec((rows, 2, cols), lambda j: (0, 0, j)),
        compiler_params=pltpu.CompilerParams(vmem_limit_bytes=48 << 20),
        name="scaled_result",
    )(total, weight_grad)


def per_device(states, norm_gain, gate_up, cotangent, prompt, step_sizes, insert_at, lengths):
    chips, cores = lax.axis_size("dp"), lax.axis_size("replica")
    shard = gate_up.shape[2]
    count = prompt.shape[0]
    fits = (
        chips == 4 and cores == 2 and 1 < lax.axis_size("tensor") <= 8 and states.shape[2] % (1024 * lax.axis_size("tensor")) == 0 and states.shape[0] == 1 and shard % (chips * 128) == 0
        and shard // chips > 512 and shard // chips <= 1024 and shard % 512 == 0
        and gate_up.shape[0] % 1024 == 0 and count % 16 == 0 and (states.shape[1] - count) % 16 == 0
    )
    if not fits:
        return per_device_general(
            states, norm_gain, gate_up, cotangent, prompt, step_sizes, insert_at, lengths
        )
    chip, core = lax.axis_index("dp"), lax.axis_index("replica")
    half = gate_up.shape[0]
    width = half * cores
    tokens = states.shape[1]
    base = tokens - count
    units = shard // chips
    start = insert_at[0]

    pair = jnp.transpose(gate_up, (1, 0, 2))

    spot = lax.broadcasted_iota(jnp.int32, (base, 1), 0)
    ahead = spot < start
    position = jnp.where(ahead, spot, spot + count)
    rows = jnp.where(ahead, states[0, :base], states[0, count:]).astype(jnp.float32)
    cot = jnp.where(ahead, cotangent[0, :base], cotangent[0, count:])
    cot = jnp.where(position < lengths[0], cot, jnp.zeros_like(cot))
    normed = (rows * row_scale(rows) * norm_gain).astype(jnp.bfloat16)
    base_rows = lax.dynamic_slice_in_dim(states[0], start, count, 0)
    base_cot = lax.dynamic_slice_in_dim(cotangent[0], start, count, 0)
    other_rows = [lax.ppermute(base_rows, "dp", [(i, i ^ m) for i in range(4)]) for m in range(1, 4)]

    adversary, xp, g_all, x_all, gp_all = main_call(
        pair, normed, cot, prompt, base_rows, other_rows, base_cot, norm_gain, step_sizes
    )
    weight_grad, total = grad_call(x_all, xp, g_all, gp_all)
    weight_step = result_call(total, weight_grad)
    column_count = width // lax.axis_size("tensor")
    prompt_final = lax.dynamic_slice_in_dim(
        adversary, lax.axis_index("tensor") * column_count, column_count, 1
    )
    return (prompt_final, weight_step)


def solution(mesh):
    return jax.shard_map(
        per_device,
        mesh=mesh,
        in_specs=(
            P(("dp", "replica"), None, None),
            P(),
            P("replica", None, "tensor"),
            P(("dp", "replica"), None, "tensor"),
            P(),
            P(),
            P(("dp", "replica")),
            P(("dp", "replica")),
        ),
        out_specs=(P(None, "tensor"), P(("dp", "replica"), None, "tensor")),
        check_vma=False,
    )
```
